32 devices in a mesh: dp: 4 (over y, x), space: 8 (over z, core).
Axes of the slice: x: 2, y: 2, z: 4, core: 2. Of those that a mesh axis runs over, the one named last changes fastest.
Arguments:
- latent: bfloat16 [4, 32, 512, 320], P('dp', 'space'), may hold values from -40 to 40
- timesteps: int32 [4], P('dp'), may hold values from 0 to 999
- norm_gain: float32 [320], replicated, may hold values from 0.1 to 1.9
- norm_bias: float32 [320], replicated, may hold values from -3 to 3
- conv_weight: bfloat16 [3, 3, 320, 320], replicated, may hold values from -0.109375 to 0.109375
- conv_bias: float32 [320], replicated, may hold values from -3 to 3
- time_weight: bfloat16 [320, 320], replicated, may hold values from -0.5 to 0.5
- cotangent: bfloat16 [4, 32, 512, 320], P('dp', 'space'), may hold values from -40 to 40
Outputs:
- block_out: bfloat16 [4, 32, 512, 320], P('dp', 'space')
- latent_grad: bfloat16 [4, 32, 512, 320], P('dp', 'space')
- weight_grad: float32 [3, 3, 320, 320], replicated
- time_grad: float32 [320, 320], replicated
The draws below stay inside these ranges and needn't reach their ends.
All inputs are finite; a program needn't handle non-finite values.
Results may differ from the reference program's by a relative error of at most 0.001.
The reference program's roundings to bfloat16 on the way (of `activated` and `embedding`) count: a program that leaves them out, or rounds other values in their place, can miss the bound.
Values may be sent and summed in bfloat16 or wider, within the bound.
No kernel may reach another device: no remote copies, remote signals or barrier semaphores. Data moves between devices by JAX's collectives and lax.ppermute only.
A program may use at most 128 MiB of HBM per device.

```python
import math
import jax
import jax.numpy as jnp
from jax import lax

CH = 320
GROUPS = 32
COLS = 512
HEIGHT = 32
IMAGES = 4


def row_profile(top_scale):
    ramp = jnp.arange(HEIGHT, dtype=jnp.float32) / max(HEIGHT - 1, 1)
    return (jnp.exp(jnp.log(top_scale) * ramp), ramp)


def draw_latent(key, part):
    first_key = jax.random.fold_in(key, 101)
    second_key = jax.random.fold_in(key, 202)
    shape = (IMAGES, HEIGHT, COLS, CH)
    noise = jnp.clip(jax.random.normal(first_key, shape, jnp.float32), -5.0, 5.0)
    top_scale = 4.0
    scales, ramp = row_profile(top_scale)
    offset = jnp.clip(jax.random.normal(second_key, (IMAGES, 1, 1, CH), jnp.float32), -3.0, 3.0)
    values = noise * scales[None, :, None, None] + 2.0 * offset * ramp[None, :, None, None]
    return jnp.clip(values, -40.0, 40.0).astype(jnp.bfloat16)


def draw_cotangent(key, part):
    first_key = jax.random.fold_in(key, 303)
    shape = (IMAGES, HEIGHT, COLS, CH)
    noise = jnp.clip(jax.random.normal(first_key, shape, jnp.float32), -5.0, 5.0)
    top_scale = 5.0
    scales, ramp = row_profile(top_scale)
    values = noise * scales[::-1][None, :, None, None]
    return jnp.clip(values, -40.0, 40.0).astype(jnp.bfloat16)


def set_ends(drawn, stream_key, low, top_value):
    longest = drawn.shape.index(max(drawn.shape))
    spots = []
    for shift in (0, 1):
        where = [jax.random.randint(jax.random.fold_in(stream_key, axis), (), 0, length) for axis, length in enumerate(drawn.shape)]
        where[longest] = (where[longest] + shift) % drawn.shape[longest]
        spots.append(tuple(where))
    return drawn.at[spots[0]].set(low).at[spots[1]].set(top_value)


def bell_draw(own_key, shape, width, bound, kind=jnp.bfloat16):
    return jnp.clip(width * jax.random.normal(own_key, shape, jnp.float32), -bound, bound).astype(kind)


def setup_inputs(seed: int = 0) -> dict:
    seeds = jax.random.split(jax.random.key(seed), 9)
    latent = draw_latent(jax.random.fold_in(seeds[8], 71), 0)
    timesteps = set_ends(jax.random.randint(seeds[1], (IMAGES,), 0, 1000), jax.random.fold_in(seeds[1], 1), 0, 999).astype(jnp.int32)
    norm_gain = jnp.clip(1.0 + 0.18 * jax.random.normal(seeds[2], (CH,), jnp.float32), 0.1, 1.9)
    norm_bias = bell_draw(seeds[3], (CH,), 0.5, 3.0, jnp.float32)
    conv_weight = bell_draw(seeds[4], (3, 3, CH, CH), (9 * CH) ** -0.5, 0.109375)
    conv_bias = bell_draw(seeds[5], (CH,), 0.5, 3.0, jnp.float32)
    time_weight = bell_draw(seeds[6], (CH, CH), (CH // 2) ** -0.5, 0.5)
    cotangent = draw_cotangent(jax.random.fold_in(seeds[8], 71), 0)
    return {"latent": latent, "timesteps": timesteps, "norm_gain": norm_gain, "norm_bias": norm_bias, "conv_weight": conv_weight, "conv_bias": conv_bias, "time_weight": time_weight, "cotangent": cotangent}


epsilon = 1e-05

def group_stats(values):
    grouped = values.reshape(-1, GROUPS, CH // GROUPS)
    group_mean = lax.optimization_barrier(jnp.mean(grouped, axis=(0, 2)))
    centered = grouped - group_mean[None, :, None]
    group_var = lax.optimization_barrier(jnp.mean(centered * centered, axis=(0, 2)))
    return (group_mean, group_var)

def per_channel(values):
    return jnp.repeat(values, CH // GROUPS)

def sinusoid(step_value):
    half_count = CH // 2
    frequency = jnp.exp(-math.log(10000.0) * jnp.arange(half_count, dtype=jnp.float32) / half_count)
    angles = step_value.astype(jnp.float32) * frequency
    return jnp.concatenate([jnp.cos(angles), jnp.sin(angles)]).astype(jnp.bfloat16)

def one_image(latent_img, step_value, grad_img, norm_gain, norm_bias, conv_weight, conv_bias, time_weight):
    latent_wide = latent_img.astype(jnp.float32)
    group_mean, group_var = group_stats(latent_wide)
    inverse_std = lax.rsqrt(group_var + epsilon)
    normed = (latent_wide - per_channel(group_mean)) * per_channel(inverse_std)
    shifted = normed * norm_gain + norm_bias
    sigmoid_act = jax.nn.sigmoid(shifted)
    activated = (shifted * sigmoid_act).astype(jnp.bfloat16)
    padded_act = jnp.pad(activated, ((1, 1), (1, 1), (0, 0)))
    padded_grad = jnp.pad(grad_img, ((1, 1), (1, 1), (0, 0)))
    grad_flat = grad_img.reshape(-1, CH)
    conv_out = jnp.zeros((HEIGHT * COLS, CH), jnp.float32)
    act_grad = jnp.zeros((HEIGHT * COLS, CH), jnp.float32)
    weight_rows = []
    for tap_row in range(3):
        weight_cols = []
        for tap_col in range(3):
            piece = padded_act[tap_row:tap_row + HEIGHT, tap_col:tap_col + COLS].reshape(-1, CH)
            conv_out = conv_out + jnp.dot(piece, conv_weight[tap_row, tap_col], preferred_element_type=jnp.float32)
            grad_piece = padded_grad[2 - tap_row:2 - tap_row + HEIGHT, 2 - tap_col:2 - tap_col + COLS].reshape(-1, CH)
            act_grad = act_grad + jnp.dot(grad_piece, conv_weight[tap_row, tap_col].T, preferred_element_type=jnp.float32)
            weight_cols.append(jnp.dot(piece.T, grad_flat, preferred_element_type=jnp.float32))
        weight_rows.append(jnp.stack(weight_cols))
    weight_part = jnp.stack(weight_rows)
    embedding = sinusoid(step_value)
    time_bias = jnp.dot(embedding[None, :], time_weight, preferred_element_type=jnp.float32)[0]
    block_out = (latent_wide + conv_out.reshape(HEIGHT, COLS, CH) + conv_bias + time_bias).astype(jnp.bfloat16)
    act_grad = act_grad.reshape(HEIGHT, COLS, CH)
    normed_grad = act_grad * sigmoid_act * (1.0 + shifted * (1.0 - sigmoid_act)) * norm_gain
    first_mean = lax.optimization_barrier(jnp.mean(normed_grad.reshape(-1, GROUPS, CH // GROUPS), axis=(0, 2)))
    second_mean = lax.optimization_barrier(jnp.mean((normed_grad * normed).reshape(-1, GROUPS, CH // GROUPS), axis=(0, 2)))
    change = per_channel(inverse_std) * (normed_grad - per_channel(first_mean) - normed * per_channel(second_mean))
    latent_grad = (grad_img.astype(jnp.float32) + change).astype(jnp.bfloat16)
    grad_total = lax.optimization_barrier(jnp.sum(grad_img.astype(jnp.float32), axis=(0, 1)))
    time_part = embedding.astype(jnp.float32)[:, None] * grad_total[None, :]
    return (block_out, latent_grad, weight_part, time_part)

def reference(latent, timesteps, norm_gain, norm_bias, conv_weight, conv_bias, time_weight, cotangent):

    def per_image(items):
        return one_image(items[0], items[1], items[2], norm_gain, norm_bias, conv_weight, conv_bias, time_weight)
    block_out, latent_grad, weight_parts, time_parts = lax.map(per_image, (latent, timesteps, cotangent))
    return (block_out, latent_grad, lax.optimization_barrier(jnp.sum(weight_parts, axis=0)), lax.optimization_barrier(jnp.sum(time_parts, axis=0)))
```

```python
import functools
import math

import jax
import jax.numpy as jnp
from jax import lax
from jax.experimental import pallas as pl
from jax.experimental.pallas import tpu as pltpu
from jax.sharding import PartitionSpec as P

GROUPS = 32
epsilon = 1e-05
f32 = jnp.float32
bf16 = jnp.bfloat16
f16 = jnp.float16
HIGHEST = lax.Precision.HIGHEST
LANES = 128


def contract(a, b, dims, precision=None):
    return lax.dot_general(a, b, (dims, ((), ())), preferred_element_type=f32, precision=precision)


def call(body, outs, args, specs=None, scratch=(), flops=0, moved=0, limit=40 << 20):
    vmem = pl.BlockSpec(memory_space=pltpu.VMEM)
    many = isinstance(outs, (list, tuple))
    return pl.pallas_call(
        body,
        out_shape=tuple(outs) if many else outs,
        in_specs=list(specs) if specs else [vmem] * len(args),
        out_specs=tuple([vmem] * len(outs)) if many else vmem,
        scratch_shapes=list(scratch),
        compiler_params=pltpu.CompilerParams(vmem_limit_bytes=limit),
        cost_estimate=pl.CostEstimate(flops=flops, bytes_accessed=moved, transcendentals=0),
    )(*args)


def member_matrix(channels):
    per_group = channels // GROUPS
    row = lax.broadcasted_iota(jnp.int32, (channels, channels), 0).astype(f32)
    col = lax.broadcasted_iota(jnp.int32, (channels, channels), 1).astype(f32)
    same = jnp.floor((row + 0.5) / per_group) == jnp.floor((col + 0.5) / per_group)
    return jnp.where(same, 1.0, 0.0).astype(f32)


def lane_form(cells):
    ones = jnp.ones((8, cells.shape[1]), f32)
    return contract(ones, cells, ((1,), (1,)), HIGHEST)


def rows_of(*rows):
    height = lax.broadcasted_iota(jnp.int32, rows[0].shape, 0)
    packed = jnp.zeros(rows[0].shape, f32)
    for number, row in enumerate(rows):
        packed = jnp.where(height == number, row, packed)
    return packed


def fold_lanes(cells):
    total = cells[:, :LANES]
    for start in range(LANES, cells.shape[1], LANES):
        total = total + cells[:, start : start + LANES]
    return total


def stats_body(count, step_ref, latent_ref, cot_ref, out_ref):
    row_count, channels, cols = latent_ref.shape
    member = member_matrix(channels)
    ones = jnp.ones((cols, LANES), bf16)
    tall = jnp.ones((8, cols), bf16)
    sums = jnp.zeros((channels, LANES), f32)
    grads = jnp.zeros((8, channels), f32)
    top = jnp.zeros((channels, LANES), f32)
    for row in range(row_count):
        sums = sums + contract(latent_ref[row], ones, ((1,), (0,)))
        grads = grads + contract(tall, cot_ref[row], ((1,), (1,)))
        size = jnp.abs(cot_ref[row].astype(f32))
        for start in range(0, cols, LANES):
            top = jnp.maximum(top, size[:, start : start + LANES])
    mean = contract(member, sums, ((1,), (0,)), HIGHEST) / count
    squares = jnp.zeros((channels, LANES), f32)
    for row in range(row_count):
        centered = latent_ref[row].astype(f32) - mean[:, :1]
        squares = squares + fold_lanes(centered * centered)
    grouped = contract(member, squares, ((1,), (0,)), HIGHEST)
    step = jnp.full((8, channels), step_ref[0].astype(f32))
    largest = jnp.broadcast_to(jnp.max(top), (8, channels))
    out_ref[...] = rows_of(
        lane_form(mean) * (1.0 / LANES), lane_form(grouped), grads, largest, step
    )


def tree_sum(parts):
    while len(parts) > 1:
        parts = [parts[i] + parts[i + 1] for i in range(0, len(parts), 2)]
    return parts[0]


def merge_body(count, total, *refs):
    out_ref = refs[-1]
    parts = [ref[...] for ref in refs[:-1]]
    mean = tree_sum([part[0:1] for part in parts]) / len(parts)
    squares = tree_sum([part[1:2] + count * (part[0:1] - mean) ** 2 for part in parts])
    grads = tree_sum([part[2:3] for part in parts])
    largest = functools.reduce(jnp.maximum, [part[3:4] for part in parts])
    if total:
        squares = lax.rsqrt(squares / total + epsilon)
    shape = parts[0].shape
    out_ref[...] = rows_of(
        *[
            jnp.broadcast_to(row, shape)
            for row in (mean, squares, grads, largest, parts[0][4:5])
        ]
    )


def column_values(stats_ref, gain_ref, bias_ref):
    channels = gain_ref.shape[1]
    shape = (8, channels)
    table = rows_of(
        jnp.broadcast_to(stats_ref[0:1], shape),
        jnp.broadcast_to(stats_ref[1:2], shape),
        jnp.broadcast_to(gain_ref[...], shape),
        jnp.broadcast_to(bias_ref[...], shape),
    ).T
    return [table[:, i : i + 1] for i in range(4)]


def normalized(cells, values):
    mean, inverse, gain, bias = values
    normed = (cells.astype(f32) - mean) * inverse
    shifted = normed * gain + bias
    return normed, shifted, jax.nn.sigmoid(shifted)


def activate(cells, values):
    _, shifted, sigmoid = normalized(cells, values)
    return (shifted * sigmoid).astype(bf16)


def shifted_cols(cells):
    cols = cells.shape[1]
    lane = lax.broadcasted_iota(jnp.int32, cells.shape, 1)
    zero = jnp.zeros_like(cells)
    after = jnp.where(lane == cols - 1, zero, pltpu.roll(cells, cols - 1, 1))
    before = jnp.where(lane == 0, zero, pltpu.roll(cells, 1, 1))
    return after, before


def put_taps(buffer_ref, place, cells, flip):
    channels, cols = cells.shape
    wide = cells.astype(f32)
    after, before = shifted_cols(wide)
    order = (after, cells, before) if flip else (before, cells, after)
    for tap, piece in enumerate(order):
        buffer_ref[tap * channels : (tap + 1) * channels, place * cols : (place + 1) * cols] = (
            piece.astype(bf16)
        )


def put_gradient(taps_ref, cot_ref, above_ref, below_ref):
    row_count = cot_ref.shape[0]
    put_taps(taps_ref, 0, above_ref[...], True)
    for row in range(row_count):
        put_taps(taps_ref, row + 1, cot_ref[row], True)
    put_taps(taps_ref, row_count + 1, below_ref[...], True)


def weight_body(
    shape, latent_ref, cot_ref, above_ref, below_ref, stats_ref, gain_ref, bias_ref,
    act_ref, out_ref, taps_ref,
):
    blocks, zones, height, width = shape
    row_count, channels, cols = latent_ref.shape
    values = column_values(stats_ref, gain_ref, bias_ref)
    for row in range(row_count):
        act_ref[:, row * cols : (row + 1) * cols] = activate(latent_ref[row], values)
    put_gradient(taps_ref, cot_ref, above_ref, below_ref)
    tap_width = zones * width // 3
    for tap_row in range(3):
        start = (2 - tap_row) * cols
        found = contract(
            act_ref[...], taps_ref[:, start : start + row_count * cols], ((1,), (1,))
        )
        for block in range(blocks):
            first = block * height
            last = min(first + height, channels)
            for zone in range(zones):
                low = max(zone * width, tap_row * tap_width)
                high = min((zone + 1) * width, (tap_row + 1) * tap_width)
                if low >= high:
                    continue
                left, right = low - zone * width, high - zone * width
                used = min(high - tap_row * tap_width, 3 * channels) + tap_row * tap_width - low
                if first >= channels or used <= 0:
                    out_ref[block, zone, :, left:right] = jnp.zeros((height, right - left), f32)
                    continue
                source = low - tap_row * tap_width
                out_ref[block, zone, : last - first, left : left + used] = found[
                    first:last, source : source + used
                ]
                if left + used < right:
                    out_ref[block, zone, :, left + used : right] = jnp.zeros(
                        (height, right - left - used), f32
                    )
                if last - first < height:
                    out_ref[block, zone, last - first :, left:right] = jnp.zeros(
                        (height - last + first, right - left), f32
                    )


def conv_body(
    ends_ref, act_ref, latent_ref, above_ref, below_ref, stats_ref, gain_ref, bias_ref,
    weight_ref, extra_ref, out_ref, taps_ref, flat_ref,
):
    row_count, channels, cols = latent_ref.shape
    values = column_values(stats_ref, gain_ref, bias_ref)
    for place, ref, end in ((0, above_ref, 0), (row_count + 1, below_ref, 1)):
        keep = ends_ref[end].astype(f32)
        put_taps(taps_ref, place, (activate(ref[...], values).astype(f32) * keep).astype(bf16), False)
    for row in range(row_count):
        put_taps(taps_ref, row + 1, act_ref[:, row * cols : (row + 1) * cols], False)
    for tap_row in range(3):
        flat_ref[tap_row] = weight_ref[tap_row].reshape(3 * channels, channels).T
    extra = jnp.broadcast_to(extra_ref[...], (8, channels)).T[:, :1]
    for row in range(row_count):
        total = latent_ref[row].astype(f32) + extra
        for tap_row in range(3):
            start = (row + tap_row) * cols
            total = total + contract(
                flat_ref[tap_row], taps_ref[:, start : start + cols], ((1,), (0,))
            )
        out_ref[row] = total.astype(bf16)


def backward_body(
    latent_ref, cot_ref, above_ref, below_ref, stats_ref, gain_ref, bias_ref, weight_ref,
    grad_ref, sums_ref, taps_ref, flat_ref,
):
    row_count, channels, cols = latent_ref.shape
    values = column_values(stats_ref, gain_ref, bias_ref)
    put_gradient(taps_ref, cot_ref, above_ref, below_ref)
    for tap_row in range(3):
        flat_ref[tap_row] = jnp.concatenate([weight_ref[tap_row, j] for j in range(3)], axis=1)
    first = jnp.zeros((channels, LANES), f32)
    second = jnp.zeros((channels, LANES), f32)
    for row in range(row_count):
        total = jnp.zeros((channels, cols), f32)
        for tap_row in range(3):
            start = (row + 2 - tap_row) * cols
            total = total + contract(
                flat_ref[tap_row], taps_ref[:, start : start + cols], ((1,), (0,))
            )
        normed, shifted, sigmoid = normalized(latent_ref[row], values)
        grad = total * sigmoid * (1.0 + shifted * (1.0 - sigmoid)) * values[2]
        grad_ref[row] = grad
        first = first + fold_lanes(grad)
        second = second + fold_lanes(grad * normed)
    member = member_matrix(channels)
    first = contract(member, first, ((1,), (0,)), HIGHEST)
    second = contract(member, second, ((1,), (0,)), HIGHEST)
    sums_ref[...] = rows_of(lane_form(first), lane_form(second))


def latent_body(
    total, parts, grad_ref, latent_ref, cot_ref, stats_ref, *refs,
):
    out_ref = refs[-1]
    row_count, channels, cols = latent_ref.shape
    sums = tree_sum([ref[...] for ref in refs[:parts]]) / total
    shape = (8, channels)
    table = rows_of(
        *[
            jnp.broadcast_to(row, shape)
            for row in (stats_ref[0:1], stats_ref[1:2], sums[0:1], sums[1:2])
        ]
    ).T
    mean, inverse, first, second = [table[:, i : i + 1] for i in range(4)]
    for row in range(row_count):
        normed = (latent_ref[row].astype(f32) - mean) * inverse
        change = inverse * (grad_ref[row] - first - normed * second)
        out_ref[row] = (cot_ref[row].astype(f32) + change).astype(bf16)


def place_body(shape, places_ref, cells_ref, out_ref, flat_ref):
    blocks, zones, height, width = shape
    channels = out_ref.shape[1]
    for block in range(blocks):
        top = pl.multiple_of(places_ref[block] * height, 8)
        for zone in range(zones):
            left = pl.multiple_of(places_ref[blocks + zone] * width, LANES)
            flat_ref[pl.ds(top, height), pl.ds(left, width)] = cells_ref[block, zone]
    tap_width = zones * width // 3
    for tap_row in range(3):
        for tap_col in range(3):
            left = tap_row * tap_width + tap_col * channels
            out_ref[tap_row * 3 + tap_col] = flat_ref[:channels, left : left + channels]


def pick(cells, index):
    return lax.dynamic_index_in_dim(cells, index, 0, keepdims=False)


def swap_space(cells, mask):
    count = lax.axis_size("space")
    return lax.ppermute(cells, "space", [(i, i ^ mask) for i in range(count)])


def swap_image(cells, masks):
    images = lax.axis_size("dp")
    count = lax.axis_size("space")
    pairs = [
        (i * count + j, (i ^ masks[j % 2]) * count + j) for i in range(images) for j in range(count)
    ]
    return lax.ppermute(cells, ("dp", "space"), pairs)


def per_device(
    latent, timesteps, norm_gain, norm_bias, conv_weight, conv_bias, time_weight, cotangent
):
    images, row_count, col_count, channels = latent.shape
    assert images == 1
    per_group = channels // GROUPS
    image_count = lax.axis_size("dp")
    slab_count = lax.axis_size("space")
    zones = slab_count // 2
    bits = image_count.bit_length() - 1
    blocks = 2 * image_count
    height = -(-channels // (8 * blocks)) * 8
    tap_width = -(-3 * channels // LANES) * LANES
    width = 3 * tap_width // zones
    local_count = row_count * col_count * per_group
    total_count = local_count * slab_count
    positions = row_count * col_count

    image_index = lax.axis_index("dp")
    slab_index = lax.axis_index("space")
    core = slab_index % 2
    zone_index = slab_index // 2

    lat = latent.transpose(0, 1, 3, 2)[0]
    cot = cotangent.transpose(0, 1, 3, 2)[0]
    gain = norm_gain.reshape(1, channels)
    bias = norm_bias.reshape(1, channels)
    smem = pl.BlockSpec(memory_space=pltpu.SMEM)
    vmem = pl.BlockSpec(memory_space=pltpu.VMEM)
    small = jax.ShapeDtypeStruct((8, channels), f32)

    down = [(i, i + 1) for i in range(slab_count - 1)]
    up = [(i + 1, i) for i in range(slab_count - 1)]

    own = call(
        functools.partial(stats_body, local_count),
        small,
        (timesteps, lat, cot),
        specs=(smem, vmem, vmem),
        moved=2 * lat.size * 2,
        flops=positions * channels * 60,
    )
    cot_above = lax.ppermute(cot[row_count - 1], "space", down)
    cot_below = lax.ppermute(cot[0], "space", up)
    pair = call(
        functools.partial(merge_body, local_count, None), small, (own, swap_space(own, 1))
    )
    parts = [pair] + [swap_space(pair, 2 * mask) for mask in range(1, zones)]
    stats = call(
        functools.partial(merge_body, 2 * local_count, total_count), small, tuple(parts)
    )
    lat_above = lax.ppermute(lat[row_count - 1], "space", down)
    lat_below = lax.ppermute(lat[0], "space", up)

    everyone = [stats] + [swap_image(stats, (mask, mask)) for mask in range(1, image_count)]
    largest = functools.reduce(jnp.maximum, [part[3, 0] for part in everyone])
    reach = math.sqrt(per_group) * jnp.max(jnp.abs(norm_gain)) + jnp.max(jnp.abs(norm_bias))
    bound = largest * reach * float(positions * slab_count * image_count)
    power = jnp.clip(jnp.floor(jnp.log2(30000.0 / jnp.maximum(bound, 1e-30))), -100.0, 100.0)
    scale = jnp.exp2(power)
    back = 1.0 / scale

    flops = 2 * positions * channels * channels * 9
    act, grads = call(
        functools.partial(weight_body, (blocks, zones, height, width)),
        (
            jax.ShapeDtypeStruct((channels, positions), bf16),
            jax.ShapeDtypeStruct((blocks, zones, height, width), f32),
        ),
        (lat, cot, cot_above, cot_below, stats, gain, bias),
        scratch=(pltpu.VMEM((3 * channels, (row_count + 2) * col_count), bf16),),
        flops=flops,
        moved=8 * lat.size,
    )

    grads = grads.reshape((2,) + (2,) * bits + (zones, height, width))
    total = pick(grads, core) + swap_space(pick(grads, 1 - core), 1)
    orders = [list(range(bits)), list(range(bits))[::-1]]
    own_bits = []
    for step in range(bits):
        shift = jnp.where(core == 0, orders[0][step], orders[1][step])
        bit = (image_index >> shift) & 1
        own_bits.append(bit)
        masks = (1 << orders[0][step], 1 << orders[1][step])
        sent = (pick(total, 1 - bit) * scale).astype(f16)
        total = pick(total, bit) + swap_image(sent, masks).astype(f32) * back
    share = pick(total, zone_index)
    for mask in range(1, zones):
        sent = (pick(total, zone_index ^ mask) * scale).astype(f16)
        share = share + swap_space(sent, 2 * mask).astype(f32) * back
    share = (share * scale).astype(f16)
    full = jnp.stack([share] + [swap_space(share, 2 * mask) for mask in range(1, zones)])
    for step in reversed(range(bits)):
        masks = (1 << orders[0][step], 1 << orders[1][step])
        full = jnp.stack([full, swap_image(full, masks)])
    full = jnp.stack([full, swap_space(full, 1)])
    cells = (full.astype(f32) * back).reshape(blocks, zones, height, width)
    places = []
    for block in range(blocks):
        other = block // image_count
        place = core ^ other
        for step in range(bits):
            flip = (block >> (bits - 1 - step)) & 1
            if other:
                shift = jnp.where(core == 1, orders[0][step], orders[1][step])
            else:
                shift = jnp.where(core == 0, orders[0][step], orders[1][step])
            place = place * 2 + (((image_index >> shift) & 1) ^ flip)
        places.append(place)
    places += [zone_index ^ mask for mask in range(zones)]
    places = jnp.stack(places).astype(jnp.int32)
    weight_grad = call(
        functools.partial(place_body, (blocks, zones, height, width)),
        jax.ShapeDtypeStruct((9, channels, channels), f32),
        (places, cells),
        specs=(smem, vmem),
        scratch=(pltpu.VMEM((blocks * height, zones * width), f32),),
        moved=8 * 9 * channels * channels,
    ).reshape(3, 3, channels, channels)

    half_count = channels // 2
    frequency = jnp.exp(-math.log(10000.0) * jnp.arange(half_count, dtype=f32) / half_count)

    def embed(step_value):
        angles = step_value * frequency
        return jnp.concatenate([jnp.cos(angles), jnp.sin(angles)]).astype(bf16)

    embedding = embed(timesteps[0].astype(f32))
    time_bias = jnp.dot(embedding[None, :], time_weight, preferred_element_type=f32)
    extra = time_bias + conv_bias.reshape(1, channels)
    ends = jnp.stack([slab_index > 0, slab_index < slab_count - 1]).astype(jnp.int32)

    taps = pltpu.VMEM((3 * channels, (row_count + 2) * col_count), bf16)
    flat = pltpu.VMEM((3, channels, 3 * channels), bf16)
    grad, sums = call(
        backward_body,
        (jax.ShapeDtypeStruct((row_count, channels, col_count), f32), small),
        (lat, cot, cot_above, cot_below, stats, gain, bias, conv_weight),
        scratch=(taps, flat),
        flops=flops,
        moved=8 * lat.size,
    )
    block_out = call(
        conv_body,
        jax.ShapeDtypeStruct((row_count, channels, col_count), bf16),
        (ends, act, lat, lat_above, lat_below, stats, gain, bias, conv_weight, extra),
        specs=(smem,) + (vmem,) * 9,
        scratch=(taps, flat),
        flops=flops,
        moved=8 * lat.size,
    )
    sums = sums + swap_space(sums, 1)
    others = [sums] + [swap_space(sums, 2 * mask) for mask in range(1, zones)]
    latent_grad = call(
        functools.partial(latent_body, total_count, len(others)),
        jax.ShapeDtypeStruct((row_count, channels, col_count), bf16),
        (grad, lat, cot, stats, *others),
        flops=lat.size * 20,
        moved=10 * lat.size,
    )

    table = jnp.stack([part[2:5] for part in everyone])
    order = jnp.arange(image_count) ^ image_index
    table = table[order]
    time_grad = jnp.zeros((channels, channels), f32)
    for image in range(image_count):
        column = embed(table[image, 2, 0]).astype(f32)
        time_grad = time_grad + column[:, None] * table[image, 0][None, :]

    block_out = block_out[None].transpose(0, 1, 3, 2)
    latent_grad = latent_grad[None].transpose(0, 1, 3, 2)
    return (block_out, latent_grad, weight_grad, time_grad)


def solution(mesh):
    return jax.shard_map(
        per_device,
        mesh=mesh,
        in_specs=(
            P("dp", "space", None, None),
            P("dp"),
            P(),
            P(),
            P(),
            P(),
            P(),
            P("dp", "space", None, None),
        ),
        out_specs=(P("dp", "space", None, None), P("dp", "space", None, None), P(), P()),
        check_vma=False,
    )
```

```python
import functools
import math

import jax
import jax.numpy as jnp
from jax import lax
from jax.experimental import pallas as pl
from jax.experimental.pallas import tpu as pltpu
from jax.sharding import PartitionSpec as P


GROUPS = 32
epsilon = 1e-05
f32 = jnp.float32
bf16 = jnp.bfloat16
f16 = jnp.float16
HIGHEST = lax.Precision.HIGHEST
LANES = 128


def contract(a, b, dims, precision=None):
    return lax.dot_general(a, b, (dims, ((), ())), preferred_element_type=f32, precision=precision)


def call(body, outs, args, specs=None, scratch=(), flops=0, moved=0, limit=40 << 20):
    vmem = pl.BlockSpec(memory_space=pltpu.VMEM)
    many = isinstance(outs, (list, tuple))
    return pl.pallas_call(
        body,
        out_shape=tuple(outs) if many else outs,
        in_specs=list(specs) if specs else [vmem] * len(args),
        out_specs=tuple([vmem] * len(outs)) if many else vmem,
        scratch_shapes=list(scratch),
        compiler_params=pltpu.CompilerParams(vmem_limit_bytes=limit),
        cost_estimate=pl.CostEstimate(flops=flops, bytes_accessed=moved, transcendentals=0),
    )(*args)


def member_matrix(channels):
    per_group = channels // GROUPS
    row = lax.broadcasted_iota(jnp.int32, (channels, channels), 0).astype(f32)
    col = lax.broadcasted_iota(jnp.int32, (channels, channels), 1).astype(f32)
    same = jnp.floor((row + 0.5) / per_group) == jnp.floor((col + 0.5) / per_group)
    return jnp.where(same, 1.0, 0.0).astype(f32)


def lane_form(cells):
    ones = jnp.ones((8, cells.shape[1]), f32)
    return contract(ones, cells, ((1,), (1,)), HIGHEST)


def rows_of(*rows):
    height = lax.broadcasted_iota(jnp.int32, rows[0].shape, 0)
    packed = jnp.zeros(rows[0].shape, f32)
    for number, row in enumerate(rows):
        packed = jnp.where(height == number, row, packed)
    return packed


def fold_lanes(cells):
    total = cells[:, :LANES]
    for start in range(LANES, cells.shape[1], LANES):
        total = total + cells[:, start : start + LANES]
    return total


def stats_body(count, step_ref, latent_ref, cot_ref, out_ref):
    row_count, channels, cols = latent_ref.shape
    member = member_matrix(channels)
    ones = jnp.ones((cols, LANES), bf16)
    tall = jnp.ones((8, cols), bf16)
    sums = jnp.zeros((channels, LANES), f32)
    grads = jnp.zeros((8, channels), f32)
    top = jnp.zeros((channels, LANES), f32)
    for row in range(row_count):
        sums = sums + contract(latent_ref[row], ones, ((1,), (0,)))
        grads = grads + contract(tall, cot_ref[row], ((1,), (1,)))
        size = jnp.abs(cot_ref[row].astype(f32))
        for start in range(0, cols, LANES):
            top = jnp.maximum(top, size[:, start : start + LANES])
    mean = contract(member, sums, ((1,), (0,)), HIGHEST) / count
    squares = jnp.zeros((channels, LANES), f32)
    for row in range(row_count):
        centered = latent_ref[row].astype(f32) - mean[:, :1]
        squares = squares + fold_lanes(centered * centered)
    grouped = contract(member, squares, ((1,), (0,)), HIGHEST)
    step = jnp.full((8, channels), step_ref[0].astype(f32))
    largest = jnp.broadcast_to(jnp.max(top), (8, channels))
    out_ref[...] = rows_of(
        lane_form(mean) * (1.0 / LANES), lane_form(grouped), grads, largest, step
    )


def tree_sum(parts):
    while len(parts) > 1:
        parts = [parts[i] + parts[i + 1] for i in range(0, len(parts), 2)]
    return parts[0]


def merge_body(count, total, *refs):
    out_ref = refs[-1]
    parts = [ref[...] for ref in refs[:-1]]
    mean = tree_sum([part[0:1] for part in parts]) / len(parts)
    squares = tree_sum([part[1:2] + count * (part[0:1] - mean) ** 2 for part in parts])
    grads = tree_sum([part[2:3] for part in parts])
    largest = functools.reduce(jnp.maximum, [part[3:4] for part in parts])
    if total:
        squares = lax.rsqrt(squares / total + epsilon)
    shape = parts[0].shape
    out_ref[...] = rows_of(
        *[
            jnp.broadcast_to(row, shape)
            for row in (mean, squares, grads, largest, parts[0][4:5])
        ]
    )


def column_values(stats_ref, gain_ref, bias_ref):
    channels = gain_ref.shape[1]
    shape = (8, channels)
    table = rows_of(
        jnp.broadcast_to(stats_ref[0:1], shape),
        jnp.broadcast_to(stats_ref[1:2], shape),
        jnp.broadcast_to(gain_ref[...], shape),
        jnp.broadcast_to(bias_ref[...], shape),
    ).T
    return [table[:, i : i + 1] for i in range(4)]


def normalized(cells, values):
    mean, inverse, gain, bias = values
    normed = (cells.astype(f32) - mean) * inverse
    shifted = normed * gain + bias
    return normed, shifted, jax.nn.sigmoid(shifted)


def activate(cells, values):
    _, shifted, sigmoid = normalized(cells, values)
    return (shifted * sigmoid).astype(bf16)


def shifted_cols(cells):
    cols = cells.shape[1]
    lane = lax.broadcasted_iota(jnp.int32, cells.shape, 1)
    zero = jnp.zeros_like(cells)
    after = jnp.where(lane == cols - 1, zero, pltpu.roll(cells, cols - 1, 1))
    before = jnp.where(lane == 0, zero, pltpu.roll(cells, 1, 1))
    return after, before


def put_taps(buffer_ref, place, cells, flip):
    channels, cols = cells.shape
    wide = cells.astype(f32)
    after, before = shifted_cols(wide)
    order = (after, cells, before) if flip else (before, cells, after)
    for tap, piece in enumerate(order):
        buffer_ref[tap * channels : (tap + 1) * channels, place * cols : (place + 1) * cols] = (
            piece.astype(bf16)
        )


def put_gradient(taps_ref, cot_ref, above_ref, below_ref):
    row_count = cot_ref.shape[0]
    put_taps(taps_ref, 0, above_ref[...], True)
    for row in range(row_count):
        put_taps(taps_ref, row + 1, cot_ref[row], True)
    put_taps(taps_ref, row_count + 1, below_ref[...], True)


def weight_body(
    shape, where_ref, latent_ref, cot_ref, above_ref, below_ref, stats_ref, gain_ref, bias_ref,
    act_ref, near_ref, far_ref, taps_ref,
):
    blocks, zones, height, width = shape
    row_count, channels, cols = latent_ref.shape
    core, mine, other, zone_index = [where_ref[i] for i in range(4)]
    values = column_values(stats_ref, gain_ref, bias_ref)
    for row in range(row_count):
        act_ref[:, row * cols : (row + 1) * cols] = activate(latent_ref[row], values)
    put_gradient(taps_ref, cot_ref, above_ref, below_ref)
    tap_width = zones * width // 3

    def store(ref, place, found, block, tap_row):
        first = block * height
        size = max(min(height, channels - first), 0)
        for zone in range(zones):
            low = max(zone * width, tap_row * tap_width)
            high = min((zone + 1) * width, (tap_row + 1) * tap_width)
            if low >= high:
                continue
            at = zone_index ^ zone
            left, right = low - zone * width, high - zone * width
            source = low - tap_row * tap_width
            used = max(min(right - left, 3 * channels - source), 0)
            if size and used:
                ref[place, at, :size, left : left + used] = found[
                    first : first + size, source : source + used
                ]
            if used < right - left:
                ref[place, at, :, left + used : right] = jnp.zeros(
                    (height, right - left - used), f32
                )
            if size < height and used:
                ref[place, at, size:, left : left + used] = jnp.zeros((height - size, used), f32)

    for tap_row in range(3):
        start = (2 - tap_row) * cols
        found = contract(
            act_ref[...], taps_ref[:, start : start + row_count * cols], ((1,), (1,))
        )
        for half in range(2):

            @pl.when(core == half)
            def _():
                for rest in range(blocks // 2):
                    store(near_ref, mine ^ rest, found, half * blocks // 2 + rest, tap_row)

            @pl.when(core != half)
            def _():
                for rest in range(blocks // 2):
                    store(far_ref, other ^ rest, found, half * blocks // 2 + rest, tap_row)


def conv_body(
    ends_ref, act_ref, latent_ref, above_ref, below_ref, stats_ref, gain_ref, bias_ref,
    weight_ref, extra_ref, out_ref, taps_ref, flat_ref,
):
    row_count, channels, cols = latent_ref.shape
    values = column_values(stats_ref, gain_ref, bias_ref)
    for place, ref, end in ((0, above_ref, 0), (row_count + 1, below_ref, 1)):
        keep = ends_ref[end].astype(f32)
        put_taps(taps_ref, place, (activate(ref[...], values).astype(f32) * keep).astype(bf16), False)
    for row in range(row_count):
        put_taps(taps_ref, row + 1, act_ref[:, row * cols : (row + 1) * cols], False)
    for tap_row in range(3):
        flat_ref[tap_row] = weight_ref[tap_row].reshape(3 * channels, channels).T
    extra = jnp.broadcast_to(extra_ref[...], (8, channels)).T[:, :1]
    for row in range(row_count):
        total = latent_ref[row].astype(f32) + extra
        for tap_row in range(3):
            start = (row + tap_row) * cols
            total = total + contract(
                flat_ref[tap_row], taps_ref[:, start : start + cols], ((1,), (0,))
            )
        out_ref[row] = total.astype(bf16)


def backward_body(
    latent_ref, cot_ref, above_ref, below_ref, stats_ref, gain_ref, bias_ref, weight_ref,
    grad_ref, sums_ref, taps_ref, flat_ref,
):
    row_count, channels, cols = latent_ref.shape
    values = column_values(stats_ref, gain_ref, bias_ref)
    put_gradient(taps_ref, cot_ref, above_ref, below_ref)
    for tap_row in range(3):
        flat_ref[tap_row] = jnp.concatenate([weight_ref[tap_row, j] for j in range(3)], axis=1)
    first = jnp.zeros((channels, LANES), f32)
    second = jnp.zeros((channels, LANES), f32)
    for row in range(row_count):
        total = jnp.zeros((channels, cols), f32)
        for tap_row in range(3):
            start = (row + 2 - tap_row) * cols
            total = total + contract(
                flat_ref[tap_row], taps_ref[:, start : start + cols], ((1,), (0,))
            )
        normed, shifted, sigmoid = normalized(latent_ref[row], values)
        grad = total * sigmoid * (1.0 + shifted * (1.0 - sigmoid)) * values[2]
        grad_ref[row] = grad
        first = first + fold_lanes(grad)
        second = second + fold_lanes(grad * normed)
    member = member_matrix(channels)
    first = contract(member, first, ((1,), (0,)), HIGHEST)
    second = contract(member, second, ((1,), (0,)), HIGHEST)
    sums_ref[...] = rows_of(lane_form(first), lane_form(second))


def latent_body(
    total, parts, grad_ref, latent_ref, cot_ref, stats_ref, *refs,
):
    out_ref = refs[-1]
    row_count, channels, _ = latent_ref.shape
    sums = tree_sum([ref[...] for ref in refs[:parts]]) / total
    shape = (8, channels)
    table = rows_of(
        *[
            jnp.broadcast_to(row, shape)
            for row in (stats_ref[0:1], stats_ref[1:2], sums[0:1], sums[1:2])
        ]
    ).T
    mean, inverse, first, second = [table[:, i : i + 1] for i in range(4)]
    for row in range(row_count):
        normed = (latent_ref[row].astype(f32) - mean) * inverse
        change = inverse * (grad_ref[row] - first - normed * second)
        out_ref[row] = (cot_ref[row].astype(f32) + change).astype(bf16)


def place_body(shape, places_ref, cells_ref, *refs):
    blocks, zones, height, width = shape
    out_ref, flat_ref, rows_ref, sem = refs[-4:]
    channels = out_ref.shape[1]
    for block in range(blocks):
        top = pl.multiple_of(places_ref[block] * height, 8)
        for zone in range(zones):
            left = pl.multiple_of(places_ref[blocks + zone] * width, LANES)
            flat_ref[pl.ds(top, height), pl.ds(left, width)] = cells_ref[block, zone]
    tap_width = zones * width // 3
    half = places_ref[blocks + zones]
    first = blocks * height
    sizes = (min(first, channels), channels - min(first, channels))
    for tap in range(9):
        left = (tap // 3) * tap_width + (tap % 3) * channels
        rows_ref[tap] = flat_ref[:, left : left + channels]
        for index in range(2):

            @pl.when(half == index)
            def _():
                pltpu.make_async_copy(
                    rows_ref.at[tap, pl.ds(0, sizes[index])],
                    out_ref.at[tap, pl.ds(index * first, sizes[index])],
                    sem,
                ).start()

    for tap in range(9):
        for index in range(2):

            @pl.when(half == index)
            def _():
                pltpu.make_async_copy(
                    rows_ref.at[tap, pl.ds(0, sizes[index])],
                    out_ref.at[tap, pl.ds(index * first, sizes[index])],
                    sem,
                ).wait()


def scale_body(factor, spread, gain_ref, bias_ref, *refs):
    parts, (scale_ref, steps_ref) = refs[:-2], refs[-2:]
    largest = functools.reduce(jnp.maximum, [ref[3:4] for ref in parts])
    top = jnp.max(largest, axis=1, keepdims=True)
    reach = spread * jnp.max(jnp.abs(gain_ref[...]), axis=1, keepdims=True) + jnp.max(
        jnp.abs(bias_ref[...]), axis=1, keepdims=True
    )
    bound = jnp.maximum(top * reach * factor, 1e-30)
    power = jnp.clip(jnp.floor(jnp.log2(30000.0 / bound)), -100.0, 100.0)
    shape = scale_ref.shape
    scale = jnp.broadcast_to(jnp.exp2(power), shape)
    scale_ref[...] = rows_of(scale, 1.0 / scale)
    steps_ref[...] = rows_of(*[jnp.broadcast_to(ref[4:5], steps_ref.shape) for ref in parts])


def time_body(embed_ref, *refs):
    out_ref = refs[-1]
    columns = embed_ref[...].T
    terms = [
        columns[:, image : image + 1] * ref[2:3] for image, ref in enumerate(refs[:-1])
    ]
    out_ref[...] = tree_sum(terms)


def swap_space(cells, mask):
    count = lax.axis_size("space")
    return lax.ppermute(cells, "space", [(i, i ^ mask) for i in range(count)])


def swap_image(cells, masks):
    images = lax.axis_size("dp")
    count = lax.axis_size("space")
    pairs = [
        (i * count + j, (i ^ masks[j % 2]) * count + j) for i in range(images) for j in range(count)
    ]
    return lax.ppermute(cells, ("dp", "space"), pairs)


def slab_program(
    latent, timesteps, norm_gain, norm_bias, conv_weight, conv_bias, time_weight, cotangent
):
    images, row_count, col_count, channels = latent.shape
    assert images == 1
    per_group = channels // GROUPS
    image_count = lax.axis_size("dp")
    slab_count = lax.axis_size("space")
    zones = slab_count // 2
    bits = image_count.bit_length() - 1
    blocks = 2 * image_count
    height = -(-channels // (8 * blocks)) * 8
    tap_width = -(-3 * channels // LANES) * LANES
    width = 3 * tap_width // zones
    local_count = row_count * col_count * per_group
    total_count = local_count * slab_count
    positions = row_count * col_count

    image_index = lax.axis_index("dp")
    slab_index = lax.axis_index("space")
    core = slab_index % 2
    zone_index = slab_index // 2

    lat = latent.transpose(0, 1, 3, 2)[0]
    cot = cotangent.transpose(0, 1, 3, 2)[0]
    gain = norm_gain.reshape(1, channels)
    bias = norm_bias.reshape(1, channels)
    smem = pl.BlockSpec(memory_space=pltpu.SMEM)
    vmem = pl.BlockSpec(memory_space=pltpu.VMEM)
    small = jax.ShapeDtypeStruct((8, channels), f32)

    down = [(i, i + 1) for i in range(slab_count - 1)]
    up = [(i + 1, i) for i in range(slab_count - 1)]

    flops = 2 * positions * channels * channels * 9
    taps = pltpu.VMEM((3 * channels, (row_count + 2) * col_count), bf16)
    flat = pltpu.VMEM((3, channels, 3 * channels), bf16)

    edges = [
        lax.ppermute(jnp.stack([cot[row], lat[row]]), "space", way)
        for row, way in ((row_count - 1, down), (0, up))
    ]
    (cot_above, lat_above), (cot_below, lat_below) = edges
    own = call(
        functools.partial(stats_body, local_count),
        small,
        (timesteps, lat, cot),
        specs=(smem, vmem, vmem),
        moved=2 * lat.size * 2,
        flops=positions * channels * 60,
    )
    partner = swap_space(own, 1)
    pair = call(functools.partial(merge_body, local_count, None), small, (own, partner))
    parts = [pair]
    for mask in range(1, zones):
        parts.append(swap_space(pair, 2 * mask))
    stats = call(
        functools.partial(merge_body, 2 * local_count, total_count), small, tuple(parts)
    )

    orders = [list(range(bits)), list(range(bits))[::-1]]

    def rest_index(which):
        index = 0
        for step in range(bits):
            shift = jnp.where(which == 0, orders[0][step], orders[1][step])
            index = index * 2 + ((image_index >> shift) & 1)
        return index

    mine, other = rest_index(core), rest_index(1 - core)
    where = jnp.stack([core, mine, other, zone_index]).astype(jnp.int32)
    share_shape = jax.ShapeDtypeStruct((blocks // 2, zones, height, width), f32)
    act, near, far = call(
        functools.partial(weight_body, (blocks, zones, height, width)),
        (jax.ShapeDtypeStruct((channels, positions), bf16), share_shape, share_shape),
        (where, lat, cot, cot_above, cot_below, stats, gain, bias),
        specs=(smem,) + (vmem,) * 7,
        scratch=(taps,),
        flops=flops,
        moved=8 * lat.size,
    )
    everyone = [stats]
    for mask in range(1, image_count):
        everyone.append(swap_image(stats, (mask, mask)))
    scales, steps = call(
        functools.partial(
            scale_body, float(positions * slab_count * image_count), math.sqrt(per_group)
        ),
        (jax.ShapeDtypeStruct((8, LANES), f32), small),
        (gain, bias, *everyone),
    )
    scale, back = scales[0, 0], scales[1, 0]

    middle = blocks // 4
    far_in = swap_space(far[middle:], 1)
    near_in = swap_space(far[:middle], 1)
    sending = near[middle:] + far_in
    keeping = near[:middle] + near_in
    for step in range(bits):
        masks = (1 << orders[0][step], 1 << orders[1][step])
        arrived = swap_image((sending * scale).astype(f16), masks)
        total = keeping + arrived.astype(f32) * back
        middle = total.shape[0] // 2
        sending, keeping = total[middle:], total[:middle]
    total = keeping[0] if bits == 0 else total[0]
    share = total[0]
    arrivals = []
    for mask in range(1, zones):
        arrivals.append(swap_space((total[mask] * scale).astype(f16), 2 * mask))
    for arrived in arrivals:
        share = share + arrived.astype(f32) * back
    share = (share * scale).astype(f16)
    collected = [share]
    for mask in range(1, zones):
        collected.append(swap_space(share, 2 * mask))
    full = jnp.stack(collected)[None]
    for step in reversed(range(bits)):
        masks = (1 << orders[0][step], 1 << orders[1][step])
        full = jnp.concatenate([full, swap_image(full, masks)])
    crossed = swap_space(full, 1)

    def place(cells, whose, half, before):
        spots = [whose ^ rest for rest in range(blocks // 2)]
        spots += [zone_index ^ mask for mask in range(zones)] + [half]
        spots = jnp.stack(spots).astype(jnp.int32)
        anywhere = pl.BlockSpec(memory_space=pl.ANY)
        args = (spots, cells.astype(f32) * back) + before
        rows = blocks // 2 * height
        return pl.pallas_call(
            functools.partial(place_body, (blocks // 2, zones, height, width)),
            out_shape=jax.ShapeDtypeStruct((9, channels, channels), f32),
            in_specs=[smem, vmem] + [anywhere] * len(before),
            out_specs=anywhere,
            scratch_shapes=[
                pltpu.VMEM((rows, zones * width), f32),
                pltpu.VMEM((9, rows, channels), f32),
                pltpu.SemaphoreType.DMA(()),
            ],
            input_output_aliases={2: 0} if before else {},
            compiler_params=pltpu.CompilerParams(vmem_limit_bytes=40 << 20),
            cost_estimate=pl.CostEstimate(
                flops=0, bytes_accessed=36 * channels * channels, transcendentals=0
            ),
        )(*args)

    weight_grad = place(full, mine, core, ())
    weight_grad = place(crossed, other, 1 - core, (weight_grad,))
    weight_grad = weight_grad.reshape(3, 3, channels, channels)

    half_count = channels // 2
    frequency = jnp.exp(-math.log(10000.0) * jnp.arange(half_count, dtype=f32) / half_count)
    angles = steps[:, :half_count] * frequency[None, :]
    embedding = jnp.concatenate([jnp.cos(angles), jnp.sin(angles)], axis=1).astype(bf16)
    time_bias = jnp.dot(embedding[:1], time_weight, preferred_element_type=f32)
    extra = time_bias + conv_bias.reshape(1, channels)
    ends = jnp.stack([slab_index > 0, slab_index < slab_count - 1]).astype(jnp.int32)
    time_grad = call(
        time_body,
        jax.ShapeDtypeStruct((channels, channels), f32),
        (embedding.astype(f32), *everyone),
    )

    grad, sums = call(
        backward_body,
        (jax.ShapeDtypeStruct((row_count, channels, col_count), f32), small),
        (lat, cot, cot_above, cot_below, stats, gain, bias, conv_weight),
        scratch=(taps, flat),
        flops=flops,
        moved=8 * lat.size,
    )
    block_out = call(
        conv_body,
        jax.ShapeDtypeStruct((row_count, channels, col_count), bf16),
        (ends, act, lat, lat_above, lat_below, stats, gain, bias, conv_weight, extra),
        specs=(smem,) + (vmem,) * 9,
        scratch=(taps, flat),
        flops=flops,
        moved=8 * lat.size,
    )
    sums = sums + swap_space(sums, 1)
    others = [sums]
    for mask in range(1, zones):
        others.append(swap_space(sums, 2 * mask))
    latent_grad = call(
        functools.partial(latent_body, total_count, len(others)),
        jax.ShapeDtypeStruct((row_count, channels, col_count), bf16),
        (grad, lat, cot, stats, *others),
        flops=lat.size * 20,
        moved=10 * lat.size,
    )

    block_out = block_out[None].transpose(0, 1, 3, 2)
    latent_grad = latent_grad[None].transpose(0, 1, 3, 2)
    return (block_out, latent_grad, weight_grad, time_grad)


def solution(mesh):
    return jax.shard_map(
        slab_program,
        mesh=mesh,
        in_specs=(
            P("dp", "space", None, None),
            P("dp"),
            P(),
            P(),
            P(),
            P(),
            P(),
            P("dp", "space", None, None),
        ),
        out_specs=(P("dp", "space", None, None), P("dp", "space", None, None), P(), P()),
        check_vma=False,
    )
```

```python
import functools
import math

import jax
import jax.numpy as jnp
from jax import lax
from jax.experimental import pallas as pl
from jax.experimental.pallas import tpu as pltpu
from jax.sharding import PartitionSpec as P


GROUPS = 32
epsilon = 1e-05
f32 = jnp.float32
bf16 = jnp.bfloat16
f16 = jnp.float16
HIGHEST = lax.Precision.HIGHEST
LANES = 128


def contract(a, b, dims, precision=None):
    return lax.dot_general(a, b, (dims, ((), ())), preferred_element_type=f32, precision=precision)


def call(body, outs, args, specs=None, scratch=(), flops=0, moved=0, limit=40 << 20):
    vmem = pl.BlockSpec(memory_space=pltpu.VMEM)
    many = isinstance(outs, (list, tuple))
    return pl.pallas_call(
        body,
        out_shape=tuple(outs) if many else outs,
        in_specs=list(specs) if specs else [vmem] * len(args),
        out_specs=tuple([vmem] * len(outs)) if many else vmem,
        scratch_shapes=list(scratch),
        compiler_params=pltpu.CompilerParams(vmem_limit_bytes=limit),
        cost_estimate=pl.CostEstimate(flops=flops, bytes_accessed=moved, transcendentals=0),
    )(*args)


def member_matrix(channels):
    per_group = channels // GROUPS
    row = lax.broadcasted_iota(jnp.int32, (channels, channels), 0).astype(f32)
    col = lax.broadcasted_iota(jnp.int32, (channels, channels), 1).astype(f32)
    same = jnp.floor((row + 0.5) / per_group) == jnp.floor((col + 0.5) / per_group)
    return jnp.where(same, 1.0, 0.0).astype(f32)


def lane_form(cells):
    ones = jnp.ones((8, cells.shape[1]), f32)
    return contract(ones, cells, ((1,), (1,)), HIGHEST)


def rows_of(*rows):
    height = lax.broadcasted_iota(jnp.int32, rows[0].shape, 0)
    packed = jnp.zeros(rows[0].shape, f32)
    for number, row in enumerate(rows):
        packed = jnp.where(height == number, row, packed)
    return packed


def fold_lanes(cells):
    total = cells[:, :LANES]
    for start in range(LANES, cells.shape[1], LANES):
        total = total + cells[:, start : start + LANES]
    return total


def stats_body(count, step_ref, latent_ref, cot_ref, out_ref):
    row_count, channels, cols = latent_ref.shape
    member = member_matrix(channels)
    ones = jnp.ones((cols, LANES), bf16)
    tall = jnp.ones((8, cols), bf16)
    sums = jnp.zeros((channels, LANES), f32)
    grads = jnp.zeros((8, channels), f32)
    top = jnp.zeros((channels, LANES), f32)
    for row in range(row_count):
        sums = sums + contract(latent_ref[row], ones, ((1,), (0,)))
        grads = grads + contract(tall, cot_ref[row], ((1,), (1,)))
        size = jnp.abs(cot_ref[row].astype(f32))
        for start in range(0, cols, LANES):
            top = jnp.maximum(top, size[:, start : start + LANES])
    mean = contract(member, sums, ((1,), (0,)), HIGHEST) / count
    squares = jnp.zeros((channels, LANES), f32)
    for row in range(row_count):
        centered = latent_ref[row].astype(f32) - mean[:, :1]
        squares = squares + fold_lanes(centered * centered)
    grouped = contract(member, squares, ((1,), (0,)), HIGHEST)
    step = jnp.full((8, channels), step_ref[0].astype(f32))
    largest = jnp.broadcast_to(jnp.max(top), (8, channels))
    out_ref[...] = rows_of(
        lane_form(mean) * (1.0 / LANES), lane_form(grouped), grads, largest, step
    )


def tree_sum(parts):
    while len(parts) > 1:
        parts = [parts[i] + parts[i + 1] for i in range(0, len(parts), 2)]
    return parts[0]


def merge_body(count, total, *refs):
    out_ref = refs[-1]
    parts = [ref[...] for ref in refs[:-1]]
    mean = tree_sum([part[0:1] for part in parts]) / len(parts)
    squares = tree_sum([part[1:2] + count * (part[0:1] - mean) ** 2 for part in parts])
    grads = tree_sum([part[2:3] for part in parts])
    largest = functools.reduce(jnp.maximum, [part[3:4] for part in parts])
    if total:
        squares = lax.rsqrt(squares / total + epsilon)
    shape = parts[0].shape
    out_ref[...] = rows_of(
        *[
            jnp.broadcast_to(row, shape)
            for row in (mean, squares, grads, largest, parts[0][4:5])
        ]
    )


def column_values(stats_ref, gain_ref, bias_ref):
    channels = gain_ref.shape[1]
    shape = (8, channels)
    table = rows_of(
        jnp.broadcast_to(stats_ref[0:1], shape),
        jnp.broadcast_to(stats_ref[1:2], shape),
        jnp.broadcast_to(gain_ref[...], shape),
        jnp.broadcast_to(bias_ref[...], shape),
    ).T
    return [table[:, i : i + 1] for i in range(4)]


def normalized(cells, values):
    mean, inverse, gain, bias = values
    normed = (cells.astype(f32) - mean) * inverse
    shifted = normed * gain + bias
    return normed, shifted, jax.nn.sigmoid(shifted)


def activate(cells, values):
    _, shifted, sigmoid = normalized(cells, values)
    return (shifted * sigmoid).astype(bf16)


def shifted_cols(cells):
    cols = cells.shape[1]
    lane = lax.broadcasted_iota(jnp.int32, cells.shape, 1)
    zero = jnp.zeros_like(cells)
    after = jnp.where(lane == cols - 1, zero, pltpu.roll(cells, cols - 1, 1))
    before = jnp.where(lane == 0, zero, pltpu.roll(cells, 1, 1))
    return after, before


def put_taps(buffer_ref, place, cells, flip):
    channels, cols = cells.shape
    wide = cells.astype(f32)
    after, before = shifted_cols(wide)
    order = (after, cells, before) if flip else (before, cells, after)
    for tap, piece in enumerate(order):
        buffer_ref[tap * channels : (tap + 1) * channels, place * cols : (place + 1) * cols] = (
            piece.astype(bf16)
        )


def put_gradient(taps_ref, cot_ref, above_ref, below_ref):
    row_count = cot_ref.shape[0]
    put_taps(taps_ref, 0, above_ref[...], True)
    for row in range(row_count):
        put_taps(taps_ref, row + 1, cot_ref[row], True)
    put_taps(taps_ref, row_count + 1, below_ref[...], True)


def weight_body(
    shape, where_ref, latent_ref, cot_ref, above_ref, below_ref, stats_ref, gain_ref, bias_ref,
    act_ref, near_ref, far_ref, taps_ref,
):
    blocks, zones, height, width = shape
    row_count, channels, cols = latent_ref.shape
    core, mine, other, zone_index = [where_ref[i] for i in range(4)]
    values = column_values(stats_ref, gain_ref, bias_ref)
    for row in range(row_count):
        act_ref[:, row * cols : (row + 1) * cols] = activate(latent_ref[row], values)
    put_gradient(taps_ref, cot_ref, above_ref, below_ref)
    tap_width = zones * width // 3

    def store(ref, place, found, block, tap_row):
        first = block * height
        size = max(min(height, channels - first), 0)
        for zone in range(zones):
            low = max(zone * width, tap_row * tap_width)
            high = min((zone + 1) * width, (tap_row + 1) * tap_width)
            if low >= high:
                continue
            at = zone_index ^ zone
            left, right = low - zone * width, high - zone * width
            source = low - tap_row * tap_width
            used = max(min(right - left, 3 * channels - source), 0)
            if size and used:
                ref[place, at, :size, left : left + used] = found[
                    first : first + size, source : source + used
                ]
            if used < right - left:
                ref[place, at, :, left + used : right] = jnp.zeros(
                    (height, right - left - used), f32
                )
            if size < height and used:
                ref[place, at, size:, left : left + used] = jnp.zeros((height - size, used), f32)

    for tap_row in range(3):
        start = (2 - tap_row) * cols
        found = contract(
            act_ref[...], taps_ref[:, start : start + row_count * cols], ((1,), (1,))
        )
        for half in range(2):

            @pl.when(core == half)
            def _():
                for rest in range(blocks // 2):
                    store(near_ref, mine ^ rest, found, half * blocks // 2 + rest, tap_row)

            @pl.when(core != half)
            def _():
                for rest in range(blocks // 2):
                    store(far_ref, other ^ rest, found, half * blocks // 2 + rest, tap_row)


def conv_body(
    ends_ref, act_ref, latent_ref, above_ref, below_ref, stats_ref, gain_ref, bias_ref,
    weight_ref, extra_ref, out_ref, taps_ref, flat_ref,
):
    row_count, channels, cols = latent_ref.shape
    values = column_values(stats_ref, gain_ref, bias_ref)
    for place, ref, end in ((0, above_ref, 0), (row_count + 1, below_ref, 1)):
        keep = ends_ref[end].astype(f32)
        put_taps(taps_ref, place, (activate(ref[...], values).astype(f32) * keep).astype(bf16), False)
    for row in range(row_count):
        put_taps(taps_ref, row + 1, act_ref[:, row * cols : (row + 1) * cols], False)
    for tap_row in range(3):
        flat_ref[tap_row] = weight_ref[tap_row].reshape(3 * channels, channels).T
    extra = jnp.broadcast_to(extra_ref[...], (8, channels)).T[:, :1]
    for row in range(row_count):
        total = latent_ref[row].astype(f32) + extra
        for tap_row in range(3):
            start = (row + tap_row) * cols
            total = total + contract(
                flat_ref[tap_row], taps_ref[:, start : start + cols], ((1,), (0,))
            )
        out_ref[row] = total.astype(bf16)


def backward_body(
    latent_ref, cot_ref, above_ref, below_ref, stats_ref, gain_ref, bias_ref, weight_ref,
    grad_ref, sums_ref, taps_ref, flat_ref,
):
    row_count, channels, cols = latent_ref.shape
    values = column_values(stats_ref, gain_ref, bias_ref)
    put_gradient(taps_ref, cot_ref, above_ref, below_ref)
    for tap_row in range(3):
        flat_ref[tap_row] = jnp.concatenate([weight_ref[tap_row, j] for j in range(3)], axis=1)
    first = jnp.zeros((channels, LANES), f32)
    second = jnp.zeros((channels, LANES), f32)
    for row in range(row_count):
        total = jnp.zeros((channels, cols), f32)
        for tap_row in range(3):
            start = (row + 2 - tap_row) * cols
            total = total + contract(
                flat_ref[tap_row], taps_ref[:, start : start + cols], ((1,), (0,))
            )
        normed, shifted, sigmoid = normalized(latent_ref[row], values)
        grad = total * sigmoid * (1.0 + shifted * (1.0 - sigmoid)) * values[2]
        grad_ref[row] = grad
        first = first + fold_lanes(grad)
        second = second + fold_lanes(grad * normed)
    member = member_matrix(channels)
    first = contract(member, first, ((1,), (0,)), HIGHEST)
    second = contract(member, second, ((1,), (0,)), HIGHEST)
    sums_ref[...] = rows_of(lane_form(first), lane_form(second))


def latent_body(total, grad_ref, latent_ref, cot_ref, stats_ref, sums_ref, out_ref):
    row_count, channels, _ = latent_ref.shape
    sums = sums_ref[0:2] / total
    shape = (8, channels)
    table = rows_of(
        *[
            jnp.broadcast_to(row, shape)
            for row in (stats_ref[0:1], stats_ref[1:2], sums[0:1], sums[1:2])
        ]
    ).T
    mean, inverse, first, second = [table[:, i : i + 1] for i in range(4)]
    for row in range(row_count):
        normed = (latent_ref[row].astype(f32) - mean) * inverse
        change = inverse * (grad_ref[row] - first - normed * second)
        out_ref[row] = (cot_ref[row].astype(f32) + change).astype(bf16)


def place_body(shape, count, places_ref, *refs):
    zones, height, width = shape
    cells = refs[:count]
    out_ref, flat_ref, rows_ref, sem = refs[-4:]
    channels = out_ref.shape[1]
    tap_width = zones * width // 3
    whole, part = channels // height, channels % height

    def copies(index, act):
        block = places_ref[index]

        def copy(size):
            return pltpu.make_async_copy(
                rows_ref.at[index, :, pl.ds(0, size)],
                out_ref.at[:, pl.ds(pl.multiple_of(block * height, 8), size)],
                sem.at[index],
            )

        @pl.when(block < whole)
        def _():
            act(copy(height))

        if part:

            @pl.when(block == whole)
            def _():
                act(copy(part))

    for index in range(count):
        for zone in range(zones):
            left = pl.multiple_of(places_ref[count + zone] * width, LANES)
            flat_ref[index, :, pl.ds(left, width)] = cells[index][zone]
        for tap in range(9):
            left = (tap // 3) * tap_width + (tap % 3) * channels
            rows_ref[index, tap] = flat_ref[index, :, left : left + channels]
        copies(index, lambda copy: copy.start())
    for index in range(count):
        copies(index, lambda copy: copy.wait())


def power_of_two(top, factor, spread, gain_ref, bias_ref, shape):
    reach = spread * jnp.max(jnp.abs(gain_ref[...]), axis=1, keepdims=True) + jnp.max(
        jnp.abs(bias_ref[...]), axis=1, keepdims=True
    )
    bound = jnp.maximum(jnp.max(top, axis=1, keepdims=True) * reach * factor, 1e-30)
    power = jnp.clip(jnp.floor(jnp.log2(30000.0 / bound)), -100.0, 100.0)
    scale = jnp.broadcast_to(jnp.exp2(power), shape)
    return rows_of(scale, 1.0 / scale)


def scale_body(factor, spread, gain_ref, bias_ref, *refs):
    parts, (scale_ref, steps_ref) = refs[:-2], refs[-2:]
    top = functools.reduce(jnp.maximum, [ref[3:4] for ref in parts])
    scale_ref[...] = power_of_two(top, factor, spread, gain_ref, bias_ref, scale_ref.shape)
    steps_ref[...] = rows_of(*[jnp.broadcast_to(ref[4:5], steps_ref.shape) for ref in parts])


def gather_body(sums_ref, partner_ref, *refs):
    parts, out_ref = refs[:-1], refs[-1]
    top = functools.reduce(jnp.maximum, [ref[3:4] for ref in parts])
    rows = [sums_ref[0:1] + partner_ref[0:1], sums_ref[1:2] + partner_ref[1:2], top]
    rows += [ref[2:3] for ref in parts]
    out_ref[...] = rows_of(*[jnp.broadcast_to(row, out_ref.shape) for row in rows])


def total_body(factor, spread, gain_ref, bias_ref, *refs):
    parts, (total_ref, scale_ref) = refs[:-2], refs[-2:]
    top = functools.reduce(jnp.maximum, [ref[2:3] for ref in parts])
    scale_ref[...] = power_of_two(top, factor, spread, gain_ref, bias_ref, scale_ref.shape)
    total_ref[...] = tree_sum([ref[...] for ref in parts])


def time_body(count, embed_ref, total_ref, out_ref):
    columns = embed_ref[...].T
    terms = [columns[:, i : i + 1] * total_ref[3 + i : 4 + i] for i in range(count)]
    out_ref[...] = tree_sum(terms)


def swap_space(cells, mask):
    count = lax.axis_size("space")
    return lax.ppermute(cells, "space", [(i, i ^ mask) for i in range(count)])


def swap_image(cells, masks):
    images = lax.axis_size("dp")
    count = lax.axis_size("space")
    pairs = [
        (i * count + j, (i ^ masks[j % 2]) * count + j) for i in range(images) for j in range(count)
    ]
    return lax.ppermute(cells, ("dp", "space"), pairs)


def slab_program(
    latent, timesteps, norm_gain, norm_bias, conv_weight, conv_bias, time_weight, cotangent
):
    images, row_count, col_count, channels = latent.shape
    assert images == 1
    per_group = channels // GROUPS
    image_count = lax.axis_size("dp")
    slab_count = lax.axis_size("space")
    zones = slab_count // 2
    bits = image_count.bit_length() - 1
    blocks = 2 * image_count
    height = -(-channels // (8 * blocks)) * 8
    tap_width = -(-3 * channels // LANES) * LANES
    width = 3 * tap_width // zones
    local_count = row_count * col_count * per_group
    total_count = local_count * slab_count
    positions = row_count * col_count

    image_index = lax.axis_index("dp")
    slab_index = lax.axis_index("space")
    core = slab_index % 2
    zone_index = slab_index // 2

    lat = latent.transpose(0, 1, 3, 2)[0]
    cot = cotangent.transpose(0, 1, 3, 2)[0]
    gain = norm_gain.reshape(1, channels)
    bias = norm_bias.reshape(1, channels)
    smem = pl.BlockSpec(memory_space=pltpu.SMEM)
    vmem = pl.BlockSpec(memory_space=pltpu.VMEM)
    small = jax.ShapeDtypeStruct((8, channels), f32)

    down = [(i, i + 1) for i in range(slab_count - 1)]
    up = [(i + 1, i) for i in range(slab_count - 1)]

    flops = 2 * positions * channels * channels * 9
    taps = pltpu.VMEM((3 * channels, (row_count + 2) * col_count), bf16)
    flat = pltpu.VMEM((3, channels, 3 * channels), bf16)

    cot_above = lax.ppermute(cot[row_count - 1], "space", down)
    cot_below = lax.ppermute(cot[0], "space", up)
    lat_above = lax.ppermute(lat[row_count - 1], "space", down)
    lat_below = lax.ppermute(lat[0], "space", up)
    own = call(
        functools.partial(stats_body, local_count),
        small,
        (timesteps, lat, cot),
        specs=(smem, vmem, vmem),
        moved=2 * lat.size * 2,
        flops=positions * channels * 60,
    )
    partner = swap_space(own, 1)
    pair = call(functools.partial(merge_body, local_count, None), small, (own, partner))
    parts = [pair]
    for mask in range(1, zones):
        parts.append(swap_space(pair, 2 * mask))
    stats = call(
        functools.partial(merge_body, 2 * local_count, total_count), small, tuple(parts)
    )

    orders = [list(range(bits)), list(range(bits))[::-1]]

    def rest_index(which):
        index = 0
        for step in range(bits):
            shift = jnp.where(which == 0, orders[0][step], orders[1][step])
            index = index * 2 + ((image_index >> shift) & 1)
        return index

    mine, other = rest_index(core), rest_index(1 - core)
    where = jnp.stack([core, mine, other, zone_index]).astype(jnp.int32)
    share_shape = jax.ShapeDtypeStruct((blocks // 2, zones, height, width), f32)
    act, near, far = call(
        functools.partial(weight_body, (blocks, zones, height, width)),
        (jax.ShapeDtypeStruct((channels, positions), bf16), share_shape, share_shape),
        (where, lat, cot, cot_above, cot_below, stats, gain, bias),
        specs=(smem,) + (vmem,) * 7,
        scratch=(taps,),
        flops=flops,
        moved=8 * lat.size,
    )
    everyone = [pair]
    for mask in range(1, image_count):
        everyone.append(swap_image(pair, (mask, mask)))
    factor, spread = float(positions * slab_count * image_count), math.sqrt(per_group)
    scales_shape = jax.ShapeDtypeStruct((8, LANES), f32)
    scales, steps = call(
        functools.partial(scale_body, factor, spread),
        (scales_shape, jax.ShapeDtypeStruct((-(-image_count // 8) * 8, channels), f32)),
        (gain, bias, *everyone),
    )
    scale, back = scales[0, 0], scales[1, 0]

    grad, sums = call(
        backward_body,
        (jax.ShapeDtypeStruct((row_count, channels, col_count), f32), small),
        (lat, cot, cot_above, cot_below, stats, gain, bias, conv_weight),
        scratch=(taps, flat),
        flops=flops,
        moved=8 * lat.size,
    )
    sums_partner = swap_space(sums, 1)
    message = jax.ShapeDtypeStruct((-(-(3 + image_count) // 8) * 8, channels), f32)
    gathered = [call(gather_body, message, (sums, sums_partner, *everyone))]
    for mask in range(1, zones):
        gathered.append(swap_space(gathered[0], 2 * mask))
    totals, line_scales = call(
        functools.partial(total_body, factor, spread),
        (message, scales_shape),
        (gain, bias, *gathered),
    )
    line_scale, line_back = line_scales[0, 0], line_scales[1, 0]

    middle = blocks // 4
    far_in = swap_space(far[middle:], 1)
    near_in = swap_space(far[:middle], 1)
    sending = near[middle:] + far_in
    keeping = near[:middle] + near_in
    for step in range(bits):
        masks = (1 << orders[0][step], 1 << orders[1][step])
        arrived = swap_image((sending * scale).astype(f16), masks)
        total = keeping + arrived.astype(f32) * back
        middle = total.shape[0] // 2
        sending, keeping = total[middle:], total[:middle]
    total = total[0] if bits else keeping[0]
    share = total[0]
    arrivals = []
    for mask in range(1, zones):
        arrivals.append(swap_space((total[mask] * line_scale).astype(f16), 2 * mask))
    for arrived in arrivals:
        share = share + arrived.astype(f32) * line_back
    share = (share * line_scale).astype(f16)
    collected = [share]
    for mask in range(1, zones):
        collected.append(swap_space(share, 2 * mask))
    pieces = [jnp.stack(collected)]
    for step in reversed(range(bits)):
        masks = (1 << orders[0][step], 1 << orders[1][step])
        arrived = []
        for piece in pieces:
            arrived.append(swap_image(piece, masks))
        pieces = pieces + arrived
    crossed = []
    for piece in pieces:
        crossed.append(swap_space(piece, 1))
    half_blocks = blocks // 2
    spots = [core * half_blocks + (mine ^ rest) for rest in range(half_blocks)]
    cross_spots = [(1 - core) * half_blocks + (other ^ rest) for rest in range(half_blocks)]
    zone_spots = [zone_index ^ mask for mask in range(zones)]

    def place(cells, at, before):
        table = jnp.stack(at + zone_spots).astype(jnp.int32)
        anywhere = pl.BlockSpec(memory_space=pl.ANY)
        count = len(cells)
        return pl.pallas_call(
            functools.partial(place_body, (zones, height, width), count),
            out_shape=jax.ShapeDtypeStruct((9, channels, channels), f32),
            in_specs=[smem] + [vmem] * count + [anywhere] * len(before),
            out_specs=anywhere,
            scratch_shapes=[
                pltpu.VMEM((count, height, zones * width), f32),
                pltpu.VMEM((count, 9, height, channels), f32),
                pltpu.SemaphoreType.DMA((count,)),
            ],
            input_output_aliases={1 + count: 0} if before else {},
            compiler_params=pltpu.CompilerParams(vmem_limit_bytes=40 << 20),
            cost_estimate=pl.CostEstimate(
                flops=0,
                bytes_accessed=8 * count * zones * height * width,
                transcendentals=0,
            ),
        )(table, *[piece.astype(f32) * line_back for piece in cells], *before)

    weight_grad = place(
        pieces[:-1] + crossed[:-1], spots[:-1] + cross_spots[:-1], ()
    )
    weight_grad = place(pieces[-1:] + crossed[-1:], spots[-1:] + cross_spots[-1:], (weight_grad,))
    weight_grad = weight_grad.reshape(3, 3, channels, channels)

    half_count = channels // 2
    frequency = jnp.exp(-math.log(10000.0) * jnp.arange(half_count, dtype=f32) / half_count)
    angles = steps[:, :half_count] * frequency[None, :]
    embedding = jnp.concatenate([jnp.cos(angles), jnp.sin(angles)], axis=1).astype(bf16)
    time_bias = jnp.dot(embedding[:1], time_weight, preferred_element_type=f32)
    extra = time_bias + conv_bias.reshape(1, channels)
    ends = jnp.stack([slab_index > 0, slab_index < slab_count - 1]).astype(jnp.int32)
    time_grad = call(
        functools.partial(time_body, image_count),
        jax.ShapeDtypeStruct((channels, channels), f32),
        (embedding.astype(f32), totals),
    )
    block_out = call(
        conv_body,
        jax.ShapeDtypeStruct((row_count, channels, col_count), bf16),
        (ends, act, lat, lat_above, lat_below, stats, gain, bias, conv_weight, extra),
        specs=(smem,) + (vmem,) * 9,
        scratch=(taps, flat),
        flops=flops,
        moved=8 * lat.size,
    )
    latent_grad = call(
        functools.partial(latent_body, total_count),
        jax.ShapeDtypeStruct((row_count, channels, col_count), bf16),
        (grad, lat, cot, stats, totals),
        flops=lat.size * 20,
        moved=10 * lat.size,
    )

    block_out = block_out[None].transpose(0, 1, 3, 2)
    latent_grad = latent_grad[None].transpose(0, 1, 3, 2)
    return (block_out, latent_grad, weight_grad, time_grad)


def solution(mesh):
    return jax.shard_map(
        slab_program,
        mesh=mesh,
        in_specs=(
            P("dp", "space", None, None),
            P("dp"),
            P(),
            P(),
            P(),
            P(),
            P(),
            P("dp", "space", None, None),
        ),
        out_specs=(P("dp", "space", None, None), P("dp", "space", None, None), P(), P()),
        check_vma=False,
    )
```

```python
import functools
import math

import jax
import jax.numpy as jnp
from jax import lax
from jax.experimental import pallas as pl
from jax.experimental.pallas import tpu as pltpu
from jax.sharding import PartitionSpec as P


GROUPS = 32
epsilon = 1e-05
f32 = jnp.float32
bf16 = jnp.bfloat16
f16 = jnp.float16
HIGHEST = lax.Precision.HIGHEST
LANES = 128
NOTE = 32


def contract(a, b, dims, precision=None):
    return lax.dot_general(a, b, (dims, ((), ())), preferred_element_type=f32, precision=precision)


def call(body, outs, args, specs=None, scratch=(), flops=0, moved=0, limit=40 << 20):
    vmem = pl.BlockSpec(memory_space=pltpu.VMEM)
    many = isinstance(outs, (list, tuple))
    return pl.pallas_call(
        body,
        out_shape=tuple(outs) if many else outs,
        in_specs=list(specs) if specs else [vmem] * len(args),
        out_specs=tuple([vmem] * len(outs)) if many else vmem,
        scratch_shapes=list(scratch),
        compiler_params=pltpu.CompilerParams(vmem_limit_bytes=limit),
        cost_estimate=pl.CostEstimate(flops=flops, bytes_accessed=moved, transcendentals=0),
    )(*args)


def member_matrix(channels):
    per_group = channels // GROUPS
    row = lax.broadcasted_iota(jnp.int32, (channels, channels), 0).astype(f32)
    col = lax.broadcasted_iota(jnp.int32, (channels, channels), 1).astype(f32)
    same = jnp.floor((row + 0.5) / per_group) == jnp.floor((col + 0.5) / per_group)
    return jnp.where(same, 1.0, 0.0).astype(f32)


def lane_form(cells):
    ones = jnp.ones((8, cells.shape[1]), f32)
    return contract(ones, cells, ((1,), (1,)), HIGHEST)


def rows_of(*rows):
    height = lax.broadcasted_iota(jnp.int32, rows[0].shape, 0)
    packed = jnp.zeros(rows[0].shape, f32)
    for number, row in enumerate(rows):
        packed = jnp.where(height == number, row, packed)
    return packed


def fold_lanes(cells):
    total = cells[:, :LANES]
    for start in range(LANES, cells.shape[1], LANES):
        total = total + cells[:, start : start + LANES]
    return total


def stats_body(
    count, step_ref, latent_hbm, cot_hbm, out_ref, down_ref, up_ref, latent_ref, cot_ref, sem
):
    row_count, channels, cols = latent_ref.shape
    loads = []
    for number, (source, target) in enumerate(((latent_hbm, latent_ref), (cot_hbm, cot_ref))):
        for row in range(row_count):
            load = pltpu.make_async_copy(source.at[row], target.at[row], sem.at[number, row])
            load.start()
            loads.append(load)
    member = member_matrix(channels)
    ones = jnp.ones((cols, LANES), bf16)
    tall = jnp.ones((8, cols), bf16)
    sums = jnp.zeros((channels, LANES), f32)
    for row in range(row_count):
        loads[row].wait()
        sums = sums + contract(latent_ref[row], ones, ((1,), (0,)))
    mean = contract(member, sums, ((1,), (0,)), HIGHEST) / count
    grads = jnp.zeros((8, channels), f32)
    top = jnp.zeros((channels, LANES), f32)
    for row in range(row_count):
        loads[row_count + row].wait()
        grads = grads + contract(tall, cot_ref[row], ((1,), (1,)))
        size = jnp.abs(cot_ref[row].astype(f32))
        for start in range(0, cols, LANES):
            top = jnp.maximum(top, size[:, start : start + LANES])
    for ref, row in ((down_ref, row_count - 1), (up_ref, 0)):
        ref[0] = cot_ref[row]
        ref[1] = latent_ref[row]
    squares = jnp.zeros((channels, LANES), f32)
    for row in range(row_count):
        centered = latent_ref[row].astype(f32) - mean[:, :1]
        squares = squares + fold_lanes(centered * centered)
    grouped = contract(member, squares, ((1,), (0,)), HIGHEST)
    step = jnp.full((8, channels), step_ref[0].astype(f32))
    largest = jnp.broadcast_to(jnp.max(top), (8, channels))
    out_ref[...] = rows_of(
        lane_form(mean) * (1.0 / LANES), lane_form(grouped), grads, largest, step
    )


def tree_sum(parts):
    while len(parts) > 1:
        parts = [parts[i] + parts[i + 1] for i in range(0, len(parts), 2)]
    return parts[0]


def merge_body(count, total, parts, *refs):
    refs, outs = refs[:parts], refs[parts:]
    parts = [ref[...] for ref in refs]
    mean = tree_sum([part[0:1] for part in parts]) / len(parts)
    squares = tree_sum([part[1:2] + count * (part[0:1] - mean) ** 2 for part in parts])
    if total:
        squares = lax.rsqrt(squares / total + epsilon)
    grads = tree_sum([part[2:3] for part in parts])
    largest = functools.reduce(jnp.maximum, [part[3:4] for part in parts])
    step = parts[0][4:5]
    shape = parts[0].shape
    rows = (mean, squares, grads, largest, step)
    outs[0][...] = rows_of(*[jnp.broadcast_to(row, shape) for row in rows])
    if len(outs) > 1:
        table_ref = outs[1]
        channels = shape[1]
        table_ref[...] = jnp.zeros(table_ref.shape, f32)
        table_ref[0:1, :channels] = grads
        table_ref[0:1, channels : channels + NOTE] = step[:, :NOTE]
        table_ref[0:1, channels + NOTE : channels + 2 * NOTE] = largest[:, :NOTE]


def column_values(stats_ref, gain_ref, bias_ref):
    channels = gain_ref.shape[0]
    shape = (8, channels)
    table = rows_of(
        jnp.broadcast_to(stats_ref[0:1], shape),
        jnp.broadcast_to(stats_ref[1:2], shape),
        jnp.broadcast_to(gain_ref[...], shape),
        jnp.broadcast_to(bias_ref[...], shape),
    ).T
    return [table[:, i : i + 1] for i in range(4)]


def normalized(cells, values):
    mean, inverse, gain, bias = values
    normed = (cells.astype(f32) - mean) * inverse
    shifted = normed * gain + bias
    return normed, shifted, jax.nn.sigmoid(shifted)


def activate(cells, values):
    _, shifted, sigmoid = normalized(cells, values)
    return (shifted * sigmoid).astype(bf16)


def shifted_cols(cells):
    cols = cells.shape[1]
    lane = lax.broadcasted_iota(jnp.int32, cells.shape, 1)
    zero = jnp.zeros_like(cells)
    after = jnp.where(lane == cols - 1, zero, pltpu.roll(cells, cols - 1, 1))
    before = jnp.where(lane == 0, zero, pltpu.roll(cells, 1, 1))
    return after, before


def put_taps(buffer_ref, place, cells, flip):
    channels, cols = cells.shape
    wide = cells.astype(f32)
    after, before = shifted_cols(wide)
    order = (after, cells, before) if flip else (before, cells, after)
    for tap, piece in enumerate(order):
        buffer_ref[tap * channels : (tap + 1) * channels, place * cols : (place + 1) * cols] = (
            piece.astype(bf16)
        )


def put_gradient(taps_ref, cot_ref, above_ref, below_ref):
    row_count = cot_ref.shape[0]
    put_taps(taps_ref, 0, above_ref[0], True)
    for row in range(row_count):
        put_taps(taps_ref, row + 1, cot_ref[row], True)
    put_taps(taps_ref, row_count + 1, below_ref[0], True)


def weight_body(
    shape, where_ref, latent_ref, cot_ref, above_ref, below_ref, stats_ref, gain_ref, bias_ref,
    act_ref, near_ref, far_ref, taps_ref,
):
    blocks, zones, height, width = shape
    row_count, channels, cols = latent_ref.shape
    core, mine, other, zone_index = [where_ref[i] for i in range(4)]
    values = column_values(stats_ref, gain_ref, bias_ref)
    for row in range(row_count):
        act_ref[:, row * cols : (row + 1) * cols] = activate(latent_ref[row], values)
    put_gradient(taps_ref, cot_ref, above_ref, below_ref)
    tap_width = zones * width // 3

    def store(ref, place, found, block, tap_row):
        first = block * height
        size = max(min(height, channels - first), 0)
        for zone in range(zones):
            low = max(zone * width, tap_row * tap_width)
            high = min((zone + 1) * width, (tap_row + 1) * tap_width)
            if low >= high:
                continue
            at = zone_index ^ zone
            left, right = low - zone * width, high - zone * width
            source = low - tap_row * tap_width
            used = max(min(right - left, 3 * channels - source), 0)
            if size and used:
                ref[place, at, :size, left : left + used] = found[
                    first : first + size, source : source + used
                ]
            if used < right - left:
                ref[place, at, :, left + used : right] = jnp.zeros(
                    (height, right - left - used), f32
                )
            if size < height and used:
                ref[place, at, size:, left : left + used] = jnp.zeros((height - size, used), f32)

    for tap_row in range(3):
        start = (2 - tap_row) * cols
        found = contract(
            act_ref[...], taps_ref[:, start : start + row_count * cols], ((1,), (1,))
        )
        for half in range(2):

            @pl.when(core == half)
            def _():
                for rest in range(blocks // 2):
                    store(near_ref, mine ^ rest, found, half * blocks // 2 + rest, tap_row)

            @pl.when(core != half)
            def _():
                for rest in range(blocks // 2):
                    store(far_ref, other ^ rest, found, half * blocks // 2 + rest, tap_row)


def conv_body(
    ends_ref, act_ref, latent_ref, above_ref, below_ref, stats_ref, gain_ref, bias_ref,
    weight_ref, extra_ref, out_ref, taps_ref, flat_ref,
):
    row_count, channels, cols = latent_ref.shape
    values = column_values(stats_ref, gain_ref, bias_ref)
    for place, ref, end in ((0, above_ref, 0), (row_count + 1, below_ref, 1)):
        keep = ends_ref[end].astype(f32)
        put_taps(taps_ref, place, (activate(ref[1], values).astype(f32) * keep).astype(bf16), False)
    for row in range(row_count):
        put_taps(taps_ref, row + 1, act_ref[:, row * cols : (row + 1) * cols], False)
    for tap_row in range(3):
        flat_ref[tap_row] = weight_ref[tap_row].reshape(3 * channels, channels).T
    extra = jnp.broadcast_to(extra_ref[...], (8, channels)).T[:, :1]
    for row in range(row_count):
        total = latent_ref[row].astype(f32) + extra
        for tap_row in range(3):
            start = (row + tap_row) * cols
            total = total + contract(
                flat_ref[tap_row], taps_ref[:, start : start + cols], ((1,), (0,))
            )
        out_ref[row] = total.astype(bf16)


def backward_body(
    latent_ref, taps_ref, stats_ref, gain_ref, bias_ref, weight_ref, grad_ref, sums_ref, flat_ref
):
    row_count, channels, cols = latent_ref.shape
    values = column_values(stats_ref, gain_ref, bias_ref)
    for tap_row in range(3):
        flat_ref[tap_row] = jnp.concatenate([weight_ref[tap_row, j] for j in range(3)], axis=1)
    first = jnp.zeros((channels, LANES), f32)
    second = jnp.zeros((channels, LANES), f32)
    for row in range(row_count):
        total = jnp.zeros((channels, cols), f32)
        for tap_row in range(3):
            start = (row + 2 - tap_row) * cols
            total = total + contract(
                flat_ref[tap_row], taps_ref[:, start : start + cols], ((1,), (0,))
            )
        normed, shifted, sigmoid = normalized(latent_ref[row], values)
        grad = total * sigmoid * (1.0 + shifted * (1.0 - sigmoid)) * values[2]
        grad_ref[row] = grad
        first = first + fold_lanes(grad)
        second = second + fold_lanes(grad * normed)
    member = member_matrix(channels)
    first = contract(member, first, ((1,), (0,)), HIGHEST)
    second = contract(member, second, ((1,), (0,)), HIGHEST)
    sums_ref[...] = rows_of(lane_form(first), lane_form(second))


def latent_body(total, grad_ref, latent_ref, cot_ref, stats_ref, sums_ref, out_ref):
    row_count, channels, _ = latent_ref.shape
    sums = sums_ref[0:2] / total
    shape = (8, channels)
    table = rows_of(
        *[
            jnp.broadcast_to(row, shape)
            for row in (stats_ref[0:1], stats_ref[1:2], sums[0:1], sums[1:2])
        ]
    ).T
    mean, inverse, first, second = [table[:, i : i + 1] for i in range(4)]
    for row in range(row_count):
        normed = (latent_ref[row].astype(f32) - mean) * inverse
        change = inverse * (grad_ref[row] - first - normed * second)
        out_ref[row] = (cot_ref[row].astype(f32) + change).astype(bf16)


def place_body(shape, count, places_ref, *refs):
    zones, height, width = shape
    cells = refs[:count]
    out_ref, flat_ref, rows_ref, sem = refs[-4:]
    channels = out_ref.shape[1]
    tap_width = zones * width // 3
    whole, part = channels // height, channels % height

    def copies(index, act):
        block = places_ref[index]

        def copy(size):
            return pltpu.make_async_copy(
                rows_ref.at[index, :, pl.ds(0, size)],
                out_ref.at[:, pl.ds(pl.multiple_of(block * height, 8), size)],
                sem.at[index],
            )

        @pl.when(block < whole)
        def _():
            act(copy(height))

        if part:

            @pl.when(block == whole)
            def _():
                act(copy(part))

    for index in range(count):
        for zone in range(zones):
            left = pl.multiple_of(places_ref[count + zone] * width, LANES)
            flat_ref[index, :, pl.ds(left, width)] = cells[index][zone]
        for tap in range(9):
            left = (tap // 3) * tap_width + (tap % 3) * channels
            rows_ref[index, tap] = flat_ref[index, :, left : left + channels]
        copies(index, lambda copy: copy.start())
    for index in range(count):
        copies(index, lambda copy: copy.wait())


def power_of_two(top, factor, spread, gain_ref, bias_ref, shape):
    gain = jnp.max(jnp.abs(gain_ref[...][None, :]), axis=1, keepdims=True)
    bias = jnp.max(jnp.abs(bias_ref[...][None, :]), axis=1, keepdims=True)
    reach = spread * gain + bias
    bound = jnp.maximum(top * reach * factor, 1e-30)
    power = jnp.clip(jnp.floor(jnp.log2(30000.0 / bound)), -100.0, 100.0)
    scale = jnp.broadcast_to(jnp.exp2(power), shape)
    return rows_of(scale, 1.0 / scale)


def largest_note(table, channels):
    return jnp.max(
        jnp.max(table[:, channels + NOTE : channels + 2 * NOTE], axis=1, keepdims=True),
        axis=0,
        keepdims=True,
    )


def spread_body(
    known, masks, factor, spread, where_ref, gain_ref, bias_ref, mine_ref, other_ref,
    table_ref, scale_ref, steps_ref,
):
    channels = gain_ref.shape[0]
    table_ref[...] = mine_ref[...]
    for core in range(2):

        @pl.when(where_ref[0] == core)
        def _():
            for row in known[core]:
                at = row ^ masks[core]
                table_ref[at : at + 1] = other_ref[row : row + 1]

    table = table_ref[...]
    scale_ref[...] = power_of_two(
        largest_note(table, channels), factor, spread, gain_ref, bias_ref, scale_ref.shape
    )
    steps_ref[...] = jnp.broadcast_to(table[:, channels : channels + 1], steps_ref.shape)


def gather_body(images, sums_ref, partner_ref, table_ref, out_ref):
    channels = sums_ref.shape[1]
    table = table_ref[...]
    rows = [sums_ref[0:1] + partner_ref[0:1], sums_ref[1:2] + partner_ref[1:2]]
    rows += [largest_note(table, channels)]
    rows += [table[i : i + 1, :channels] for i in range(images)]
    out_ref[...] = rows_of(*[jnp.broadcast_to(row, out_ref.shape) for row in rows])


def total_body(factor, spread, gain_ref, bias_ref, *refs):
    parts, (total_ref, scale_ref) = refs[:-2], refs[-2:]
    top = functools.reduce(jnp.maximum, [ref[2:3, 0:1] for ref in parts])
    scale_ref[...] = power_of_two(top, factor, spread, gain_ref, bias_ref, scale_ref.shape)
    total_ref[...] = tree_sum([ref[...] for ref in parts])


def time_body(count, embed_ref, total_ref, out_ref):
    columns = embed_ref[...].T
    terms = [columns[:, i : i + 1] * total_ref[3 + i : 4 + i] for i in range(count)]
    out_ref[...] = tree_sum(terms)


def swap_space(cells, mask):
    count = lax.axis_size("space")
    return lax.ppermute(cells, "space", [(i, i ^ mask) for i in range(count)])


def swap_image(cells, masks):
    images = lax.axis_size("dp")
    count = lax.axis_size("space")
    pairs = [
        (i * count + j, (i ^ masks[j % 2]) * count + j) for i in range(images) for j in range(count)
    ]
    return lax.ppermute(cells, ("dp", "space"), pairs)


def slab_program(
    latent, timesteps, norm_gain, norm_bias, conv_weight, conv_bias, time_weight, cotangent
):
    images, row_count, col_count, channels = latent.shape
    assert images == 1
    per_group = channels // GROUPS
    image_count = lax.axis_size("dp")
    slab_count = lax.axis_size("space")
    zones = slab_count // 2
    bits = image_count.bit_length() - 1
    blocks = 2 * image_count
    height = -(-channels // (8 * blocks)) * 8
    tap_width = -(-3 * channels // LANES) * LANES
    width = 3 * tap_width // zones
    local_count = row_count * col_count * per_group
    total_count = local_count * slab_count
    positions = row_count * col_count

    image_index = lax.axis_index("dp")
    slab_index = lax.axis_index("space")
    core = slab_index % 2
    zone_index = slab_index // 2

    lat = latent.transpose(0, 1, 3, 2)[0]
    cot = cotangent.transpose(0, 1, 3, 2)[0]
    gain, bias = norm_gain, norm_bias
    smem = pl.BlockSpec(memory_space=pltpu.SMEM)
    vmem = pl.BlockSpec(memory_space=pltpu.VMEM)
    small = jax.ShapeDtypeStruct((8, channels), f32)

    down = [(i, i + 1) for i in range(slab_count - 1)]
    up = [(i + 1, i) for i in range(slab_count - 1)]

    flops = 2 * positions * channels * channels * 9
    taps = pltpu.VMEM((3 * channels, (row_count + 2) * col_count), bf16)
    flat = pltpu.VMEM((3, channels, 3 * channels), bf16)

    edge = jax.ShapeDtypeStruct((2, channels, col_count), bf16)
    anywhere = pl.BlockSpec(memory_space=pl.ANY)
    slab = pltpu.VMEM((row_count, channels, col_count), bf16)
    own, edge_down, edge_up = call(
        functools.partial(stats_body, local_count),
        (small, edge, edge),
        (timesteps, lat, cot),
        specs=(smem, anywhere, anywhere),
        scratch=(slab, slab, pltpu.SemaphoreType.DMA((2, row_count))),
        moved=2 * lat.size * 2,
        flops=positions * channels * 60,
        limit=12 << 20,
    )
    partner = swap_space(own, 1)
    above = lax.ppermute(edge_down, "space", down)
    below = lax.ppermute(edge_up, "space", up)
    table_shape = jax.ShapeDtypeStruct((-(-image_count // 8) * 8, channels + 2 * NOTE), f32)
    pair, table = call(
        functools.partial(merge_body, local_count, None, 2),
        (small, table_shape),
        (own, partner),
        limit=4 << 20,
    )
    parts = [pair]
    for mask in range(1, zones):
        parts.append(swap_space(pair, 2 * mask))
    stats = call(
        functools.partial(merge_body, 2 * local_count, total_count, zones),
        (small,),
        tuple(parts),
        limit=4 << 20,
    )[0]

    orders = [list(range(bits)), list(range(bits))[::-1]]

    def rest_index(which):
        index = 0
        for step in range(bits):
            shift = jnp.where(which == 0, orders[0][step], orders[1][step])
            index = index * 2 + ((image_index >> shift) & 1)
        return index

    mine, other = rest_index(core), rest_index(1 - core)
    where = jnp.stack([core, mine, other, zone_index]).astype(jnp.int32)
    share_shape = jax.ShapeDtypeStruct((blocks // 2, zones, height, width), f32)
    taps_shape = jax.ShapeDtypeStruct((3 * channels, (row_count + 2) * col_count), bf16)
    act, near, far, grad_taps = call(
        functools.partial(weight_body, (blocks, zones, height, width)),
        (jax.ShapeDtypeStruct((channels, positions), bf16), share_shape, share_shape, taps_shape),
        (where, lat, cot, above, below, stats, gain, bias),
        specs=(smem,) + (vmem,) * 7,
        flops=flops,
        moved=8 * lat.size,
        limit=20 << 20,
    )
    factor, spread = float(positions * slab_count * image_count), math.sqrt(per_group)
    scales_shape = jax.ShapeDtypeStruct((8, LANES), f32)
    steps_shape = jax.ShapeDtypeStruct((table_shape.shape[0], channels), f32)
    known = ([0], [0])
    scales = []
    for step in range(bits):
        masks = (1 << orders[0][step], 1 << orders[1][step])
        arrived = swap_image(table, masks)
        table, found, steps = call(
            functools.partial(spread_body, known, masks, factor, spread),
            (table_shape, scales_shape, steps_shape),
            (where, gain, bias, table, arrived),
            specs=(smem,) + (vmem,) * 4,
            limit=4 << 20,
        )
        scales.append((found[0, 0], found[1, 0]))
        known = tuple(rows + [row ^ mask for row in rows] for rows, mask in zip(known, masks))

    grad, sums = call(
        backward_body,
        (jax.ShapeDtypeStruct((row_count, channels, col_count), f32), small),
        (lat, grad_taps, stats, gain, bias, conv_weight),
        scratch=(flat,),
        flops=flops,
        moved=8 * lat.size,
        limit=20 << 20,
    )
    sums_partner = swap_space(sums, 1)
    message = jax.ShapeDtypeStruct((-(-(3 + image_count) // 8) * 8, channels), f32)
    gathered = [
        call(
            functools.partial(gather_body, image_count),
            message,
            (sums, sums_partner, table),
            limit=4 << 20,
        )
    ]
    for mask in range(1, zones):
        gathered.append(swap_space(gathered[0], 2 * mask))
    totals, line_scales = call(
        functools.partial(total_body, factor, spread),
        (message, scales_shape),
        (gain, bias, *gathered),
        limit=4 << 20,
    )
    line_scale, line_back = line_scales[0, 0], line_scales[1, 0]

    middle = blocks // 4
    far_in = swap_space(far[middle:], 1)
    near_in = swap_space(far[:middle], 1)
    sending = near[middle:] + far_in
    keeping = near[:middle] + near_in
    for step in range(bits):
        masks = (1 << orders[0][step], 1 << orders[1][step])
        scale, back = scales[step]
        arrived = swap_image((sending * scale).astype(f16), masks)
        total = keeping + arrived.astype(f32) * back
        middle = total.shape[0] // 2
        sending, keeping = total[middle:], total[:middle]
    total = total[0] if bits else keeping[0]
    share = total[0]
    arrivals = []
    for mask in range(1, zones):
        arrivals.append(swap_space((total[mask] * line_scale).astype(f16), 2 * mask))
    for arrived in arrivals:
        share = share + arrived.astype(f32) * line_back
    share = (share * line_scale).astype(f16)
    collected = [share]
    for mask in range(1, zones):
        collected.append(swap_space(share, 2 * mask))
    pieces = [jnp.stack(collected)]
    for step in reversed(range(bits)):
        masks = (1 << orders[0][step], 1 << orders[1][step])
        arrived = []
        for piece in pieces:
            arrived.append(swap_image(piece, masks))
        pieces = pieces + arrived
    crossed = []
    for piece in pieces:
        crossed.append(swap_space(piece, 1))
    half_blocks = blocks // 2
    spots = [core * half_blocks + (mine ^ rest) for rest in range(half_blocks)]
    cross_spots = [(1 - core) * half_blocks + (other ^ rest) for rest in range(half_blocks)]
    zone_spots = [zone_index ^ mask for mask in range(zones)]

    def place(cells, at, before):
        table = jnp.stack(at + zone_spots).astype(jnp.int32)
        count = len(cells)
        return pl.pallas_call(
            functools.partial(place_body, (zones, height, width), count),
            out_shape=jax.ShapeDtypeStruct((9, channels, channels), f32),
            in_specs=[smem] + [vmem] * count + [anywhere] * len(before),
            out_specs=anywhere,
            scratch_shapes=[
                pltpu.VMEM((count, height, zones * width), f32),
                pltpu.VMEM((count, 9, height, channels), f32),
                pltpu.SemaphoreType.DMA((count,)),
            ],
            input_output_aliases={1 + count: 0} if before else {},
            compiler_params=pltpu.CompilerParams(vmem_limit_bytes=12 << 20),
            cost_estimate=pl.CostEstimate(
                flops=0,
                bytes_accessed=8 * count * zones * height * width,
                transcendentals=0,
            ),
        )(table, *[piece.astype(f32) * line_back for piece in cells], *before)

    weight_grad = place(
        pieces[:-1] + crossed[:-1], spots[:-1] + cross_spots[:-1], ()
    )
    weight_grad = place(pieces[-1:] + crossed[-1:], spots[-1:] + cross_spots[-1:], (weight_grad,))
    weight_grad = weight_grad.reshape(3, 3, channels, channels)

    half_count = channels // 2
    frequency = jnp.exp(-math.log(10000.0) * jnp.arange(half_count, dtype=f32) / half_count)
    angles = steps[:, :half_count] * frequency[None, :]
    embedding = jnp.concatenate([jnp.cos(angles), jnp.sin(angles)], axis=1).astype(bf16)
    time_bias = jnp.dot(embedding[:1], time_weight, preferred_element_type=f32)
    extra = time_bias + conv_bias.reshape(1, channels)
    ends = jnp.stack([slab_index > 0, slab_index < slab_count - 1]).astype(jnp.int32)
    time_grad = call(
        functools.partial(time_body, image_count),
        jax.ShapeDtypeStruct((channels, channels), f32),
        (embedding.astype(f32), totals),
        limit=4 << 20,
    )
    block_out = call(
        conv_body,
        jax.ShapeDtypeStruct((row_count, channels, col_count), bf16),
        (ends, act, lat, above, below, stats, gain, bias, conv_weight, extra),
        specs=(smem,) + (vmem,) * 9,
        scratch=(taps, flat),
        flops=flops,
        moved=8 * lat.size,
        limit=20 << 20,
    )
    latent_grad = call(
        functools.partial(latent_body, total_count),
        jax.ShapeDtypeStruct((row_count, channels, col_count), bf16),
        (grad, lat, cot, stats, totals),
        flops=lat.size * 20,
        moved=10 * lat.size,
        limit=12 << 20,
    )

    block_out = block_out[None].transpose(0, 1, 3, 2)
    latent_grad = latent_grad[None].transpose(0, 1, 3, 2)
    return (block_out, latent_grad, weight_grad, time_grad)


def solution(mesh):
    return jax.shard_map(
        slab_program,
        mesh=mesh,
        in_specs=(
            P("dp", "space", None, None),
            P("dp"),
            P(),
            P(),
            P(),
            P(),
            P(),
            P("dp", "space", None, None),
        ),
        out_specs=(P("dp", "space", None, None), P("dp", "space", None, None), P(), P()),
        check_vma=False,
    )
```

```python
import functools
import math

import jax
import jax.numpy as jnp
from jax import lax
from jax.experimental import pallas as pl
from jax.experimental.pallas import tpu as pltpu
from jax.sharding import PartitionSpec as P


GROUPS = 32
epsilon = 1e-05
f32 = jnp.float32
bf16 = jnp.bfloat16
f16 = jnp.float16
HIGHEST = lax.Precision.HIGHEST
LANES = 128
NOTE = 32


def contract(a, b, dims, precision=None):
    return lax.dot_general(a, b, (dims, ((), ())), preferred_element_type=f32, precision=precision)


def call(
    body, outs, args, specs=None, out_specs=None, scratch=(), flops=0, moved=0, limit=40 << 20
):
    vmem = pl.BlockSpec(memory_space=pltpu.VMEM)
    many = isinstance(outs, (list, tuple))
    return pl.pallas_call(
        body,
        out_shape=tuple(outs) if many else outs,
        in_specs=list(specs) if specs else [vmem] * len(args),
        out_specs=out_specs or (tuple([vmem] * len(outs)) if many else vmem),
        scratch_shapes=list(scratch),
        compiler_params=pltpu.CompilerParams(vmem_limit_bytes=limit),
        cost_estimate=pl.CostEstimate(flops=flops, bytes_accessed=moved, transcendentals=0),
    )(*args)


def member_matrix(channels):
    per_group = channels // GROUPS
    row = lax.broadcasted_iota(jnp.int32, (channels, channels), 0).astype(f32)
    col = lax.broadcasted_iota(jnp.int32, (channels, channels), 1).astype(f32)
    same = jnp.floor((row + 0.5) / per_group) == jnp.floor((col + 0.5) / per_group)
    return jnp.where(same, 1.0, 0.0).astype(f32)


def lane_form(cells):
    ones = jnp.ones((8, cells.shape[1]), f32)
    return contract(ones, cells, ((1,), (1,)), HIGHEST)


def rows_of(*rows):
    height = lax.broadcasted_iota(jnp.int32, rows[0].shape, 0)
    packed = jnp.zeros(rows[0].shape, f32)
    for number, row in enumerate(rows):
        packed = jnp.where(height == number, row, packed)
    return packed


def fold_lanes(cells):
    total = cells[:, :LANES]
    for start in range(LANES, cells.shape[1], LANES):
        total = total + cells[:, start : start + LANES]
    return total


def stats_body(count, step_ref, latent_ref, cot_ref, out_ref):
    row_count, channels, cols = latent_ref.shape
    member = member_matrix(channels)
    ones = jnp.ones((cols, LANES), bf16)
    tall = jnp.ones((8, cols), bf16)
    sums = jnp.zeros((channels, LANES), f32)
    grads = jnp.zeros((8, channels), f32)
    top = jnp.zeros((channels, LANES), f32)
    for row in range(row_count):
        sums = sums + contract(latent_ref[row], ones, ((1,), (0,)))
        grads = grads + contract(tall, cot_ref[row], ((1,), (1,)))
        size = jnp.abs(cot_ref[row].astype(f32))
        for start in range(0, cols, LANES):
            top = jnp.maximum(top, size[:, start : start + LANES])
    mean = contract(member, sums, ((1,), (0,)), HIGHEST) / count
    squares = jnp.zeros((channels, LANES), f32)
    for row in range(row_count):
        centered = latent_ref[row].astype(f32) - mean[:, :1]
        squares = squares + fold_lanes(centered * centered)
    grouped = contract(member, squares, ((1,), (0,)), HIGHEST)
    step = jnp.full((8, channels), step_ref[0].astype(f32))
    largest = jnp.broadcast_to(jnp.max(top), (8, channels))
    out_ref[...] = rows_of(
        lane_form(mean) * (1.0 / LANES), lane_form(grouped), grads, largest, step
    )


def tree_sum(parts):
    while len(parts) > 1:
        parts = [parts[i] + parts[i + 1] for i in range(0, len(parts), 2)]
    return parts[0]


def merge_body(count, total, parts, *refs):
    refs, outs = refs[:parts], refs[parts:]
    parts = [ref[...] for ref in refs]
    mean = tree_sum([part[0:1] for part in parts]) / len(parts)
    squares = tree_sum([part[1:2] + count * (part[0:1] - mean) ** 2 for part in parts])
    if total:
        squares = lax.rsqrt(squares / total + epsilon)
    grads = tree_sum([part[2:3] for part in parts])
    largest = functools.reduce(jnp.maximum, [part[3:4] for part in parts])
    step = parts[0][4:5]
    shape = parts[0].shape
    rows = (mean, squares, grads, largest, step)
    outs[0][...] = rows_of(*[jnp.broadcast_to(row, shape) for row in rows])
    if len(outs) > 1:
        table_ref = outs[1]
        channels = shape[1]
        table_ref[...] = jnp.zeros(table_ref.shape, f32)
        table_ref[0:1, :channels] = grads
        table_ref[0:1, channels : channels + NOTE] = step[:, :NOTE]
        table_ref[0:1, channels + NOTE : channels + 2 * NOTE] = largest[:, :NOTE]


def column_values(stats_ref, gain_ref, bias_ref):
    channels = gain_ref.shape[0]
    shape = (8, channels)
    table = rows_of(
        jnp.broadcast_to(stats_ref[0:1], shape),
        jnp.broadcast_to(stats_ref[1:2], shape),
        jnp.broadcast_to(gain_ref[...], shape),
        jnp.broadcast_to(bias_ref[...], shape),
    ).T
    return [table[:, i : i + 1] for i in range(4)]


def normalized(cells, values):
    mean, inverse, gain, bias = values
    normed = (cells.astype(f32) - mean) * inverse
    shifted = normed * gain + bias
    return normed, shifted, jax.nn.sigmoid(shifted)


def activate(cells, values):
    _, shifted, sigmoid = normalized(cells, values)
    return (shifted * sigmoid).astype(bf16)


def shifted_cols(cells):
    cols = cells.shape[1]
    lane = lax.broadcasted_iota(jnp.int32, cells.shape, 1)
    zero = jnp.zeros_like(cells)
    after = jnp.where(lane == cols - 1, zero, pltpu.roll(cells, cols - 1, 1))
    before = jnp.where(lane == 0, zero, pltpu.roll(cells, 1, 1))
    return after, before


def put_taps(buffer_ref, place, cells, flip):
    channels, cols = cells.shape
    wide = cells.astype(f32)
    after, before = shifted_cols(wide)
    order = (after, cells, before) if flip else (before, cells, after)
    for tap, piece in enumerate(order):
        buffer_ref[tap * channels : (tap + 1) * channels, place * cols : (place + 1) * cols] = (
            piece.astype(bf16)
        )


def taps_body(cot_ref, above_ref, below_ref, taps_ref):
    row_count = cot_ref.shape[0]
    put_taps(taps_ref, 0, above_ref[0], True)
    for row in range(row_count):
        put_taps(taps_ref, row + 1, cot_ref[row], True)
    put_taps(taps_ref, row_count + 1, below_ref[0], True)


def weight_body(
    shape, where_ref, latent_ref, taps_ref, stats_ref, gain_ref, bias_ref,
    act_out, near_ref, far_ref, act_ref, sem,
):
    blocks, zones, height, width = shape
    row_count, channels, cols = latent_ref.shape
    core, mine, other, zone_index = [where_ref[i] for i in range(4)]
    values = column_values(stats_ref, gain_ref, bias_ref)
    for row in range(row_count):
        act_ref[:, row * cols : (row + 1) * cols] = activate(latent_ref[row], values)
    kept = pltpu.make_async_copy(act_ref, act_out, sem)
    kept.start()
    tap_width = zones * width // 3

    def store(ref, place, found, block, tap_row):
        first = block * height
        size = max(min(height, channels - first), 0)
        for zone in range(zones):
            low = max(zone * width, tap_row * tap_width)
            high = min((zone + 1) * width, (tap_row + 1) * tap_width)
            if low >= high:
                continue
            at = zone_index ^ zone
            left, right = low - zone * width, high - zone * width
            source = low - tap_row * tap_width
            used = max(min(right - left, 3 * channels - source), 0)
            if size and used:
                ref[place, at, :size, left : left + used] = found[
                    first : first + size, source : source + used
                ]
            if used < right - left:
                ref[place, at, :, left + used : right] = jnp.zeros(
                    (height, right - left - used), f32
                )
            if size < height and used:
                ref[place, at, size:, left : left + used] = jnp.zeros((height - size, used), f32)

    for tap_row in range(3):
        start = (2 - tap_row) * cols
        found = contract(
            act_ref[...], taps_ref[:, start : start + row_count * cols], ((1,), (1,))
        )
        for half in range(2):

            @pl.when(core == half)
            def _():
                for rest in range(blocks // 2):
                    store(near_ref, mine ^ rest, found, half * blocks // 2 + rest, tap_row)

            @pl.when(core != half)
            def _():
                for rest in range(blocks // 2):
                    store(far_ref, other ^ rest, found, half * blocks // 2 + rest, tap_row)

    kept.wait()


def conv_body(
    ends_ref, act_ref, latent_ref, above_ref, below_ref, stats_ref, gain_ref, bias_ref,
    weight_ref, extra_ref, out_ref, taps_ref, flat_ref,
):
    row_count, channels, cols = latent_ref.shape
    values = column_values(stats_ref, gain_ref, bias_ref)
    for place, ref, end in ((0, above_ref, 0), (row_count + 1, below_ref, 1)):
        keep = ends_ref[end].astype(f32)
        put_taps(taps_ref, place, (activate(ref[1], values).astype(f32) * keep).astype(bf16), False)
    for row in range(row_count):
        put_taps(taps_ref, row + 1, act_ref[:, row * cols : (row + 1) * cols], False)
    for tap_row in range(3):
        flat_ref[tap_row] = weight_ref[tap_row].reshape(3 * channels, channels).T
    extra = jnp.broadcast_to(extra_ref[...], (8, channels)).T[:, :1]
    for row in range(row_count):
        total = latent_ref[row].astype(f32) + extra
        for tap_row in range(3):
            start = (row + tap_row) * cols
            total = total + contract(
                flat_ref[tap_row], taps_ref[:, start : start + cols], ((1,), (0,))
            )
        out_ref[row] = total.astype(bf16)


def backward_body(
    latent_ref, taps_ref, stats_ref, gain_ref, bias_ref, weight_ref, grad_out, sums_ref, flat_ref,
    grad_ref, sem,
):
    row_count, channels, cols = latent_ref.shape
    values = column_values(stats_ref, gain_ref, bias_ref)
    for tap_row in range(3):
        flat_ref[tap_row] = jnp.concatenate([weight_ref[tap_row, j] for j in range(3)], axis=1)
    kept = []
    first = jnp.zeros((channels, LANES), f32)
    second = jnp.zeros((channels, LANES), f32)
    for row in range(row_count):
        total = jnp.zeros((channels, cols), f32)
        for tap_row in range(3):
            start = (row + 2 - tap_row) * cols
            total = total + contract(
                flat_ref[tap_row], taps_ref[:, start : start + cols], ((1,), (0,))
            )
        normed, shifted, sigmoid = normalized(latent_ref[row], values)
        grad = total * sigmoid * (1.0 + shifted * (1.0 - sigmoid)) * values[2]
        grad_ref[row] = grad
        kept.append(pltpu.make_async_copy(grad_ref.at[row], grad_out.at[row], sem.at[row]))
        kept[row].start()
        first = first + fold_lanes(grad)
        second = second + fold_lanes(grad * normed)
    member = member_matrix(channels)
    first = contract(member, first, ((1,), (0,)), HIGHEST)
    second = contract(member, second, ((1,), (0,)), HIGHEST)
    sums_ref[...] = rows_of(lane_form(first), lane_form(second))
    for copy in kept:
        copy.wait()


def latent_body(total, grad_ref, latent_ref, cot_ref, stats_ref, sums_ref, out_ref):
    row_count, channels, _ = latent_ref.shape
    sums = sums_ref[0:2] / total
    shape = (8, channels)
    table = rows_of(
        *[
            jnp.broadcast_to(row, shape)
            for row in (stats_ref[0:1], stats_ref[1:2], sums[0:1], sums[1:2])
        ]
    ).T
    mean, inverse, first, second = [table[:, i : i + 1] for i in range(4)]
    for row in range(row_count):
        normed = (latent_ref[row].astype(f32) - mean) * inverse
        change = inverse * (grad_ref[row] - first - normed * second)
        out_ref[row] = (cot_ref[row].astype(f32) + change).astype(bf16)


def place_body(shape, count, places_ref, *refs):
    zones, height, width = shape
    cells = refs[:count]
    out_ref, flat_ref, rows_ref, sem = refs[-4:]
    channels = out_ref.shape[1]
    tap_width = zones * width // 3
    whole, part = channels // height, channels % height

    def copies(index, act):
        block = places_ref[index]

        def copy(size):
            return pltpu.make_async_copy(
                rows_ref.at[index, :, pl.ds(0, size)],
                out_ref.at[:, pl.ds(pl.multiple_of(block * height, 8), size)],
                sem.at[index],
            )

        @pl.when(block < whole)
        def _():
            act(copy(height))

        if part:

            @pl.when(block == whole)
            def _():
                act(copy(part))

    for index in range(count):
        for zone in range(zones):
            left = pl.multiple_of(places_ref[count + zone] * width, LANES)
            flat_ref[index, :, pl.ds(left, width)] = cells[index][zone]
        for tap in range(9):
            left = (tap // 3) * tap_width + (tap % 3) * channels
            rows_ref[index, tap] = flat_ref[index, :, left : left + channels]
        copies(index, lambda copy: copy.start())
    for index in range(count):
        copies(index, lambda copy: copy.wait())


def power_of_two(top, factor, spread, gain_ref, bias_ref, shape):
    gain = jnp.max(jnp.abs(gain_ref[...][None, :]), axis=1, keepdims=True)
    bias = jnp.max(jnp.abs(bias_ref[...][None, :]), axis=1, keepdims=True)
    reach = spread * gain + bias
    bound = jnp.maximum(top * reach * factor, 1e-30)
    power = jnp.clip(jnp.floor(jnp.log2(30000.0 / bound)), -100.0, 100.0)
    scale = jnp.broadcast_to(jnp.exp2(power), shape)
    return rows_of(scale, 1.0 / scale)


def largest_note(table, channels):
    return jnp.max(
        jnp.max(table[:, channels + NOTE : channels + 2 * NOTE], axis=1, keepdims=True),
        axis=0,
        keepdims=True,
    )


def spread_body(
    known, masks, factor, spread, where_ref, gain_ref, bias_ref, mine_ref, other_ref,
    table_ref, scale_ref, steps_ref,
):
    channels = gain_ref.shape[0]
    table_ref[...] = mine_ref[...]
    for core in range(2):

        @pl.when(where_ref[0] == core)
        def _():
            for row in known[core]:
                at = row ^ masks[core]
                table_ref[at : at + 1] = other_ref[row : row + 1]

    table = table_ref[...]
    scale_ref[...] = power_of_two(
        largest_note(table, channels), factor, spread, gain_ref, bias_ref, scale_ref.shape
    )
    steps_ref[...] = jnp.broadcast_to(table[:, channels : channels + 1], steps_ref.shape)


def gather_body(images, sums_ref, partner_ref, table_ref, out_ref):
    channels = sums_ref.shape[1]
    table = table_ref[...]
    rows = [sums_ref[0:1] + partner_ref[0:1], sums_ref[1:2] + partner_ref[1:2]]
    rows += [largest_note(table, channels)]
    rows += [table[i : i + 1, :channels] for i in range(images)]
    out_ref[...] = rows_of(*[jnp.broadcast_to(row, out_ref.shape) for row in rows])


def total_body(factor, spread, gain_ref, bias_ref, *refs):
    parts, (total_ref, scale_ref) = refs[:-2], refs[-2:]
    top = functools.reduce(jnp.maximum, [ref[2:3, 0:1] for ref in parts])
    scale_ref[...] = power_of_two(top, factor, spread, gain_ref, bias_ref, scale_ref.shape)
    total_ref[...] = tree_sum([ref[...] for ref in parts])


def time_body(count, embed_ref, total_ref, out_ref):
    columns = embed_ref[...].T
    terms = [columns[:, i : i + 1] * total_ref[3 + i : 4 + i] for i in range(count)]
    out_ref[...] = tree_sum(terms)


def swap_space(cells, mask):
    count = lax.axis_size("space")
    return lax.ppermute(cells, "space", [(i, i ^ mask) for i in range(count)])


def swap_image(cells, masks):
    images = lax.axis_size("dp")
    count = lax.axis_size("space")
    pairs = [
        (i * count + j, (i ^ masks[j % 2]) * count + j) for i in range(images) for j in range(count)
    ]
    return lax.ppermute(cells, ("dp", "space"), pairs)


def slab_program(
    latent, timesteps, norm_gain, norm_bias, conv_weight, conv_bias, time_weight, cotangent
):
    images, row_count, col_count, channels = latent.shape
    assert images == 1
    per_group = channels // GROUPS
    image_count = lax.axis_size("dp")
    slab_count = lax.axis_size("space")
    zones = slab_count // 2
    bits = image_count.bit_length() - 1
    blocks = 2 * image_count
    height = -(-channels // (8 * blocks)) * 8
    tap_width = -(-3 * channels // LANES) * LANES
    width = 3 * tap_width // zones
    local_count = row_count * col_count * per_group
    total_count = local_count * slab_count
    positions = row_count * col_count

    image_index = lax.axis_index("dp")
    slab_index = lax.axis_index("space")
    core = slab_index % 2
    zone_index = slab_index // 2

    lat = latent.transpose(0, 1, 3, 2)[0]
    cot = cotangent.transpose(0, 1, 3, 2)[0]
    gain, bias = norm_gain, norm_bias
    smem = pl.BlockSpec(memory_space=pltpu.SMEM)
    vmem = pl.BlockSpec(memory_space=pltpu.VMEM)
    anywhere = pl.BlockSpec(memory_space=pl.ANY)
    small = jax.ShapeDtypeStruct((8, channels), f32)

    down = [(i, i + 1) for i in range(slab_count - 1)]
    up = [(i + 1, i) for i in range(slab_count - 1)]

    flops = 2 * positions * channels * channels * 9
    taps = pltpu.VMEM((3 * channels, (row_count + 2) * col_count), bf16)
    flat = pltpu.VMEM((3, channels, 3 * channels), bf16)

    above = lax.ppermute(jnp.stack([cot[row_count - 1], lat[row_count - 1]]), "space", down)
    below = lax.ppermute(jnp.stack([cot[0], lat[0]]), "space", up)
    own = call(
        functools.partial(stats_body, local_count),
        small,
        (timesteps, lat, cot),
        specs=(smem, vmem, vmem),
        moved=2 * lat.size * 2,
        flops=positions * channels * 60,
        limit=12 << 20,
    )
    partner = swap_space(own, 1)
    table_shape = jax.ShapeDtypeStruct((-(-image_count // 8) * 8, channels + 2 * NOTE), f32)
    pair, table = call(
        functools.partial(merge_body, local_count, None, 2),
        (small, table_shape),
        (own, partner),
        limit=4 << 20,
    )
    parts = [pair]
    for mask in range(1, zones):
        parts.append(swap_space(pair, 2 * mask))
    stats = call(
        functools.partial(merge_body, 2 * local_count, total_count, zones),
        (small,),
        tuple(parts),
        limit=4 << 20,
    )[0]

    orders = [list(range(bits)), list(range(bits))[::-1]]

    def rest_index(which):
        index = 0
        for step in range(bits):
            shift = jnp.where(which == 0, orders[0][step], orders[1][step])
            index = index * 2 + ((image_index >> shift) & 1)
        return index

    mine, other = rest_index(core), rest_index(1 - core)
    where = jnp.stack([core, mine, other, zone_index]).astype(jnp.int32)
    share_shape = jax.ShapeDtypeStruct((blocks // 2, zones, height, width), f32)
    taps_shape = jax.ShapeDtypeStruct((3 * channels, (row_count + 2) * col_count), bf16)
    hbm = pl.BlockSpec(memory_space=pltpu.HBM)
    grad_taps = call(
        taps_body, taps_shape, (cot, above, below), moved=12 * lat.size, limit=12 << 20
    )
    act_shape = jax.ShapeDtypeStruct((channels, positions), bf16)
    act, near, far = call(
        functools.partial(weight_body, (blocks, zones, height, width)),
        (act_shape, share_shape, share_shape),
        (where, lat, grad_taps, stats, gain, bias),
        specs=(smem,) + (vmem,) * 5,
        out_specs=(hbm, vmem, vmem),
        scratch=(pltpu.VMEM(act_shape.shape, bf16), pltpu.SemaphoreType.DMA(())),
        flops=flops,
        moved=8 * lat.size,
        limit=20 << 20,
    )
    factor, spread = float(positions * slab_count * image_count), math.sqrt(per_group)
    scales_shape = jax.ShapeDtypeStruct((8, LANES), f32)
    steps_shape = jax.ShapeDtypeStruct((table_shape.shape[0], channels), f32)
    known = ([0], [0])
    scales = []
    for step in range(bits):
        masks = (1 << orders[0][step], 1 << orders[1][step])
        arrived = swap_image(table, masks)
        table, found, steps = call(
            functools.partial(spread_body, known, masks, factor, spread),
            (table_shape, scales_shape, steps_shape),
            (where, gain, bias, table, arrived),
            specs=(smem,) + (vmem,) * 4,
            limit=4 << 20,
        )
        scales.append((found[0, 0], found[1, 0]))
        known = tuple(rows + [row ^ mask for row in rows] for rows, mask in zip(known, masks))

    grad, sums = call(
        backward_body,
        (jax.ShapeDtypeStruct((row_count, channels, col_count), f32), small),
        (lat, grad_taps, stats, gain, bias, conv_weight),
        out_specs=(hbm, vmem),
        scratch=(
            flat,
            pltpu.VMEM((row_count, channels, col_count), f32),
            pltpu.SemaphoreType.DMA((row_count,)),
        ),
        flops=flops,
        moved=8 * lat.size,
        limit=20 << 20,
    )
    sums_partner = swap_space(sums, 1)
    message = jax.ShapeDtypeStruct((-(-(3 + image_count) // 8) * 8, channels), f32)
    gathered = [
        call(
            functools.partial(gather_body, image_count),
            message,
            (sums, sums_partner, table),
            limit=4 << 20,
        )
    ]
    for mask in range(1, zones):
        gathered.append(swap_space(gathered[0], 2 * mask))
    totals, line_scales = call(
        functools.partial(total_body, factor, spread),
        (message, scales_shape),
        (gain, bias, *gathered),
        limit=4 << 20,
    )
    line_scale, line_back = line_scales[0, 0], line_scales[1, 0]

    middle = blocks // 4
    far_in = swap_space(far[middle:], 1)
    near_in = swap_space(far[:middle], 1)
    sending = near[middle:] + far_in
    keeping = near[:middle] + near_in
    for step in range(bits):
        masks = (1 << orders[0][step], 1 << orders[1][step])
        scale, back = scales[step]
        arrived = swap_image((sending * scale).astype(f16), masks)
        middle = keeping.shape[0] // 2

        def joined(first, last):
            return keeping[first:last] + arrived[first:last].astype(f32) * back

        if middle:
            sending, keeping = joined(middle, 2 * middle), joined(0, middle)
    sent = []
    for mask in range(1, zones):
        block = keeping[0, mask] + arrived[0, mask].astype(f32) * back
        sent.append(swap_space((block * line_scale).astype(f16), 2 * mask))
    share = keeping[0, 0] + arrived[0, 0].astype(f32) * back
    for arrived in sent:
        share = share + arrived.astype(f32) * line_back
    share = (share * line_scale).astype(f16)
    collected = [share]
    for mask in range(1, zones):
        collected.append(swap_space(share, 2 * mask))
    pieces = [jnp.stack(collected)]
    for step in reversed(range(bits)):
        masks = (1 << orders[0][step], 1 << orders[1][step])
        arrived = []
        for piece in pieces:
            arrived.append(swap_image(piece, masks))
        pieces = pieces + arrived
    crossed = []
    for piece in pieces:
        crossed.append(swap_space(piece, 1))
    half_blocks = blocks // 2
    spots = [core * half_blocks + (mine ^ rest) for rest in range(half_blocks)]
    cross_spots = [(1 - core) * half_blocks + (other ^ rest) for rest in range(half_blocks)]
    zone_spots = [zone_index ^ mask for mask in range(zones)]

    def place(cells, at, before):
        table = jnp.stack(at + zone_spots).astype(jnp.int32)
        count = len(cells)
        return pl.pallas_call(
            functools.partial(place_body, (zones, height, width), count),
            out_shape=jax.ShapeDtypeStruct((9, channels, channels), f32),
            in_specs=[smem] + [vmem] * count + [anywhere] * len(before),
            out_specs=anywhere,
            scratch_shapes=[
                pltpu.VMEM((count, height, zones * width), f32),
                pltpu.VMEM((count, 9, height, channels), f32),
                pltpu.SemaphoreType.DMA((count,)),
            ],
            input_output_aliases={1 + count: 0} if before else {},
            compiler_params=pltpu.CompilerParams(vmem_limit_bytes=12 << 20),
            cost_estimate=pl.CostEstimate(
                flops=0,
                bytes_accessed=8 * count * zones * height * width,
                transcendentals=0,
            ),
        )(table, *[piece.astype(f32) * line_back for piece in cells], *before)

    weight_grad = place(
        pieces[:-1] + crossed[:-1], spots[:-1] + cross_spots[:-1], ()
    )
    weight_grad = place(pieces[-1:] + crossed[-1:], spots[-1:] + cross_spots[-1:], (weight_grad,))
    weight_grad = weight_grad.reshape(3, 3, channels, channels)

    half_count = channels // 2
    frequency = jnp.exp(-math.log(10000.0) * jnp.arange(half_count, dtype=f32) / half_count)
    angles = steps[:, :half_count] * frequency[None, :]
    embedding = jnp.concatenate([jnp.cos(angles), jnp.sin(angles)], axis=1).astype(bf16)
    time_bias = jnp.dot(embedding[:1], time_weight, preferred_element_type=f32)
    extra = time_bias + conv_bias.reshape(1, channels)
    ends = jnp.stack([slab_index > 0, slab_index < slab_count - 1]).astype(jnp.int32)
    time_grad = call(
        functools.partial(time_body, image_count),
        jax.ShapeDtypeStruct((channels, channels), f32),
        (embedding.astype(f32), totals),
        limit=4 << 20,
    )
    block_out = call(
        conv_body,
        jax.ShapeDtypeStruct((row_count, channels, col_count), bf16),
        (ends, act, lat, above, below, stats, gain, bias, conv_weight, extra),
        specs=(smem,) + (vmem,) * 9,
        scratch=(taps, flat),
        flops=flops,
        moved=8 * lat.size,
        limit=20 << 20,
    )
    latent_grad = call(
        functools.partial(latent_body, total_count),
        jax.ShapeDtypeStruct((row_count, channels, col_count), bf16),
        (grad, lat, cot, stats, totals),
        flops=lat.size * 20,
        moved=10 * lat.size,
        limit=12 << 20,
    )

    block_out = block_out[None].transpose(0, 1, 3, 2)
    latent_grad = latent_grad[None].transpose(0, 1, 3, 2)
    return (block_out, latent_grad, weight_grad, time_grad)


def solution(mesh):
    return jax.shard_map(
        slab_program,
        mesh=mesh,
        in_specs=(
            P("dp", "space", None, None),
            P("dp"),
            P(),
            P(),
            P(),
            P(),
            P(),
            P("dp", "space", None, None),
        ),
        out_specs=(P("dp", "space", None, None), P("dp", "space", None, None), P(), P()),
        check_vma=False,
    )
```

```python
import functools
import math

import jax
import jax.numpy as jnp
from jax import lax
from jax.experimental import pallas as pl
from jax.experimental.pallas import tpu as pltpu
from jax.sharding import PartitionSpec as P


GROUPS = 32
epsilon = 1e-05
f32 = jnp.float32
bf16 = jnp.bfloat16
f16 = jnp.float16
HIGHEST = lax.Precision.HIGHEST
LANES = 128
NOTE = 32


def contract(a, b, dims, precision=None):
    return lax.dot_general(a, b, (dims, ((), ())), preferred_element_type=f32, precision=precision)


def call(body, outs, args, specs=None, scratch=(), flops=0, moved=0, limit=40 << 20):
    vmem = pl.BlockSpec(memory_space=pltpu.VMEM)
    many = isinstance(outs, (list, tuple))
    return pl.pallas_call(
        body,
        out_shape=tuple(outs) if many else outs,
        in_specs=list(specs) if specs else [vmem] * len(args),
        out_specs=tuple([vmem] * len(outs)) if many else vmem,
        scratch_shapes=list(scratch),
        compiler_params=pltpu.CompilerParams(vmem_limit_bytes=limit),
        cost_estimate=pl.CostEstimate(flops=flops, bytes_accessed=moved, transcendentals=0),
    )(*args)


def member_matrix(channels):
    per_group = channels // GROUPS
    row = lax.broadcasted_iota(jnp.int32, (channels, channels), 0).astype(f32)
    col = lax.broadcasted_iota(jnp.int32, (channels, channels), 1).astype(f32)
    same = jnp.floor((row + 0.5) / per_group) == jnp.floor((col + 0.5) / per_group)
    return jnp.where(same, 1.0, 0.0).astype(f32)


def lane_form(cells):
    ones = jnp.ones((8, cells.shape[1]), f32)
    return contract(ones, cells, ((1,), (1,)), HIGHEST)


def rows_of(*rows):
    height = lax.broadcasted_iota(jnp.int32, rows[0].shape, 0)
    packed = jnp.zeros(rows[0].shape, f32)
    for number, row in enumerate(rows):
        packed = jnp.where(height == number, row, packed)
    return packed


def fold_lanes(cells):
    total = cells[:, :LANES]
    for start in range(LANES, cells.shape[1], LANES):
        total = total + cells[:, start : start + LANES]
    return total


def stats_body(
    count, step_ref, latent_hbm, cot_hbm, out_ref, down_ref, up_ref, latent_ref, cot_ref, sem
):
    row_count, channels, cols = latent_ref.shape
    loads = []
    for number, (source, target) in enumerate(((latent_hbm, latent_ref), (cot_hbm, cot_ref))):
        for row in range(row_count):
            load = pltpu.make_async_copy(source.at[row], target.at[row], sem.at[number, row])
            load.start()
            loads.append(load)
    member = member_matrix(channels)
    ones = jnp.ones((cols, LANES), bf16)
    tall = jnp.ones((8, cols), bf16)
    sums = jnp.zeros((channels, LANES), f32)
    for row in range(row_count):
        loads[row].wait()
        sums = sums + contract(latent_ref[row], ones, ((1,), (0,)))
    mean = contract(member, sums, ((1,), (0,)), HIGHEST) / count
    grads = jnp.zeros((8, channels), f32)
    top = jnp.zeros((channels, LANES), f32)
    for row in range(row_count):
        loads[row_count + row].wait()
        grads = grads + contract(tall, cot_ref[row], ((1,), (1,)))
        size = jnp.abs(cot_ref[row].astype(f32))
        for start in range(0, cols, LANES):
            top = jnp.maximum(top, size[:, start : start + LANES])
    for ref, row in ((down_ref, row_count - 1), (up_ref, 0)):
        ref[0] = cot_ref[row]
        ref[1] = latent_ref[row]
    squares = jnp.zeros((channels, LANES), f32)
    for row in range(row_count):
        centered = latent_ref[row].astype(f32) - mean[:, :1]
        squares = squares + fold_lanes(centered * centered)
    grouped = contract(member, squares, ((1,), (0,)), HIGHEST)
    step = jnp.full((8, channels), step_ref[0].astype(f32))
    largest = jnp.broadcast_to(jnp.max(top), (8, channels))
    out_ref[...] = rows_of(
        lane_form(mean) * (1.0 / LANES), lane_form(grouped), grads, largest, step
    )


def tree_sum(parts):
    while len(parts) > 1:
        parts = [parts[i] + parts[i + 1] for i in range(0, len(parts), 2)]
    return parts[0]


def merge_body(count, total, parts, *refs):
    refs, outs = refs[:parts], refs[parts:]
    parts = [ref[...] for ref in refs]
    mean = tree_sum([part[0:1] for part in parts]) / len(parts)
    squares = tree_sum([part[1:2] + count * (part[0:1] - mean) ** 2 for part in parts])
    if total:
        squares = lax.rsqrt(squares / total + epsilon)
    grads = tree_sum([part[2:3] for part in parts])
    largest = functools.reduce(jnp.maximum, [part[3:4] for part in parts])
    step = parts[0][4:5]
    shape = parts[0].shape
    rows = (mean, squares, grads, largest, step)
    outs[0][...] = rows_of(*[jnp.broadcast_to(row, shape) for row in rows])
    if len(outs) > 1:
        table_ref = outs[1]
        channels = shape[1]
        table_ref[...] = jnp.zeros(table_ref.shape, f32)
        table_ref[0:1, :channels] = grads
        table_ref[0:1, channels : channels + NOTE] = step[:, :NOTE]
        table_ref[0:1, channels + NOTE : channels + 2 * NOTE] = largest[:, :NOTE]


def column_values(stats_ref, gain_ref, bias_ref):
    channels = gain_ref.shape[0]
    shape = (8, channels)
    table = rows_of(
        jnp.broadcast_to(stats_ref[0:1], shape),
        jnp.broadcast_to(stats_ref[1:2], shape),
        jnp.broadcast_to(gain_ref[...], shape),
        jnp.broadcast_to(bias_ref[...], shape),
    ).T
    return [table[:, i : i + 1] for i in range(4)]


def normalized(cells, values):
    mean, inverse, gain, bias = values
    normed = (cells.astype(f32) - mean) * inverse
    shifted = normed * gain + bias
    return normed, shifted, jax.nn.sigmoid(shifted)


def activate(cells, values):
    _, shifted, sigmoid = normalized(cells, values)
    return (shifted * sigmoid).astype(bf16)


def shifted_cols(cells):
    cols = cells.shape[1]
    lane = lax.broadcasted_iota(jnp.int32, cells.shape, 1)
    zero = jnp.zeros_like(cells)
    after = jnp.where(lane == cols - 1, zero, pltpu.roll(cells, cols - 1, 1))
    before = jnp.where(lane == 0, zero, pltpu.roll(cells, 1, 1))
    return after, before


def put_taps(buffer_ref, place, cells, flip):
    channels, cols = cells.shape
    wide = cells.astype(f32)
    after, before = shifted_cols(wide)
    order = (after, cells, before) if flip else (before, cells, after)
    for tap, piece in enumerate(order):
        buffer_ref[tap * channels : (tap + 1) * channels, place * cols : (place + 1) * cols] = (
            piece.astype(bf16)
        )


def taps_body(cot_ref, taps_ref):
    for row in range(cot_ref.shape[0]):
        put_taps(taps_ref, row, cot_ref[row], True)


def middle_body(latent_ref, taps_ref, stats_ref, gain_ref, bias_ref, act_ref, found_ref):
    row_count, _, cols = latent_ref.shape
    values = column_values(stats_ref, gain_ref, bias_ref)
    for row in range(row_count):
        act_ref[:, row * cols : (row + 1) * cols] = activate(latent_ref[row], values)
    found_ref[...] = contract(act_ref[...], taps_ref[...], ((1,), (1,)))


def weight_body(
    shape, cols, where_ref, act_ref, taps_ref, above_ref, below_ref, middle_ref,
    near_ref, low_ref, high_ref, edge_ref,
):
    blocks, zones, height, width = shape
    channels, positions = act_ref.shape
    core, mine, other, zone_index = [where_ref[i] for i in range(4)]
    quarter = blocks // 4
    put_taps(edge_ref, 0, above_ref[0], True)
    put_taps(edge_ref, 1, below_ref[0], True)
    tap_width = zones * width // 3

    def store(ref, place, found, block, tap_row):
        first = block * height
        size = max(min(height, channels - first), 0)
        for zone in range(zones):
            low = max(zone * width, tap_row * tap_width)
            high = min((zone + 1) * width, (tap_row + 1) * tap_width)
            if low >= high:
                continue
            at = zone_index ^ zone
            left, right = low - zone * width, high - zone * width
            source = low - tap_row * tap_width
            used = max(min(right - left, 3 * channels - source), 0)
            if size and used:
                ref[place, at, :size, left : left + used] = found[
                    first : first + size, source : source + used
                ]
            if used < right - left:
                ref[place, at, :, left + used : right] = jnp.zeros(
                    (height, right - left - used), f32
                )
            if size < height and used:
                ref[place, at, size:, left : left + used] = jnp.zeros((height - size, used), f32)

    for tap_row in (1, 0, 2):
        if tap_row == 1:
            found = middle_ref
        else:
            inner = slice(0, positions - cols) if tap_row == 0 else slice(cols, positions)
            shifted = slice(cols, positions) if tap_row == 0 else slice(0, positions - cols)
            outer = slice(positions - cols, positions) if tap_row == 0 else slice(0, cols)
            edge = slice(cols, 2 * cols) if tap_row == 0 else slice(0, cols)
            found = contract(act_ref[:, inner], taps_ref[:, shifted], ((1,), (1,)))
            found = found + contract(act_ref[:, outer], edge_ref[:, edge], ((1,), (1,)))
        for half in range(2):

            @pl.when(core == half)
            def _():
                for rest in range(blocks // 2):
                    store(near_ref, mine ^ rest, found, half * blocks // 2 + rest, tap_row)

            for top in range(2):

                @pl.when((core != half) & (other // quarter == top))
                def _():
                    for rest in range(blocks // 2):
                        ref = high_ref if rest // quarter != top else low_ref
                        at = (other ^ rest) % quarter
                        store(ref, at, found, half * blocks // 2 + rest, tap_row)


def conv_body(
    ends_ref, latent_ref, above_ref, below_ref, stats_ref, gain_ref, bias_ref, weight_ref,
    extra_ref, out_ref, taps_ref, flat_ref,
):
    row_count, channels, cols = latent_ref.shape
    values = column_values(stats_ref, gain_ref, bias_ref)
    for place, ref, end in ((0, above_ref, 0), (row_count + 1, below_ref, 1)):
        keep = ends_ref[end].astype(f32)
        put_taps(taps_ref, place, (activate(ref[1], values).astype(f32) * keep).astype(bf16), False)
    for row in range(row_count):
        put_taps(taps_ref, row + 1, activate(latent_ref[row], values), False)
    for tap_row in range(3):
        flat_ref[tap_row] = weight_ref[tap_row].reshape(3 * channels, channels).T
    extra = jnp.broadcast_to(extra_ref[...], (8, channels)).T[:, :1]
    for row in range(row_count):
        total = latent_ref[row].astype(f32) + extra
        for tap_row in range(3):
            start = (row + tap_row) * cols
            total = total + contract(
                flat_ref[tap_row], taps_ref[:, start : start + cols], ((1,), (0,))
            )
        out_ref[row] = total.astype(bf16)


def backward_body(
    latent_ref, taps_ref, edge_ref, stats_ref, gain_ref, bias_ref, weight_ref,
    grad_ref, sums_ref, flat_ref,
):
    row_count, channels, cols = latent_ref.shape
    values = column_values(stats_ref, gain_ref, bias_ref)
    for tap_row in range(3):
        flat_ref[tap_row] = jnp.concatenate([weight_ref[tap_row, j] for j in range(3)], axis=1)
    first = jnp.zeros((channels, LANES), f32)
    second = jnp.zeros((channels, LANES), f32)
    for row in range(row_count):
        total = jnp.zeros((channels, cols), f32)
        for tap_row in range(3):
            source = row + 1 - tap_row
            if 0 <= source < row_count:
                piece = taps_ref[:, source * cols : (source + 1) * cols]
            else:
                start = cols if source > 0 else 0
                piece = edge_ref[:, start : start + cols]
            total = total + contract(flat_ref[tap_row], piece, ((1,), (0,)))
        normed, shifted, sigmoid = normalized(latent_ref[row], values)
        grad = total * sigmoid * (1.0 + shifted * (1.0 - sigmoid)) * values[2]
        grad_ref[row] = grad
        first = first + fold_lanes(grad)
        second = second + fold_lanes(grad * normed)
    member = member_matrix(channels)
    first = contract(member, first, ((1,), (0,)), HIGHEST)
    second = contract(member, second, ((1,), (0,)), HIGHEST)
    sums_ref[...] = rows_of(lane_form(first), lane_form(second))


def latent_body(total, grad_ref, latent_ref, cot_ref, stats_ref, sums_ref, out_ref):
    row_count, channels, _ = latent_ref.shape
    sums = sums_ref[0:2] / total
    shape = (8, channels)
    table = rows_of(
        *[
            jnp.broadcast_to(row, shape)
            for row in (stats_ref[0:1], stats_ref[1:2], sums[0:1], sums[1:2])
        ]
    ).T
    mean, inverse, first, second = [table[:, i : i + 1] for i in range(4)]
    for row in range(row_count):
        normed = (latent_ref[row].astype(f32) - mean) * inverse
        change = inverse * (grad_ref[row] - first - normed * second)
        out_ref[row] = (cot_ref[row].astype(f32) + change).astype(bf16)


def place_body(shape, count, places_ref, *refs):
    zones, height, width = shape
    cells = refs[:count]
    out_ref, flat_ref, rows_ref, sem = refs[-4:]
    channels = out_ref.shape[1]
    tap_width = zones * width // 3
    whole, part = channels // height, channels % height

    def copies(index, act):
        block = places_ref[index]

        def copy(size):
            return pltpu.make_async_copy(
                rows_ref.at[index, :, pl.ds(0, size)],
                out_ref.at[:, pl.ds(pl.multiple_of(block * height, 8), size)],
                sem.at[index],
            )

        @pl.when(block < whole)
        def _():
            act(copy(height))

        if part:

            @pl.when(block == whole)
            def _():
                act(copy(part))

    for index in range(count):
        for zone in range(zones):
            left = pl.multiple_of(places_ref[count + zone] * width, LANES)
            flat_ref[index, :, pl.ds(left, width)] = cells[index][zone]
        for tap in range(9):
            left = (tap // 3) * tap_width + (tap % 3) * channels
            rows_ref[index, tap] = flat_ref[index, :, left : left + channels]
        copies(index, lambda copy: copy.start())
    for index in range(count):
        copies(index, lambda copy: copy.wait())


def power_of_two(top, factor, spread, gain_ref, bias_ref, shape):
    gain = jnp.max(jnp.abs(gain_ref[...][None, :]), axis=1, keepdims=True)
    bias = jnp.max(jnp.abs(bias_ref[...][None, :]), axis=1, keepdims=True)
    reach = spread * gain + bias
    bound = jnp.maximum(top * reach * factor, 1e-30)
    power = jnp.clip(jnp.floor(jnp.log2(30000.0 / bound)), -100.0, 100.0)
    scale = jnp.broadcast_to(jnp.exp2(power), shape)
    return rows_of(scale, 1.0 / scale)


def largest_note(table, channels):
    return jnp.max(
        jnp.max(table[:, channels + NOTE : channels + 2 * NOTE], axis=1, keepdims=True),
        axis=0,
        keepdims=True,
    )


def spread_body(
    known, masks, factor, spread, where_ref, gain_ref, bias_ref, mine_ref, other_ref,
    table_ref, scale_ref, steps_ref,
):
    channels = gain_ref.shape[0]
    table_ref[...] = mine_ref[...]
    for core in range(2):

        @pl.when(where_ref[0] == core)
        def _():
            for row in known[core]:
                at = row ^ masks[core]
                table_ref[at : at + 1] = other_ref[row : row + 1]

    table = table_ref[...]
    scale_ref[...] = power_of_two(
        largest_note(table, channels), factor, spread, gain_ref, bias_ref, scale_ref.shape
    )
    steps_ref[...] = jnp.broadcast_to(table[:, channels : channels + 1], steps_ref.shape)


def gather_body(images, sums_ref, partner_ref, table_ref, out_ref):
    channels = sums_ref.shape[1]
    table = table_ref[...]
    rows = [sums_ref[0:1] + partner_ref[0:1], sums_ref[1:2] + partner_ref[1:2]]
    rows += [largest_note(table, channels)]
    rows += [table[i : i + 1, :channels] for i in range(images)]
    out_ref[...] = rows_of(*[jnp.broadcast_to(row, out_ref.shape) for row in rows])


def total_body(factor, spread, gain_ref, bias_ref, *refs):
    parts, (total_ref, scale_ref) = refs[:-2], refs[-2:]
    top = functools.reduce(jnp.maximum, [ref[2:3, 0:1] for ref in parts])
    scale_ref[...] = power_of_two(top, factor, spread, gain_ref, bias_ref, scale_ref.shape)
    total_ref[...] = tree_sum([ref[...] for ref in parts])


def time_body(count, embed_ref, total_ref, out_ref):
    columns = embed_ref[...].T
    terms = [columns[:, i : i + 1] * total_ref[3 + i : 4 + i] for i in range(count)]
    out_ref[...] = tree_sum(terms)


def swap_space(cells, mask):
    count = lax.axis_size("space")
    return lax.ppermute(cells, "space", [(i, i ^ mask) for i in range(count)])


def swap_image(cells, masks):
    images = lax.axis_size("dp")
    count = lax.axis_size("space")
    pairs = [
        (i * count + j, (i ^ masks[j % 2]) * count + j) for i in range(images) for j in range(count)
    ]
    return lax.ppermute(cells, ("dp", "space"), pairs)


def slab_program(
    latent, timesteps, norm_gain, norm_bias, conv_weight, conv_bias, time_weight, cotangent
):
    images, row_count, col_count, channels = latent.shape
    assert images == 1
    per_group = channels // GROUPS
    image_count = lax.axis_size("dp")
    slab_count = lax.axis_size("space")
    zones = slab_count // 2
    bits = image_count.bit_length() - 1
    blocks = 2 * image_count
    height = -(-channels // (8 * blocks)) * 8
    tap_width = -(-3 * channels // LANES) * LANES
    width = 3 * tap_width // zones
    local_count = row_count * col_count * per_group
    total_count = local_count * slab_count
    positions = row_count * col_count

    image_index = lax.axis_index("dp")
    slab_index = lax.axis_index("space")
    core = slab_index % 2
    zone_index = slab_index // 2

    lat = latent.transpose(0, 1, 3, 2)[0]
    cot = cotangent.transpose(0, 1, 3, 2)[0]
    gain, bias = norm_gain, norm_bias
    smem = pl.BlockSpec(memory_space=pltpu.SMEM)
    vmem = pl.BlockSpec(memory_space=pltpu.VMEM)
    small = jax.ShapeDtypeStruct((8, channels), f32)

    down = [(i, i + 1) for i in range(slab_count - 1)]
    up = [(i + 1, i) for i in range(slab_count - 1)]

    flops = 2 * positions * channels * channels * 9
    taps = pltpu.VMEM((3 * channels, (row_count + 2) * col_count), bf16)
    flat = pltpu.VMEM((3, channels, 3 * channels), bf16)

    edge = jax.ShapeDtypeStruct((2, channels, col_count), bf16)
    anywhere = pl.BlockSpec(memory_space=pl.ANY)
    slab = pltpu.VMEM((row_count, channels, col_count), bf16)
    own, edge_down, edge_up = call(
        functools.partial(stats_body, local_count),
        (small, edge, edge),
        (timesteps, lat, cot),
        specs=(smem, anywhere, anywhere),
        scratch=(slab, slab, pltpu.SemaphoreType.DMA((2, row_count))),
        moved=2 * lat.size * 2,
        flops=positions * channels * 60,
        limit=None,
    )
    partner = swap_space(own, 1)
    above = lax.ppermute(edge_down, "space", down)
    below = lax.ppermute(edge_up, "space", up)
    table_shape = jax.ShapeDtypeStruct((-(-image_count // 8) * 8, channels + 2 * NOTE), f32)
    pair, table = call(
        functools.partial(merge_body, local_count, None, 2),
        (small, table_shape),
        (own, partner),
        limit=4 << 20,
    )
    parts = [pair]
    for mask in range(1, zones):
        parts.append(swap_space(pair, 2 * mask))
    stats = call(
        functools.partial(merge_body, 2 * local_count, total_count, zones),
        (small,),
        tuple(parts),
        limit=4 << 20,
    )[0]

    orders = [list(range(bits)), list(range(bits))[::-1]]

    def rest_index(which):
        index = 0
        for step in range(bits):
            shift = jnp.where(which == 0, orders[0][step], orders[1][step])
            index = index * 2 + ((image_index >> shift) & 1)
        return index

    mine, other = rest_index(core), rest_index(1 - core)
    where = jnp.stack([core, mine, other, zone_index]).astype(jnp.int32)
    part_shape = jax.ShapeDtypeStruct((blocks // 4, zones, height, width), f32)
    share_shape = jax.ShapeDtypeStruct((blocks // 2, zones, height, width), f32)
    taps_shape = jax.ShapeDtypeStruct((3 * channels, positions), bf16)
    grad_taps = call(taps_body, taps_shape, (cot,), moved=10 * lat.size, limit=6 << 20)
    act, middle_rows = call(
        middle_body,
        (
            jax.ShapeDtypeStruct((channels, positions), bf16),
            jax.ShapeDtypeStruct((channels, 3 * channels), f32),
        ),
        (lat, grad_taps, stats, gain, bias),
        flops=flops // 3,
        moved=8 * lat.size,
        limit=8 << 20,
    )
    near, far_low, far_high, edge_taps = call(
        functools.partial(weight_body, (blocks, zones, height, width), col_count),
        (
            share_shape,
            part_shape,
            part_shape,
            jax.ShapeDtypeStruct((3 * channels, 2 * col_count), bf16),
        ),
        (where, act, grad_taps, above, below, middle_rows),
        specs=(smem,) + (vmem,) * 5,
        flops=flops,
        moved=8 * lat.size,
        limit=12 << 20,
    )
    factor, spread = float(positions * slab_count * image_count), math.sqrt(per_group)
    scales_shape = jax.ShapeDtypeStruct((8, LANES), f32)
    steps_shape = jax.ShapeDtypeStruct((table_shape.shape[0], channels), f32)
    known = ([0], [0])
    scales = []
    for step in range(bits):
        masks = (1 << orders[0][step], 1 << orders[1][step])
        arrived = swap_image(table, masks)
        table, found, steps = call(
            functools.partial(spread_body, known, masks, factor, spread),
            (table_shape, scales_shape, steps_shape),
            (where, gain, bias, table, arrived),
            specs=(smem,) + (vmem,) * 4,
            limit=4 << 20,
        )
        scales.append((found[0, 0], found[1, 0]))
        known = tuple(rows + [row ^ mask for row in rows] for rows, mask in zip(known, masks))

    grad, sums = call(
        backward_body,
        (jax.ShapeDtypeStruct((row_count, channels, col_count), f32), small),
        (lat, grad_taps, edge_taps, stats, gain, bias, conv_weight),
        scratch=(flat,),
        flops=flops,
        moved=8 * lat.size,
        limit=8 << 20,
    )
    sums_partner = swap_space(sums, 1)
    message = jax.ShapeDtypeStruct((-(-(3 + image_count) // 8) * 8, channels), f32)
    gathered = [
        call(
            functools.partial(gather_body, image_count),
            message,
            (sums, sums_partner, table),
            limit=4 << 20,
        )
    ]
    for mask in range(1, zones):
        gathered.append(swap_space(gathered[0], 2 * mask))
    totals, line_scales = call(
        functools.partial(total_body, factor, spread),
        (message, scales_shape),
        (gain, bias, *gathered),
        limit=4 << 20,
    )
    line_scale, line_back = line_scales[0, 0], line_scales[1, 0]

    middle = blocks // 4
    far_in = swap_space(far_high, 1)
    near_in = swap_space(far_low, 1)
    sending = near[middle:] + far_in
    keeping = near[:middle] + near_in
    for step in range(bits):
        masks = (1 << orders[0][step], 1 << orders[1][step])
        scale, back = scales[step]
        arrived = swap_image((sending * scale).astype(f16), masks)
        total = keeping + arrived.astype(f32) * back
        middle = total.shape[0] // 2
        sending, keeping = total[middle:], total[:middle]
    total = total[0] if bits else keeping[0]
    share = total[0]
    arrivals = []
    for mask in range(1, zones):
        arrivals.append(swap_space((total[mask] * line_scale).astype(f16), 2 * mask))
    for arrived in arrivals:
        share = share + arrived.astype(f32) * line_back
    share = (share * line_scale).astype(f16)
    collected = [share]
    for mask in range(1, zones):
        collected.append(swap_space(share, 2 * mask))
    pieces = [jnp.stack(collected)]
    for step in reversed(range(bits)):
        masks = (1 << orders[0][step], 1 << orders[1][step])
        arrived = []
        for piece in pieces:
            arrived.append(swap_image(piece, masks))
        pieces = pieces + arrived
    crossed = []
    for piece in pieces:
        crossed.append(swap_space(piece, 1))
    half_blocks = blocks // 2
    spots = [core * half_blocks + (mine ^ rest) for rest in range(half_blocks)]
    cross_spots = [(1 - core) * half_blocks + (other ^ rest) for rest in range(half_blocks)]
    zone_spots = [zone_index ^ mask for mask in range(zones)]

    def place(cells, at, before):
        table = jnp.stack(at + zone_spots).astype(jnp.int32)
        count = len(cells)
        return pl.pallas_call(
            functools.partial(place_body, (zones, height, width), count),
            out_shape=jax.ShapeDtypeStruct((9, channels, channels), f32),
            in_specs=[smem] + [vmem] * count + [anywhere] * len(before),
            out_specs=anywhere,
            scratch_shapes=[
                pltpu.VMEM((count, height, zones * width), f32),
                pltpu.VMEM((count, 9, height, channels), f32),
                pltpu.SemaphoreType.DMA((count,)),
            ],
            input_output_aliases={1 + count: 0} if before else {},
            compiler_params=pltpu.CompilerParams(vmem_limit_bytes=12 << 20),
            cost_estimate=pl.CostEstimate(
                flops=0,
                bytes_accessed=8 * count * zones * height * width,
                transcendentals=0,
            ),
        )(table, *[piece.astype(f32) * line_back for piece in cells], *before)

    weight_grad = place(
        pieces[:-1] + crossed[:-1], spots[:-1] + cross_spots[:-1], ()
    )
    weight_grad = place(pieces[-1:] + crossed[-1:], spots[-1:] + cross_spots[-1:], (weight_grad,))
    weight_grad = weight_grad.reshape(3, 3, channels, channels)

    half_count = channels // 2
    frequency = jnp.exp(-math.log(10000.0) * jnp.arange(half_count, dtype=f32) / half_count)
    angles = steps[:, :half_count] * frequency[None, :]
    embedding = jnp.concatenate([jnp.cos(angles), jnp.sin(angles)], axis=1).astype(bf16)
    time_bias = jnp.dot(embedding[:1], time_weight, preferred_element_type=f32)
    extra = time_bias + conv_bias.reshape(1, channels)
    ends = jnp.stack([slab_index > 0, slab_index < slab_count - 1]).astype(jnp.int32)
    time_grad = call(
        functools.partial(time_body, image_count),
        jax.ShapeDtypeStruct((channels, channels), f32),
        (embedding.astype(f32), totals),
        limit=4 << 20,
    )
    block_out = call(
        conv_body,
        jax.ShapeDtypeStruct((row_count, channels, col_count), bf16),
        (ends, lat, above, below, stats, gain, bias, conv_weight, extra),
        specs=(smem,) + (vmem,) * 8,
        scratch=(taps, flat),
        flops=flops,
        moved=8 * lat.size,
        limit=14 << 20,
    )
    latent_grad = call(
        functools.partial(latent_body, total_count),
        jax.ShapeDtypeStruct((row_count, channels, col_count), bf16),
        (grad, lat, cot, stats, totals),
        flops=lat.size * 20,
        moved=10 * lat.size,
        limit=12 << 20,
    )

    block_out = block_out[None].transpose(0, 1, 3, 2)
    latent_grad = latent_grad[None].transpose(0, 1, 3, 2)
    return (block_out, latent_grad, weight_grad, time_grad)


def solution(mesh):
    return jax.shard_map(
        slab_program,
        mesh=mesh,
        in_specs=(
            P("dp", "space", None, None),
            P("dp"),
            P(),
            P(),
            P(),
            P(),
            P(),
            P("dp", "space", None, None),
        ),
        out_specs=(P("dp", "space", None, None), P("dp", "space", None, None), P(), P()),
        check_vma=False,
    )
```

```python
import functools
import math

import jax
import jax.numpy as jnp
from jax import lax
from jax.experimental import pallas as pl
from jax.experimental.pallas import tpu as pltpu
from jax.sharding import PartitionSpec as P


GROUPS = 32
epsilon = 1e-05
f32 = jnp.float32
bf16 = jnp.bfloat16
f16 = jnp.float16
HIGHEST = lax.Precision.HIGHEST
LANES = 128
NOTE = 32


def contract(a, b, dims, precision=None):
    return lax.dot_general(a, b, (dims, ((), ())), preferred_element_type=f32, precision=precision)


def call(body, outs, args, specs=None, scratch=(), flops=0, moved=0, limit=40 << 20):
    vmem = pl.BlockSpec(memory_space=pltpu.VMEM)
    many = isinstance(outs, (list, tuple))
    return pl.pallas_call(
        body,
        out_shape=tuple(outs) if many else outs,
        in_specs=list(specs) if specs else [vmem] * len(args),
        out_specs=tuple([vmem] * len(outs)) if many else vmem,
        scratch_shapes=list(scratch),
        compiler_params=pltpu.CompilerParams(vmem_limit_bytes=limit),
        cost_estimate=pl.CostEstimate(flops=flops, bytes_accessed=moved, transcendentals=0),
    )(*args)


def member_matrix(channels):
    per_group = channels // GROUPS
    row = lax.broadcasted_iota(jnp.int32, (channels, channels), 0).astype(f32)
    col = lax.broadcasted_iota(jnp.int32, (channels, channels), 1).astype(f32)
    same = jnp.floor((row + 0.5) / per_group) == jnp.floor((col + 0.5) / per_group)
    return jnp.where(same, 1.0, 0.0).astype(f32)


def lane_form(cells):
    ones = jnp.ones((8, cells.shape[1]), f32)
    return contract(ones, cells, ((1,), (1,)), HIGHEST)


def rows_of(*rows):
    height = lax.broadcasted_iota(jnp.int32, rows[0].shape, 0)
    packed = jnp.zeros(rows[0].shape, f32)
    for number, row in enumerate(rows):
        packed = jnp.where(height == number, row, packed)
    return packed


def fold_lanes(cells):
    total = cells[:, :LANES]
    for start in range(LANES, cells.shape[1], LANES):
        total = total + cells[:, start : start + LANES]
    return total


def stats_body(count, step_ref, latent_hbm, cot_hbm, out_ref, latent_ref, cot_ref, sem):
    row_count, channels, cols = latent_ref.shape
    loads = []
    for number, (source, target) in enumerate(((latent_hbm, latent_ref), (cot_hbm, cot_ref))):
        for row in range(row_count):
            load = pltpu.make_async_copy(source.at[row], target.at[row], sem.at[number, row])
            load.start()
            loads.append(load)
    member = member_matrix(channels)
    ones = jnp.ones((cols, LANES), bf16)
    sums = jnp.zeros((channels, LANES), f32)
    for row in range(row_count):
        loads[row].wait()
        sums = sums + contract(latent_ref[row], ones, ((1,), (0,)))
    mean = contract(member, sums, ((1,), (0,)), HIGHEST) / count
    squares = jnp.zeros((channels, LANES), f32)
    for row in range(row_count):
        centered = latent_ref[row].astype(f32) - mean[:, :1]
        squares = squares + fold_lanes(centered * centered)
    grouped = contract(member, squares, ((1,), (0,)), HIGHEST)
    top = jnp.zeros((channels, LANES), bf16)
    for row in range(row_count):
        loads[row_count + row].wait()
        size = jnp.abs(cot_ref[row])
        for start in range(0, cols, LANES):
            top = jnp.maximum(top, size[:, start : start + LANES])
    step = jnp.full((8, channels), step_ref[0].astype(f32))
    largest = jnp.broadcast_to(jnp.max(top.astype(f32)), (8, channels))
    out_ref[...] = rows_of(lane_form(mean) * (1.0 / LANES), lane_form(grouped), largest, step)


def tree_sum(parts):
    while len(parts) > 1:
        parts = [parts[i] + parts[i + 1] for i in range(0, len(parts), 2)]
    return parts[0]


def merge_body(count, total, *refs):
    parts, out_ref = [ref[...] for ref in refs[:-1]], refs[-1]
    mean = tree_sum([part[0:1] for part in parts]) / len(parts)
    squares = tree_sum([part[1:2] + count * (part[0:1] - mean) ** 2 for part in parts])
    if total:
        squares = lax.rsqrt(squares / total + epsilon)
    largest = functools.reduce(jnp.maximum, [part[2:3] for part in parts])
    rows = (mean, squares, largest, parts[0][3:4])
    out_ref[...] = rows_of(*[jnp.broadcast_to(row, out_ref.shape) for row in rows])


def column_values(stats_ref, gain_ref, bias_ref):
    channels = gain_ref.shape[0]
    shape = (8, channels)
    table = rows_of(
        jnp.broadcast_to(stats_ref[0:1], shape),
        jnp.broadcast_to(stats_ref[1:2], shape),
        jnp.broadcast_to(gain_ref[...], shape),
        jnp.broadcast_to(bias_ref[...], shape),
    ).T
    return [table[:, i : i + 1] for i in range(4)]


def normalized(cells, values):
    mean, inverse, gain, bias = values
    normed = (cells.astype(f32) - mean) * inverse
    shifted = normed * gain + bias
    return normed, shifted, jax.nn.sigmoid(shifted)


def activate(cells, values):
    _, shifted, sigmoid = normalized(cells, values)
    return (shifted * sigmoid).astype(bf16)


def shifted_cols(cells):
    cols = cells.shape[1]
    lane = lax.broadcasted_iota(jnp.int32, cells.shape, 1)
    zero = jnp.zeros_like(cells)
    after = jnp.where(lane == cols - 1, zero, pltpu.roll(cells, cols - 1, 1))
    before = jnp.where(lane == 0, zero, pltpu.roll(cells, 1, 1))
    return after, before


def put_taps(buffer_ref, place, cells, flip):
    channels, cols = cells.shape
    wide = cells.astype(f32)
    after, before = shifted_cols(wide)
    order = (after, cells, before) if flip else (before, cells, after)
    for tap, piece in enumerate(order):
        buffer_ref[tap * channels : (tap + 1) * channels, place * cols : (place + 1) * cols] = (
            piece.astype(bf16)
        )


def taps_body(cot_ref, taps_ref, sums_ref):
    row_count, channels, cols = cot_ref.shape
    tall = jnp.ones((8, cols), bf16)
    sums = jnp.zeros((8, channels), f32)
    for row in range(row_count):
        put_taps(taps_ref, row, cot_ref[row], True)
        sums = sums + contract(tall, cot_ref[row], ((1,), (1,)))
    sums_ref[...] = sums


def middle_body(
    latent_ref, taps_ref, stats_ref, gain_ref, bias_ref, sums_ref, act_ref, found_ref, table_ref
):
    row_count, channels, cols = latent_ref.shape
    table_ref[...] = jnp.zeros(table_ref.shape, f32)
    table_ref[0:1, :channels] = sums_ref[0:1]
    table_ref[0:1, channels : channels + NOTE] = stats_ref[3:4, :NOTE]
    table_ref[0:1, channels + NOTE : channels + 2 * NOTE] = stats_ref[2:3, :NOTE]
    values = column_values(stats_ref, gain_ref, bias_ref)
    for row in range(row_count):
        act_ref[:, row * cols : (row + 1) * cols] = activate(latent_ref[row], values)
    found_ref[...] = contract(act_ref[...], taps_ref[...], ((1,), (1,)))


def weight_body(
    shape, cols, where_ref, act_ref, taps_ref, above_ref, below_ref, middle_ref,
    near_ref, low_ref, high_ref, edge_ref,
):
    blocks, zones, height, width = shape
    channels, positions = act_ref.shape
    core, mine, other, zone_index = [where_ref[i] for i in range(4)]
    quarter = blocks // 4
    put_taps(edge_ref, 0, above_ref[...], True)
    put_taps(edge_ref, 1, below_ref[...], True)
    tap_width = zones * width // 3

    def store(ref, place, found, block, tap_row):
        first = block * height
        size = max(min(height, channels - first), 0)
        for zone in range(zones):
            low = max(zone * width, tap_row * tap_width)
            high = min((zone + 1) * width, (tap_row + 1) * tap_width)
            if low >= high:
                continue
            at = zone_index ^ zone
            left, right = low - zone * width, high - zone * width
            source = low - tap_row * tap_width
            used = max(min(right - left, 3 * channels - source), 0)
            if size and used:
                ref[place, at, :size, left : left + used] = found[
                    first : first + size, source : source + used
                ]
            if used < right - left:
                ref[place, at, :, left + used : right] = jnp.zeros(
                    (height, right - left - used), f32
                )
            if size < height and used:
                ref[place, at, size:, left : left + used] = jnp.zeros((height - size, used), f32)

    for tap_row in (1, 0, 2):
        if tap_row == 1:
            found = middle_ref
        else:
            inner = slice(0, positions - cols) if tap_row == 0 else slice(cols, positions)
            shifted = slice(cols, positions) if tap_row == 0 else slice(0, positions - cols)
            outer = slice(positions - cols, positions) if tap_row == 0 else slice(0, cols)
            edge = slice(cols, 2 * cols) if tap_row == 0 else slice(0, cols)
            found = contract(act_ref[:, inner], taps_ref[:, shifted], ((1,), (1,)))
            found = found + contract(act_ref[:, outer], edge_ref[:, edge], ((1,), (1,)))
        for half in range(2):

            @pl.when(core == half)
            def _():
                for rest in range(blocks // 2):
                    store(near_ref, mine ^ rest, found, half * blocks // 2 + rest, tap_row)

            for top in range(2):

                @pl.when((core != half) & (other // quarter == top))
                def _():
                    for rest in range(blocks // 2):
                        ref = high_ref if rest // quarter != top else low_ref
                        at = (other ^ rest) % quarter
                        store(ref, at, found, half * blocks // 2 + rest, tap_row)


def conv_body(
    ends_ref, latent_ref, above_ref, below_ref, stats_ref, gain_ref, bias_ref, weight_ref,
    extra_ref, out_ref, taps_ref, flat_ref,
):
    row_count, channels, cols = latent_ref.shape
    values = column_values(stats_ref, gain_ref, bias_ref)
    for place, ref, end in ((0, above_ref, 0), (row_count + 1, below_ref, 1)):
        keep = ends_ref[end].astype(f32)
        put_taps(taps_ref, place, (activate(ref[...], values).astype(f32) * keep).astype(bf16), False)
    for row in range(row_count):
        put_taps(taps_ref, row + 1, activate(latent_ref[row], values), False)
    for tap_row in range(3):
        flat_ref[tap_row] = weight_ref[tap_row].reshape(3 * channels, channels).T
    extra = jnp.broadcast_to(extra_ref[...], (8, channels)).T[:, :1]
    for row in range(row_count):
        total = latent_ref[row].astype(f32) + extra
        for tap_row in range(3):
            start = (row + tap_row) * cols
            total = total + contract(
                flat_ref[tap_row], taps_ref[:, start : start + cols], ((1,), (0,))
            )
        out_ref[row] = total.astype(bf16)


def backward_body(
    latent_ref, taps_ref, edge_ref, stats_ref, gain_ref, bias_ref, weight_ref,
    grad_ref, sums_ref, flat_ref,
):
    row_count, channels, cols = latent_ref.shape
    values = column_values(stats_ref, gain_ref, bias_ref)
    for tap_row in range(3):
        flat_ref[tap_row] = jnp.concatenate([weight_ref[tap_row, j] for j in range(3)], axis=1)
    first = jnp.zeros((channels, LANES), f32)
    second = jnp.zeros((channels, LANES), f32)
    for row in range(row_count):
        total = jnp.zeros((channels, cols), f32)
        for tap_row in range(3):
            source = row + 1 - tap_row
            if 0 <= source < row_count:
                piece = taps_ref[:, source * cols : (source + 1) * cols]
            else:
                start = cols if source > 0 else 0
                piece = edge_ref[:, start : start + cols]
            total = total + contract(flat_ref[tap_row], piece, ((1,), (0,)))
        normed, shifted, sigmoid = normalized(latent_ref[row], values)
        grad = total * sigmoid * (1.0 + shifted * (1.0 - sigmoid)) * values[2]
        grad_ref[row] = grad
        first = first + fold_lanes(grad)
        second = second + fold_lanes(grad * normed)
    member = member_matrix(channels)
    first = contract(member, first, ((1,), (0,)), HIGHEST)
    second = contract(member, second, ((1,), (0,)), HIGHEST)
    sums_ref[...] = rows_of(lane_form(first), lane_form(second))


def latent_body(total, grad_ref, latent_ref, cot_ref, stats_ref, sums_ref, out_ref):
    row_count, channels, _ = latent_ref.shape
    sums = sums_ref[0:2] / total
    shape = (8, channels)
    table = rows_of(
        *[
            jnp.broadcast_to(row, shape)
            for row in (stats_ref[0:1], stats_ref[1:2], sums[0:1], sums[1:2])
        ]
    ).T
    mean, inverse, first, second = [table[:, i : i + 1] for i in range(4)]
    for row in range(row_count):
        normed = (latent_ref[row].astype(f32) - mean) * inverse
        change = inverse * (grad_ref[row] - first - normed * second)
        out_ref[row] = (cot_ref[row].astype(f32) + change).astype(bf16)


def place_body(shape, count, places_ref, *refs):
    zones, height, width = shape
    cells = refs[:count]
    out_ref, flat_ref, rows_ref, sem = refs[-4:]
    channels = out_ref.shape[1]
    tap_width = zones * width // 3
    whole, part = channels // height, channels % height

    def copies(index, act):
        block = places_ref[index]

        def copy(size):
            return pltpu.make_async_copy(
                rows_ref.at[index, :, pl.ds(0, size)],
                out_ref.at[:, pl.ds(pl.multiple_of(block * height, 8), size)],
                sem.at[index],
            )

        @pl.when(block < whole)
        def _():
            act(copy(height))

        if part:

            @pl.when(block == whole)
            def _():
                act(copy(part))

    for index in range(count):
        for zone in range(zones):
            left = pl.multiple_of(places_ref[count + zone] * width, LANES)
            flat_ref[index, :, pl.ds(left, width)] = cells[index][zone]
        for tap in range(9):
            left = (tap // 3) * tap_width + (tap % 3) * channels
            rows_ref[index, tap] = flat_ref[index, :, left : left + channels]
        copies(index, lambda copy: copy.start())
    for index in range(count):
        copies(index, lambda copy: copy.wait())


def power_of_two(top, factor, spread, gain_ref, bias_ref, shape):
    gain = jnp.max(jnp.abs(gain_ref[...][None, :]), axis=1, keepdims=True)
    bias = jnp.max(jnp.abs(bias_ref[...][None, :]), axis=1, keepdims=True)
    reach = spread * gain + bias
    bound = jnp.maximum(top * reach * factor, 1e-30)
    power = jnp.clip(jnp.floor(jnp.log2(30000.0 / bound)), -100.0, 100.0)
    scale = jnp.broadcast_to(jnp.exp2(power), shape)
    return rows_of(scale, 1.0 / scale)


def largest_note(table, channels):
    return jnp.max(
        jnp.max(table[:, channels + NOTE : channels + 2 * NOTE], axis=1, keepdims=True),
        axis=0,
        keepdims=True,
    )


def spread_body(
    known, masks, factor, spread, where_ref, gain_ref, bias_ref, mine_ref, other_ref,
    table_ref, scale_ref, steps_ref,
):
    channels = gain_ref.shape[0]
    table_ref[...] = mine_ref[...]
    for core in range(2):

        @pl.when(where_ref[0] == core)
        def _():
            for row in known[core]:
                at = row ^ masks[core]
                table_ref[at : at + 1] = other_ref[row : row + 1]

    table = table_ref[...]
    scale_ref[...] = power_of_two(
        largest_note(table, channels), factor, spread, gain_ref, bias_ref, scale_ref.shape
    )
    steps_ref[...] = jnp.broadcast_to(table[:, channels : channels + 1], steps_ref.shape)


def gather_body(images, sums_ref, table_ref, out_ref):
    channels = sums_ref.shape[1]
    rows = [sums_ref[0:1], sums_ref[1:2]]
    rows += [table_ref[i : i + 1, :channels] for i in range(images)]
    out_ref[...] = rows_of(*[jnp.broadcast_to(row, out_ref.shape) for row in rows])


def total_body(*refs):
    refs[-1][...] = tree_sum([ref[...] for ref in refs[:-1]])


def time_body(count, embed_ref, total_ref, out_ref):
    columns = embed_ref[...].T
    terms = [columns[:, i : i + 1] * total_ref[2 + i : 3 + i] for i in range(count)]
    out_ref[...] = tree_sum(terms)


def swap_space(cells, mask):
    count = lax.axis_size("space")
    return lax.ppermute(cells, "space", [(i, i ^ mask) for i in range(count)])


def swap_image(cells, masks):
    images = lax.axis_size("dp")
    count = lax.axis_size("space")
    pairs = [
        (i * count + j, (i ^ masks[j % 2]) * count + j) for i in range(images) for j in range(count)
    ]
    return lax.ppermute(cells, ("dp", "space"), pairs)


def slab_program(
    latent, timesteps, norm_gain, norm_bias, conv_weight, conv_bias, time_weight, cotangent
):
    images, row_count, col_count, channels = latent.shape
    assert images == 1
    per_group = channels // GROUPS
    image_count = lax.axis_size("dp")
    slab_count = lax.axis_size("space")
    zones = slab_count // 2
    bits = image_count.bit_length() - 1
    blocks = 2 * image_count
    height = -(-channels // (8 * blocks)) * 8
    tap_width = -(-3 * channels // LANES) * LANES
    width = 3 * tap_width // zones
    local_count = row_count * col_count * per_group
    total_count = local_count * slab_count
    positions = row_count * col_count

    image_index = lax.axis_index("dp")
    slab_index = lax.axis_index("space")
    core = slab_index % 2
    zone_index = slab_index // 2

    lat = latent.transpose(0, 1, 3, 2)[0]
    cot = cotangent.transpose(0, 1, 3, 2)[0]
    gain, bias = norm_gain, norm_bias
    smem = pl.BlockSpec(memory_space=pltpu.SMEM)
    vmem = pl.BlockSpec(memory_space=pltpu.VMEM)
    anywhere = pl.BlockSpec(memory_space=pl.ANY)
    small = jax.ShapeDtypeStruct((8, channels), f32)

    down = [(i, i + 1) for i in range(slab_count - 1)]
    up = [(i + 1, i) for i in range(slab_count - 1)]

    flops = 2 * positions * channels * channels * 9
    taps = pltpu.VMEM((3 * channels, (row_count + 2) * col_count), bf16)
    flat = pltpu.VMEM((3, channels, 3 * channels), bf16)

    slab = pltpu.VMEM((row_count, channels, col_count), bf16)
    own = call(
        functools.partial(stats_body, local_count),
        small,
        (timesteps, lat, cot),
        specs=(smem, anywhere, anywhere),
        scratch=(slab, slab, pltpu.SemaphoreType.DMA((2, row_count))),
        moved=2 * lat.size * 2,
        flops=positions * channels * 60,
        limit=63 << 20,
    )
    partner = swap_space(own, 1)
    pair = call(
        functools.partial(merge_body, local_count, None), small, (own, partner), limit=4 << 20
    )
    parts = [pair]
    for mask in range(1, zones):
        parts.append(swap_space(pair, 2 * mask))
    above = lax.ppermute(cot[row_count - 1], "space", down)
    below = lax.ppermute(cot[0], "space", up)
    lat_above = lax.ppermute(lat[row_count - 1], "space", down)
    lat_below = lax.ppermute(lat[0], "space", up)
    stats = call(
        functools.partial(merge_body, 2 * local_count, total_count),
        small,
        tuple(parts),
        limit=4 << 20,
    )

    orders = [list(range(bits)), list(range(bits))[::-1]]

    def rest_index(which):
        index = 0
        for step in range(bits):
            shift = jnp.where(which == 0, orders[0][step], orders[1][step])
            index = index * 2 + ((image_index >> shift) & 1)
        return index

    mine, other = rest_index(core), rest_index(1 - core)
    where = jnp.stack([core, mine, other, zone_index]).astype(jnp.int32)
    part_shape = jax.ShapeDtypeStruct((blocks // 4, zones, height, width), f32)
    share_shape = jax.ShapeDtypeStruct((blocks // 2, zones, height, width), f32)
    taps_shape = jax.ShapeDtypeStruct((3 * channels, positions), bf16)
    grad_taps, col_sums = call(
        taps_body, (taps_shape, small), (cot,), moved=10 * lat.size, limit=6 << 20
    )
    table_shape = jax.ShapeDtypeStruct((-(-image_count // 8) * 8, channels + 2 * NOTE), f32)
    act, middle_rows, table = call(
        middle_body,
        (
            jax.ShapeDtypeStruct((channels, positions), bf16),
            jax.ShapeDtypeStruct((channels, 3 * channels), f32),
            table_shape,
        ),
        (lat, grad_taps, stats, gain, bias, col_sums),
        flops=flops // 3,
        moved=8 * lat.size,
        limit=8 << 20,
    )
    near, far_low, far_high, edge_taps = call(
        functools.partial(weight_body, (blocks, zones, height, width), col_count),
        (
            share_shape,
            part_shape,
            part_shape,
            jax.ShapeDtypeStruct((3 * channels, 2 * col_count), bf16),
        ),
        (where, act, grad_taps, above, below, middle_rows),
        specs=(smem,) + (vmem,) * 5,
        flops=flops,
        moved=8 * lat.size,
        limit=12 << 20,
    )
    factor, spread = float(positions * slab_count * image_count), math.sqrt(per_group)
    scales_shape = jax.ShapeDtypeStruct((8, LANES), f32)
    steps_shape = jax.ShapeDtypeStruct((table_shape.shape[0], channels), f32)
    known = ([0], [0])
    scales = []
    for step in range(bits):
        masks = (1 << orders[0][step], 1 << orders[1][step])
        arrived = swap_image(table, masks)
        table, found, steps = call(
            functools.partial(spread_body, known, masks, factor, spread),
            (table_shape, scales_shape, steps_shape),
            (where, gain, bias, table, arrived),
            specs=(smem,) + (vmem,) * 4,
            limit=4 << 20,
        )
        scales.append((found[0, 0], found[1, 0]))
        known = tuple(rows + [row ^ mask for row in rows] for rows, mask in zip(known, masks))

    grad, sums = call(
        backward_body,
        (jax.ShapeDtypeStruct((row_count, channels, col_count), f32), small),
        (lat, grad_taps, edge_taps, stats, gain, bias, conv_weight),
        scratch=(flat,),
        flops=flops,
        moved=8 * lat.size,
        limit=8 << 20,
    )
    message = jax.ShapeDtypeStruct((-(-(2 + image_count) // 8) * 8, channels), f32)
    gathered = call(
        functools.partial(gather_body, image_count), message, (sums, table), limit=4 << 20
    )
    gathered = [gathered + swap_space(gathered, 1)]
    for mask in range(1, zones):
        gathered.append(swap_space(gathered[0], 2 * mask))
    totals = call(total_body, message, tuple(gathered), limit=4 << 20)
    line_scale, line_back = scales[-1]

    middle = blocks // 4
    far_in = swap_space(far_high, 1)
    near_in = swap_space(far_low, 1)
    sending = near[middle:] + far_in
    keeping = near[:middle] + near_in
    for step in range(bits):
        masks = (1 << orders[0][step], 1 << orders[1][step])
        scale, back = scales[step]
        arrived = swap_image((sending * scale).astype(f16), masks)
        total = keeping + arrived.astype(f32) * back
        middle = total.shape[0] // 2
        sending, keeping = total[middle:], total[:middle]
    total = total[0] if bits else keeping[0]
    share = total[0]
    arrivals = []
    for mask in range(1, zones):
        arrivals.append(swap_space((total[mask] * line_scale).astype(f16), 2 * mask))
    for arrived in arrivals:
        share = share + arrived.astype(f32) * line_back
    share = (share * line_scale).astype(f16)
    collected = [share]
    for mask in range(1, zones):
        collected.append(swap_space(share, 2 * mask))
    pieces = [jnp.stack(collected)]
    for step in reversed(range(bits)):
        masks = (1 << orders[0][step], 1 << orders[1][step])
        arrived = []
        for piece in pieces:
            arrived.append(swap_image(piece, masks))
        pieces = pieces + arrived
    crossed = []
    for piece in pieces:
        crossed.append(swap_space(piece, 1))
    half_blocks = blocks // 2
    spots = [core * half_blocks + (mine ^ rest) for rest in range(half_blocks)]
    cross_spots = [(1 - core) * half_blocks + (other ^ rest) for rest in range(half_blocks)]
    zone_spots = [zone_index ^ mask for mask in range(zones)]

    def place(cells, at, before):
        table = jnp.stack(at + zone_spots).astype(jnp.int32)
        count = len(cells)
        return pl.pallas_call(
            functools.partial(place_body, (zones, height, width), count),
            out_shape=jax.ShapeDtypeStruct((9, channels, channels), f32),
            in_specs=[smem] + [vmem] * count + [anywhere] * len(before),
            out_specs=anywhere,
            scratch_shapes=[
                pltpu.VMEM((count, height, zones * width), f32),
                pltpu.VMEM((count, 9, height, channels), f32),
                pltpu.SemaphoreType.DMA((count,)),
            ],
            input_output_aliases={1 + count: 0} if before else {},
            compiler_params=pltpu.CompilerParams(vmem_limit_bytes=12 << 20),
            cost_estimate=pl.CostEstimate(
                flops=0,
                bytes_accessed=8 * count * zones * height * width,
                transcendentals=0,
            ),
        )(table, *[piece.astype(f32) * line_back for piece in cells], *before)

    weight_grad = place(
        pieces[:-1] + crossed[:-1], spots[:-1] + cross_spots[:-1], ()
    )
    weight_grad = place(pieces[-1:] + crossed[-1:], spots[-1:] + cross_spots[-1:], (weight_grad,))
    weight_grad = weight_grad.reshape(3, 3, channels, channels)

    half_count = channels // 2
    frequency = jnp.exp(-math.log(10000.0) * jnp.arange(half_count, dtype=f32) / half_count)
    angles = steps[:, :half_count] * frequency[None, :]
    embedding = jnp.concatenate([jnp.cos(angles), jnp.sin(angles)], axis=1).astype(bf16)
    time_bias = jnp.dot(embedding[:1], time_weight, preferred_element_type=f32)
    extra = time_bias + conv_bias.reshape(1, channels)
    ends = jnp.stack([slab_index > 0, slab_index < slab_count - 1]).astype(jnp.int32)
    time_grad = call(
        functools.partial(time_body, image_count),
        jax.ShapeDtypeStruct((channels, channels), f32),
        (embedding.astype(f32), totals),
        limit=4 << 20,
    )
    block_out = call(
        conv_body,
        jax.ShapeDtypeStruct((row_count, channels, col_count), bf16),
        (ends, lat, lat_above, lat_below, stats, gain, bias, conv_weight, extra),
        specs=(smem,) + (vmem,) * 8,
        scratch=(taps, flat),
        flops=flops,
        moved=8 * lat.size,
        limit=14 << 20,
    )
    latent_grad = call(
        functools.partial(latent_body, total_count),
        jax.ShapeDtypeStruct((row_count, channels, col_count), bf16),
        (grad, lat, cot, stats, totals),
        flops=lat.size * 20,
        moved=10 * lat.size,
        limit=12 << 20,
    )

    block_out = block_out[None].transpose(0, 1, 3, 2)
    latent_grad = latent_grad[None].transpose(0, 1, 3, 2)
    return (block_out, latent_grad, weight_grad, time_grad)


def solution(mesh):
    return jax.shard_map(
        slab_program,
        mesh=mesh,
        in_specs=(
            P("dp", "space", None, None),
            P("dp"),
            P(),
            P(),
            P(),
            P(),
            P(),
            P("dp", "space", None, None),
        ),
        out_specs=(P("dp", "space", None, None), P("dp", "space", None, None), P(), P()),
        check_vma=False,
    )
```

```python
import functools
import math

import jax
import jax.numpy as jnp
from jax import lax
from jax.experimental import pallas as pl
from jax.experimental.pallas import tpu as pltpu
from jax.sharding import PartitionSpec as P


GROUPS = 32
epsilon = 1e-05
f32 = jnp.float32
bf16 = jnp.bfloat16
f16 = jnp.float16
HIGHEST = lax.Precision.HIGHEST
LANES = 128
NOTE = 32


def contract(a, b, dims, precision=None):
    return lax.dot_general(a, b, (dims, ((), ())), preferred_element_type=f32, precision=precision)


def call(body, outs, args, specs=None, scratch=(), flops=0, moved=0, limit=40 << 20):
    vmem = pl.BlockSpec(memory_space=pltpu.VMEM)
    many = isinstance(outs, (list, tuple))
    return pl.pallas_call(
        body,
        out_shape=tuple(outs) if many else outs,
        in_specs=list(specs) if specs else [vmem] * len(args),
        out_specs=tuple([vmem] * len(outs)) if many else vmem,
        scratch_shapes=list(scratch),
        compiler_params=pltpu.CompilerParams(vmem_limit_bytes=limit),
        cost_estimate=pl.CostEstimate(flops=flops, bytes_accessed=moved, transcendentals=0),
    )(*args)


def member_matrix(channels):
    per_group = channels // GROUPS
    row = lax.broadcasted_iota(jnp.int32, (channels, channels), 0).astype(f32)
    col = lax.broadcasted_iota(jnp.int32, (channels, channels), 1).astype(f32)
    same = jnp.floor((row + 0.5) / per_group) == jnp.floor((col + 0.5) / per_group)
    return jnp.where(same, 1.0, 0.0).astype(f32)


def lane_form(cells):
    ones = jnp.ones((8, cells.shape[1]), f32)
    return contract(ones, cells, ((1,), (1,)), HIGHEST)


def rows_of(*rows):
    height = lax.broadcasted_iota(jnp.int32, rows[0].shape, 0)
    packed = jnp.zeros(rows[0].shape, f32)
    for number, row in enumerate(rows):
        packed = jnp.where(height == number, row, packed)
    return packed


def fold_lanes(cells):
    total = cells[:, :LANES]
    for start in range(LANES, cells.shape[1], LANES):
        total = total + cells[:, start : start + LANES]
    return total


def stats_body(count, step_ref, latent_hbm, cot_hbm, out_ref, latent_ref, cot_ref, sem):
    row_count, channels, cols = latent_ref.shape
    loads = []
    for number, (source, target) in enumerate(((latent_hbm, latent_ref), (cot_hbm, cot_ref))):
        for row in range(row_count):
            load = pltpu.make_async_copy(source.at[row], target.at[row], sem.at[number, row])
            load.start()
            loads.append(load)
    member = member_matrix(channels)
    ones = jnp.ones((cols, LANES), bf16)
    sums = jnp.zeros((channels, LANES), f32)
    for row in range(row_count):
        loads[row].wait()
        sums = sums + contract(latent_ref[row], ones, ((1,), (0,)))
    mean = contract(member, sums, ((1,), (0,)), HIGHEST) / count
    squares = jnp.zeros((channels, LANES), f32)
    for row in range(row_count):
        centered = latent_ref[row].astype(f32) - mean[:, :1]
        squares = squares + fold_lanes(centered * centered)
    grouped = contract(member, squares, ((1,), (0,)), HIGHEST)
    top = jnp.zeros((channels, LANES), bf16)
    for row in range(row_count):
        loads[row_count + row].wait()
        size = jnp.abs(cot_ref[row])
        for start in range(0, cols, LANES):
            top = jnp.maximum(top, size[:, start : start + LANES])
    step = jnp.full((8, channels), step_ref[0].astype(f32))
    largest = jnp.broadcast_to(jnp.max(top.astype(f32)), (8, channels))
    out_ref[...] = rows_of(lane_form(mean) * (1.0 / LANES), lane_form(grouped), largest, step)


def tree_sum(parts):
    while len(parts) > 1:
        parts = [parts[i] + parts[i + 1] for i in range(0, len(parts), 2)]
    return parts[0]


def merge_body(count, total, *refs):
    parts, out_ref = [ref[...] for ref in refs[:-1]], refs[-1]
    mean = tree_sum([part[0:1] for part in parts]) / len(parts)
    squares = tree_sum([part[1:2] + count * (part[0:1] - mean) ** 2 for part in parts])
    if total:
        squares = lax.rsqrt(squares / total + epsilon)
    largest = functools.reduce(jnp.maximum, [part[2:3] for part in parts])
    rows = (mean, squares, largest, parts[0][3:4])
    out_ref[...] = rows_of(*[jnp.broadcast_to(row, out_ref.shape) for row in rows])


def column_values(stats_ref, gain_ref, bias_ref):
    channels = gain_ref.shape[0]
    shape = (8, channels)
    table = rows_of(
        jnp.broadcast_to(stats_ref[0:1], shape),
        jnp.broadcast_to(stats_ref[1:2], shape),
        jnp.broadcast_to(gain_ref[...], shape),
        jnp.broadcast_to(bias_ref[...], shape),
    ).T
    return [table[:, i : i + 1] for i in range(4)]


def normalized(cells, values):
    mean, inverse, gain, bias = values
    normed = (cells.astype(f32) - mean) * inverse
    shifted = normed * gain + bias
    return normed, shifted, jax.nn.sigmoid(shifted)


def activate(cells, values):
    _, shifted, sigmoid = normalized(cells, values)
    return (shifted * sigmoid).astype(bf16)


def shifted_cols(cells):
    cols = cells.shape[1]
    lane = lax.broadcasted_iota(jnp.int32, cells.shape, 1)
    zero = jnp.zeros_like(cells)
    after = jnp.where(lane == cols - 1, zero, pltpu.roll(cells, cols - 1, 1))
    before = jnp.where(lane == 0, zero, pltpu.roll(cells, 1, 1))
    return after, before


def put_taps(buffer_ref, place, cells, flip):
    channels, cols = cells.shape
    wide = cells.astype(f32)
    after, before = shifted_cols(wide)
    order = (after, cells, before) if flip else (before, cells, after)
    for tap, piece in enumerate(order):
        buffer_ref[tap * channels : (tap + 1) * channels, place * cols : (place + 1) * cols] = (
            piece.astype(bf16)
        )


def taps_body(cot_ref, taps_ref, sums_ref):
    row_count, channels, cols = cot_ref.shape
    tall = jnp.ones((8, cols), bf16)
    sums = jnp.zeros((8, channels), f32)
    for row in range(row_count):
        put_taps(taps_ref, row, cot_ref[row], True)
        sums = sums + contract(tall, cot_ref[row], ((1,), (1,)))
    sums_ref[...] = sums


def middle_body(
    factor, spread, latent_ref, taps_ref, stats_ref, gain_ref, bias_ref, sums_ref, act_ref, found_ref, table_ref
):
    row_count, channels, cols = latent_ref.shape
    table_ref[...] = jnp.zeros(table_ref.shape, f32)
    table_ref[0:1, :channels] = sums_ref[0:1]
    table_ref[0:1, channels : channels + NOTE] = stats_ref[3:4, :NOTE]
    gain = jnp.max(jnp.abs(gain_ref[...][None, :]), axis=1, keepdims=True)
    bias = jnp.max(jnp.abs(bias_ref[...][None, :]), axis=1, keepdims=True)
    bound = stats_ref[2:3] * ((spread * gain + bias) * factor)
    table_ref[0:1, channels + NOTE : channels + 2 * NOTE] = bound[:, :NOTE]
    values = column_values(stats_ref, gain_ref, bias_ref)
    for row in range(row_count):
        act_ref[:, row * cols : (row + 1) * cols] = activate(latent_ref[row], values)
    found_ref[...] = contract(act_ref[...], taps_ref[...], ((1,), (1,)))


def weight_body(
    shape, cols, where_ref, act_ref, taps_ref, above_ref, below_ref, middle_ref,
    near_ref, low_ref, high_ref, edge_ref,
):
    blocks, zones, height, width = shape
    channels, positions = act_ref.shape
    core, mine, other, zone_index = [where_ref[i] for i in range(4)]
    quarter = blocks // 4
    put_taps(edge_ref, 0, above_ref[...], True)
    put_taps(edge_ref, 1, below_ref[...], True)
    tap_width = zones * width // 3

    def store(ref, place, found, block, tap_row):
        first = block * height
        size = max(min(height, channels - first), 0)
        for zone in range(zones):
            low = max(zone * width, tap_row * tap_width)
            high = min((zone + 1) * width, (tap_row + 1) * tap_width)
            if low >= high:
                continue
            at = zone_index ^ zone
            left, right = low - zone * width, high - zone * width
            source = low - tap_row * tap_width
            used = max(min(right - left, 3 * channels - source), 0)
            if size and used:
                ref[place, at, :size, left : left + used] = found[
                    first : first + size, source : source + used
                ]
            if used < right - left:
                ref[place, at, :, left + used : right] = jnp.zeros(
                    (height, right - left - used), f32
                )
            if size < height and used:
                ref[place, at, size:, left : left + used] = jnp.zeros((height - size, used), f32)

    for tap_row in (1, 0, 2):
        if tap_row == 1:
            found = middle_ref
        else:
            inner = slice(0, positions - cols) if tap_row == 0 else slice(cols, positions)
            shifted = slice(cols, positions) if tap_row == 0 else slice(0, positions - cols)
            outer = slice(positions - cols, positions) if tap_row == 0 else slice(0, cols)
            edge = slice(cols, 2 * cols) if tap_row == 0 else slice(0, cols)
            found = contract(act_ref[:, inner], taps_ref[:, shifted], ((1,), (1,)))
            found = found + contract(act_ref[:, outer], edge_ref[:, edge], ((1,), (1,)))
        for half in range(2):

            @pl.when(core == half)
            def _():
                for rest in range(blocks // 2):
                    store(near_ref, mine ^ rest, found, half * blocks // 2 + rest, tap_row)

            for top in range(2):

                @pl.when((core != half) & (other // quarter == top))
                def _():
                    for rest in range(blocks // 2):
                        ref = high_ref if rest // quarter != top else low_ref
                        at = (other ^ rest) % quarter
                        store(ref, at, found, half * blocks // 2 + rest, tap_row)


def conv_body(
    where_ref, latent_ref, above_ref, below_ref, stats_ref, gain_ref, bias_ref, weight_ref,
    extra_ref, out_ref, taps_ref, flat_ref,
):
    row_count, channels, cols = latent_ref.shape
    values = column_values(stats_ref, gain_ref, bias_ref)
    for place, ref, end in ((0, above_ref, 4), (row_count + 1, below_ref, 5)):
        keep = where_ref[end].astype(f32)
        put_taps(taps_ref, place, (activate(ref[...], values).astype(f32) * keep).astype(bf16), False)
    for row in range(row_count):
        put_taps(taps_ref, row + 1, activate(latent_ref[row], values), False)
    for tap_row in range(3):
        flat_ref[tap_row] = weight_ref[tap_row].reshape(3 * channels, channels).T
    extra = jnp.broadcast_to(extra_ref[...], (8, channels)).T[:, :1]
    for row in range(row_count):
        total = latent_ref[row].astype(f32) + extra
        for tap_row in range(3):
            start = (row + tap_row) * cols
            total = total + contract(
                flat_ref[tap_row], taps_ref[:, start : start + cols], ((1,), (0,))
            )
        out_ref[row] = total.astype(bf16)


def backward_body(
    latent_ref, taps_ref, edge_ref, stats_ref, gain_ref, bias_ref, weight_ref,
    grad_ref, sums_ref, flat_ref,
):
    row_count, channels, cols = latent_ref.shape
    values = column_values(stats_ref, gain_ref, bias_ref)
    for tap_row in range(3):
        flat_ref[tap_row] = jnp.concatenate([weight_ref[tap_row, j] for j in range(3)], axis=1)
    first = jnp.zeros((channels, LANES), f32)
    second = jnp.zeros((channels, LANES), f32)
    for row in range(row_count):
        total = jnp.zeros((channels, cols), f32)
        for tap_row in range(3):
            source = row + 1 - tap_row
            if 0 <= source < row_count:
                piece = taps_ref[:, source * cols : (source + 1) * cols]
            else:
                start = cols if source > 0 else 0
                piece = edge_ref[:, start : start + cols]
            total = total + contract(flat_ref[tap_row], piece, ((1,), (0,)))
        normed, shifted, sigmoid = normalized(latent_ref[row], values)
        grad = total * sigmoid * (1.0 + shifted * (1.0 - sigmoid)) * values[2]
        grad_ref[row] = grad
        first = first + fold_lanes(grad)
        second = second + fold_lanes(grad * normed)
    member = member_matrix(channels)
    first = contract(member, first, ((1,), (0,)), HIGHEST)
    second = contract(member, second, ((1,), (0,)), HIGHEST)
    sums_ref[...] = rows_of(lane_form(first), lane_form(second))


def latent_body(total, grad_ref, latent_ref, cot_ref, stats_ref, sums_ref, out_ref):
    row_count, channels, _ = latent_ref.shape
    sums = sums_ref[0:2] / total
    shape = (8, channels)
    table = rows_of(
        *[
            jnp.broadcast_to(row, shape)
            for row in (stats_ref[0:1], stats_ref[1:2], sums[0:1], sums[1:2])
        ]
    ).T
    mean, inverse, first, second = [table[:, i : i + 1] for i in range(4)]
    for row in range(row_count):
        normed = (latent_ref[row].astype(f32) - mean) * inverse
        change = inverse * (grad_ref[row] - first - normed * second)
        out_ref[row] = (cot_ref[row].astype(f32) + change).astype(bf16)


def place_body(shape, half_blocks, pieces, where_ref, *refs):
    zones, height, width = shape
    count = len(pieces)
    cells = refs[:count]
    core, mine, other, zone_index = [where_ref[i] for i in range(4)]
    spots = [
        (1 - core) * half_blocks + (other ^ rest) if crossed else core * half_blocks + (mine ^ rest)
        for crossed, rest in pieces
    ]
    out_ref, flat_ref, rows_ref, sem = refs[-4:]
    channels = out_ref.shape[1]
    tap_width = zones * width // 3
    whole, part = channels // height, channels % height

    def copies(index, act):
        block = spots[index]

        def copy(size):
            return pltpu.make_async_copy(
                rows_ref.at[index, :, pl.ds(0, size)],
                out_ref.at[:, pl.ds(pl.multiple_of(block * height, 8), size)],
                sem.at[index],
            )

        @pl.when(block < whole)
        def _():
            act(copy(height))

        if part:

            @pl.when(block == whole)
            def _():
                act(copy(part))

    for index in range(count):
        for zone in range(zones):
            left = pl.multiple_of((zone_index ^ zone) * width, LANES)
            flat_ref[index, :, pl.ds(left, width)] = cells[index][zone]
        for tap in range(9):
            left = (tap // 3) * tap_width + (tap % 3) * channels
            rows_ref[index, tap] = flat_ref[index, :, left : left + channels]
        copies(index, lambda copy: copy.start())
    for index in range(count):
        copies(index, lambda copy: copy.wait())


def spread_body(
    known, masks, where_ref, mine_ref, other_ref, table_ref, scale_ref, back_ref, steps_ref
):
    channels = steps_ref.shape[1]
    table_ref[...] = mine_ref[...]
    for core in range(2):

        @pl.when(where_ref[0] == core)
        def _():
            for row in known[core]:
                at = row ^ masks[core]
                table_ref[at : at + 1] = other_ref[row : row + 1]

    table = table_ref[...]
    bound = jnp.max(table[:, channels + NOTE : channels + NOTE + 1], axis=0, keepdims=True)
    power = jnp.floor(jnp.log2(30000.0 / jnp.maximum(bound, 1e-30)))
    power = jnp.clip(power, -100.0, 100.0)
    scale_ref[...] = jnp.exp2(power)
    back_ref[...] = 1.0 / jnp.exp2(power)
    steps_ref[...] = jnp.broadcast_to(table[:, channels : channels + 1], steps_ref.shape)


def gather_body(images, sums_ref, table_ref, out_ref):
    channels = sums_ref.shape[1]
    rows = [sums_ref[0:1], sums_ref[1:2]]
    rows += [table_ref[i : i + 1, :channels] for i in range(images)]
    out_ref[...] = rows_of(*[jnp.broadcast_to(row, out_ref.shape) for row in rows])


def total_body(*refs):
    refs[-1][...] = tree_sum([ref[...] for ref in refs[:-1]])


def time_body(count, embed_ref, total_ref, out_ref):
    columns = embed_ref[...].T
    terms = [columns[:, i : i + 1] * total_ref[2 + i : 3 + i] for i in range(count)]
    out_ref[...] = tree_sum(terms)


def swap_space(cells, mask):
    count = lax.axis_size("space")
    return lax.ppermute(cells, "space", [(i, i ^ mask) for i in range(count)])


def swap_image(cells, masks):
    images = lax.axis_size("dp")
    count = lax.axis_size("space")
    pairs = [
        (i * count + j, (i ^ masks[j % 2]) * count + j) for i in range(images) for j in range(count)
    ]
    return lax.ppermute(cells, ("dp", "space"), pairs)


def slab_program(
    latent, timesteps, norm_gain, norm_bias, conv_weight, conv_bias, time_weight, cotangent
):
    images, row_count, col_count, channels = latent.shape
    assert images == 1
    per_group = channels // GROUPS
    image_count = lax.axis_size("dp")
    slab_count = lax.axis_size("space")
    zones = slab_count // 2
    bits = image_count.bit_length() - 1
    blocks = 2 * image_count
    height = -(-channels // (8 * blocks)) * 8
    tap_width = -(-3 * channels // LANES) * LANES
    width = 3 * tap_width // zones
    local_count = row_count * col_count * per_group
    total_count = local_count * slab_count
    positions = row_count * col_count

    image_index = lax.axis_index("dp")
    slab_index = lax.axis_index("space")
    core = slab_index % 2
    zone_index = slab_index // 2

    lat = latent.transpose(0, 1, 3, 2)[0]
    cot = cotangent.transpose(0, 1, 3, 2)[0]
    gain, bias = norm_gain, norm_bias
    smem = pl.BlockSpec(memory_space=pltpu.SMEM)
    vmem = pl.BlockSpec(memory_space=pltpu.VMEM)
    anywhere = pl.BlockSpec(memory_space=pl.ANY)
    small = jax.ShapeDtypeStruct((8, channels), f32)

    down = [(i, i + 1) for i in range(slab_count - 1)]
    up = [(i + 1, i) for i in range(slab_count - 1)]

    flops = 2 * positions * channels * channels * 9
    taps = pltpu.VMEM((3 * channels, (row_count + 2) * col_count), bf16)
    flat = pltpu.VMEM((3, channels, 3 * channels), bf16)

    slab = pltpu.VMEM((row_count, channels, col_count), bf16)
    own = call(
        functools.partial(stats_body, local_count),
        small,
        (timesteps, lat, cot),
        specs=(smem, anywhere, anywhere),
        scratch=(slab, slab, pltpu.SemaphoreType.DMA((2, row_count))),
        moved=2 * lat.size * 2,
        flops=positions * channels * 60,
        limit=63 << 20,
    )
    partner = swap_space(own, 1)
    pair = call(
        functools.partial(merge_body, local_count, None), small, (own, partner), limit=4 << 20
    )
    parts = [pair]
    for mask in range(1, zones):
        parts.append(swap_space(pair, 2 * mask))
    above = lax.ppermute(cot[row_count - 1], "space", down)
    below = lax.ppermute(cot[0], "space", up)
    lat_above = lax.ppermute(lat[row_count - 1], "space", down)
    lat_below = lax.ppermute(lat[0], "space", up)
    stats = call(
        functools.partial(merge_body, 2 * local_count, total_count),
        small,
        tuple(parts),
        limit=4 << 20,
    )

    orders = [list(range(bits)), list(range(bits))[::-1]]

    def rest_index(which):
        index = 0
        for step in range(bits):
            shift = jnp.where(which == 0, orders[0][step], orders[1][step])
            index = index * 2 + ((image_index >> shift) & 1)
        return index

    mine, other = rest_index(core), rest_index(1 - core)
    inside = [slab_index > 0, slab_index < slab_count - 1]
    where = jnp.stack([core, mine, other, zone_index] + [x.astype(core.dtype) for x in inside])
    where = where.astype(jnp.int32)
    part_shape = jax.ShapeDtypeStruct((blocks // 4, zones, height, width), f32)
    share_shape = jax.ShapeDtypeStruct((blocks // 2, zones, height, width), f32)
    taps_shape = jax.ShapeDtypeStruct((3 * channels, positions), bf16)
    grad_taps, col_sums = call(
        taps_body, (taps_shape, small), (cot,), moved=10 * lat.size, limit=6 << 20
    )
    table_shape = jax.ShapeDtypeStruct((-(-image_count // 8) * 8, channels + 2 * NOTE), f32)
    factor, spread = float(positions * slab_count * image_count), math.sqrt(per_group)
    act, middle_rows, table = call(
        functools.partial(middle_body, factor, spread),
        (
            jax.ShapeDtypeStruct((channels, positions), bf16),
            jax.ShapeDtypeStruct((channels, 3 * channels), f32),
            table_shape,
        ),
        (lat, grad_taps, stats, gain, bias, col_sums),
        flops=flops // 3,
        moved=8 * lat.size,
        limit=8 << 20,
    )
    near, far_low, far_high, edge_taps = call(
        functools.partial(weight_body, (blocks, zones, height, width), col_count),
        (
            share_shape,
            part_shape,
            part_shape,
            jax.ShapeDtypeStruct((3 * channels, 2 * col_count), bf16),
        ),
        (where, act, grad_taps, above, below, middle_rows),
        specs=(smem,) + (vmem,) * 5,
        flops=flops,
        moved=8 * lat.size,
        limit=12 << 20,
    )
    unit = jax.ShapeDtypeStruct((1, 1), f32)
    steps_shape = jax.ShapeDtypeStruct((table_shape.shape[0], channels), f32)
    known = ([0], [0])
    scales = []
    for step in range(bits):
        masks = (1 << orders[0][step], 1 << orders[1][step])
        arrived = swap_image(table, masks)
        table, scale, back, steps = call(
            functools.partial(spread_body, known, masks),
            (table_shape, unit, unit, steps_shape),
            (where, table, arrived),
            specs=(smem,) + (vmem,) * 2,
            limit=4 << 20,
        )
        scales.append((scale[0, 0], back[0, 0]))
        known = tuple(rows + [row ^ mask for row in rows] for rows, mask in zip(known, masks))

    grad, sums = call(
        backward_body,
        (jax.ShapeDtypeStruct((row_count, channels, col_count), f32), small),
        (lat, grad_taps, edge_taps, stats, gain, bias, conv_weight),
        scratch=(flat,),
        flops=flops,
        moved=8 * lat.size,
        limit=8 << 20,
    )
    message = jax.ShapeDtypeStruct((-(-(2 + image_count) // 8) * 8, channels), f32)
    gathered = call(
        functools.partial(gather_body, image_count), message, (sums, table), limit=4 << 20
    )
    gathered = [gathered + swap_space(gathered, 1)]
    for mask in range(1, zones):
        gathered.append(swap_space(gathered[0], 2 * mask))
    totals = call(total_body, message, tuple(gathered), limit=4 << 20)
    line_scale, line_back = scales[-1]

    middle = blocks // 4
    far_in = swap_space(far_high, 1)
    near_in = swap_space(far_low, 1)
    sent = ((near[middle:] + far_in) * scales[0][0]).astype(f16)
    near, near_in, _ = lax.optimization_barrier((near, near_in, sent))
    keeping = near[:middle] + near_in
    for step in range(bits):
        masks = (1 << orders[0][step], 1 << orders[1][step])
        arrived = swap_image(sent, masks)
        back = scales[step][1]
        middle = keeping.shape[0] // 2
        if middle:
            total = keeping[middle:] + arrived[middle:].astype(f32) * back
            sent = (total * scales[step + 1][0]).astype(f16)
            keeping, arrived, _ = lax.optimization_barrier((keeping, arrived, sent))
            keeping = keeping[:middle] + arrived[:middle].astype(f32) * back
    sent = []
    for mask in range(1, zones):
        total = keeping[0, mask] + arrived[0, mask].astype(f32) * back
        sent.append((total * line_scale).astype(f16))
    keeping, arrived, *_ = lax.optimization_barrier((keeping, arrived, *sent))
    share = keeping[0, 0] + arrived[0, 0].astype(f32) * back
    for mask in range(1, zones):
        share = share + swap_space(sent[mask - 1], 2 * mask).astype(f32) * line_back
    share = (share * line_scale).astype(f16)
    collected = [share]
    for mask in range(1, zones):
        collected.append(swap_space(share, 2 * mask))
    pieces = [jnp.stack(collected)]
    for step in reversed(range(bits)):
        masks = (1 << orders[0][step], 1 << orders[1][step])
        arrived = []
        for piece in pieces:
            arrived.append(swap_image(piece, masks))
        pieces = pieces + arrived
    crossed = []
    for piece in pieces:
        crossed.append(swap_space(piece, 1))
    half_blocks = blocks // 2
    numbers = list(range(half_blocks))

    def place(chosen, before):
        count = len(chosen)
        cells = []
        for is_crossed, rest in chosen:
            piece = crossed[rest] if is_crossed else pieces[rest]
            cells.append(piece.astype(f32) * line_back)
        return pl.pallas_call(
            functools.partial(place_body, (zones, height, width), half_blocks, chosen),
            out_shape=jax.ShapeDtypeStruct((9, channels, channels), f32),
            in_specs=[smem] + [vmem] * count + [anywhere] * len(before),
            out_specs=anywhere,
            scratch_shapes=[
                pltpu.VMEM((count, height, zones * width), f32),
                pltpu.VMEM((count, 9, height, channels), f32),
                pltpu.SemaphoreType.DMA((count,)),
            ],
            input_output_aliases={1 + count: 0} if before else {},
            compiler_params=pltpu.CompilerParams(vmem_limit_bytes=12 << 20),
            cost_estimate=pl.CostEstimate(
                flops=0,
                bytes_accessed=8 * count * zones * height * width,
                transcendentals=0,
            ),
        )(where, *cells, *before)

    early = [(side, rest) for side in (False, True) for rest in numbers[:-1]]
    weight_grad = place(early, ())
    weight_grad = place([(False, numbers[-1]), (True, numbers[-1])], (weight_grad,))
    weight_grad = weight_grad.reshape(3, 3, channels, channels)

    half_count = channels // 2
    frequency = jnp.exp(-math.log(10000.0) * jnp.arange(half_count, dtype=f32) / half_count)
    angles = steps[:, :half_count] * frequency[None, :]
    embedding = jnp.concatenate([jnp.cos(angles), jnp.sin(angles)], axis=1).astype(bf16)
    time_bias = jnp.dot(embedding[:1], time_weight, preferred_element_type=f32)
    extra = time_bias + conv_bias.reshape(1, channels)
    time_grad = call(
        functools.partial(time_body, image_count),
        jax.ShapeDtypeStruct((channels, channels), f32),
        (embedding.astype(f32), totals),
        limit=4 << 20,
    )
    block_out = call(
        conv_body,
        jax.ShapeDtypeStruct((row_count, channels, col_count), bf16),
        (where, lat, lat_above, lat_below, stats, gain, bias, conv_weight, extra),
        specs=(smem,) + (vmem,) * 8,
        scratch=(taps, flat),
        flops=flops,
        moved=8 * lat.size,
        limit=14 << 20,
    )
    latent_grad = call(
        functools.partial(latent_body, total_count),
        jax.ShapeDtypeStruct((row_count, channels, col_count), bf16),
        (grad, lat, cot, stats, totals),
        flops=lat.size * 20,
        moved=10 * lat.size,
        limit=12 << 20,
    )

    block_out = block_out[None].transpose(0, 1, 3, 2)
    latent_grad = latent_grad[None].transpose(0, 1, 3, 2)
    return (block_out, latent_grad, weight_grad, time_grad)


def solution(mesh):
    return jax.shard_map(
        slab_program,
        mesh=mesh,
        in_specs=(
            P("dp", "space", None, None),
            P("dp"),
            P(),
            P(),
            P(),
            P(),
            P(),
            P("dp", "space", None, None),
        ),
        out_specs=(P("dp", "space", None, None), P("dp", "space", None, None), P(), P()),
        check_vma=False,
    )
```

```python
import functools
import math

import jax
import jax.numpy as jnp
from jax import lax
from jax.experimental import pallas as pl
from jax.experimental.pallas import tpu as pltpu
from jax.sharding import PartitionSpec as P


GROUPS = 32
epsilon = 1e-05
f32 = jnp.float32
bf16 = jnp.bfloat16
f16 = jnp.float16
HIGHEST = lax.Precision.HIGHEST
LANES = 128
NOTE = 32


def contract(a, b, dims, precision=None):
    return lax.dot_general(a, b, (dims, ((), ())), preferred_element_type=f32, precision=precision)


def call(body, outs, args, specs=None, scratch=(), flops=0, moved=0, limit=40 << 20):
    vmem = pl.BlockSpec(memory_space=pltpu.VMEM)
    many = isinstance(outs, (list, tuple))
    return pl.pallas_call(
        body,
        out_shape=tuple(outs) if many else outs,
        in_specs=list(specs) if specs else [vmem] * len(args),
        out_specs=tuple([vmem] * len(outs)) if many else vmem,
        scratch_shapes=list(scratch),
        compiler_params=pltpu.CompilerParams(vmem_limit_bytes=limit),
        cost_estimate=pl.CostEstimate(flops=flops, bytes_accessed=moved, transcendentals=0),
    )(*args)


def member_matrix(channels):
    per_group = channels // GROUPS
    row = lax.broadcasted_iota(jnp.int32, (channels, channels), 0).astype(f32)
    col = lax.broadcasted_iota(jnp.int32, (channels, channels), 1).astype(f32)
    same = jnp.floor((row + 0.5) / per_group) == jnp.floor((col + 0.5) / per_group)
    return jnp.where(same, 1.0, 0.0).astype(f32)


def lane_form(cells):
    ones = jnp.ones((8, cells.shape[1]), f32)
    return contract(ones, cells, ((1,), (1,)), HIGHEST)


def rows_of(*rows):
    height = lax.broadcasted_iota(jnp.int32, rows[0].shape, 0)
    packed = jnp.zeros(rows[0].shape, f32)
    for number, row in enumerate(rows):
        packed = jnp.where(height == number, row, packed)
    return packed


def fold_lanes(cells):
    total = cells[:, :LANES]
    for start in range(LANES, cells.shape[1], LANES):
        total = total + cells[:, start : start + LANES]
    return total


def stats_body(count, step_ref, latent_hbm, cot_hbm, out_ref, latent_ref, cot_ref, sem):
    row_count, channels, cols = latent_ref.shape
    loads = []
    for number, (source, target) in enumerate(((latent_hbm, latent_ref), (cot_hbm, cot_ref))):
        for row in range(row_count):
            load = pltpu.make_async_copy(source.at[row], target.at[row], sem.at[number, row])
            load.start()
            loads.append(load)
    member = member_matrix(channels)
    ones = jnp.ones((cols, LANES), bf16)
    sums = jnp.zeros((channels, LANES), f32)
    for row in range(row_count):
        loads[row].wait()
        sums = sums + contract(latent_ref[row], ones, ((1,), (0,)))
    mean = contract(member, sums, ((1,), (0,)), HIGHEST) / count
    squares = jnp.zeros((channels, LANES), f32)
    for row in range(row_count):
        centered = latent_ref[row].astype(f32) - mean[:, :1]
        squares = squares + fold_lanes(centered * centered)
    grouped = contract(member, squares, ((1,), (0,)), HIGHEST)
    top = jnp.zeros((channels, LANES), bf16)
    for row in range(row_count):
        loads[row_count + row].wait()
        size = jnp.abs(cot_ref[row])
        for start in range(0, cols, LANES):
            top = jnp.maximum(top, size[:, start : start + LANES])
    step = jnp.full((8, channels), step_ref[0].astype(f32))
    largest = jnp.broadcast_to(jnp.max(top.astype(f32)), (8, channels))
    out_ref[...] = rows_of(lane_form(mean) * (1.0 / LANES), lane_form(grouped), largest, step)


def tree_sum(parts):
    while len(parts) > 1:
        parts = [parts[i] + parts[i + 1] for i in range(0, len(parts), 2)]
    return parts[0]


def merge_body(count, total, *refs):
    parts, out_ref = [ref[...] for ref in refs[:-1]], refs[-1]
    mean = tree_sum([part[0:1] for part in parts]) / len(parts)
    squares = tree_sum([part[1:2] + count * (part[0:1] - mean) ** 2 for part in parts])
    if total:
        squares = lax.rsqrt(squares / total + epsilon)
    largest = functools.reduce(jnp.maximum, [part[2:3] for part in parts])
    rows = (mean, squares, largest, parts[0][3:4])
    out_ref[...] = rows_of(*[jnp.broadcast_to(row, out_ref.shape) for row in rows])


def column_values(stats_ref, gain_ref, bias_ref):
    channels = gain_ref.shape[0]
    shape = (8, channels)
    table = rows_of(
        jnp.broadcast_to(stats_ref[0:1], shape),
        jnp.broadcast_to(stats_ref[1:2], shape),
        jnp.broadcast_to(gain_ref[...], shape),
        jnp.broadcast_to(bias_ref[...], shape),
    ).T
    return [table[:, i : i + 1] for i in range(4)]


def normalized(cells, values):
    mean, inverse, gain, bias = values
    normed = (cells.astype(f32) - mean) * inverse
    shifted = normed * gain + bias
    return normed, shifted, jax.nn.sigmoid(shifted)


def activate(cells, values):
    _, shifted, sigmoid = normalized(cells, values)
    return (shifted * sigmoid).astype(bf16)


def shifted_cols(cells):
    cols = cells.shape[1]
    lane = lax.broadcasted_iota(jnp.int32, cells.shape, 1)
    zero = jnp.zeros_like(cells)
    after = jnp.where(lane == cols - 1, zero, pltpu.roll(cells, cols - 1, 1))
    before = jnp.where(lane == 0, zero, pltpu.roll(cells, 1, 1))
    return after, before


def put_taps(buffer_ref, place, cells, flip):
    channels, cols = cells.shape
    wide = cells.astype(f32)
    after, before = shifted_cols(wide)
    order = (after, cells, before) if flip else (before, cells, after)
    for tap, piece in enumerate(order):
        buffer_ref[tap * channels : (tap + 1) * channels, place * cols : (place + 1) * cols] = (
            piece.astype(bf16)
        )


def taps_body(cot_ref, taps_ref, sums_ref):
    row_count, channels, cols = cot_ref.shape
    tall = jnp.ones((8, cols), bf16)
    sums = jnp.zeros((8, channels), f32)
    for row in range(row_count):
        put_taps(taps_ref, row, cot_ref[row], True)
        sums = sums + contract(tall, cot_ref[row], ((1,), (1,)))
    sums_ref[...] = sums


def middle_body(
    factor, spread, latent_ref, taps_ref, stats_ref, gain_ref, bias_ref, sums_ref, act_ref, found_ref, table_ref
):
    row_count, channels, cols = latent_ref.shape
    table_ref[...] = jnp.zeros(table_ref.shape, f32)
    table_ref[0:1, :channels] = sums_ref[0:1]
    table_ref[0:1, channels : channels + NOTE] = stats_ref[3:4, :NOTE]
    gain = jnp.max(jnp.abs(gain_ref[...][None, :]), axis=1, keepdims=True)
    bias = jnp.max(jnp.abs(bias_ref[...][None, :]), axis=1, keepdims=True)
    bound = stats_ref[2:3] * ((spread * gain + bias) * factor)
    table_ref[0:1, channels + NOTE : channels + 2 * NOTE] = bound[:, :NOTE]
    values = column_values(stats_ref, gain_ref, bias_ref)
    for row in range(row_count):
        act_ref[:, row * cols : (row + 1) * cols] = activate(latent_ref[row], values)
    found_ref[...] = contract(act_ref[...], taps_ref[...], ((1,), (1,)))


def weight_body(
    shape, cols, where_ref, act_ref, taps_ref, above_ref, below_ref, middle_ref,
    near_ref, low_ref, high_ref, edge_ref,
):
    blocks, zones, height, width = shape
    channels, positions = act_ref.shape
    core, mine, other, zone_index = [where_ref[i] for i in range(4)]
    quarter = blocks // 4
    put_taps(edge_ref, 0, above_ref[...], True)
    put_taps(edge_ref, 1, below_ref[...], True)
    tap_width = zones * width // 3

    def store(ref, place, found, block, tap_row):
        first = block * height
        size = max(min(height, channels - first), 0)
        for zone in range(zones):
            low = max(zone * width, tap_row * tap_width)
            high = min((zone + 1) * width, (tap_row + 1) * tap_width)
            if low >= high:
                continue
            at = zone_index ^ zone
            left, right = low - zone * width, high - zone * width
            source = low - tap_row * tap_width
            used = max(min(right - left, 3 * channels - source), 0)
            if size and used:
                ref[place, at, :size, left : left + used] = found[
                    first : first + size, source : source + used
                ]
            if used < right - left:
                ref[place, at, :, left + used : right] = jnp.zeros(
                    (height, right - left - used), f32
                )
            if size < height and used:
                ref[place, at, size:, left : left + used] = jnp.zeros((height - size, used), f32)

    for tap_row in (1, 0, 2):
        if tap_row == 1:
            found = middle_ref
        else:
            inner = slice(0, positions - cols) if tap_row == 0 else slice(cols, positions)
            shifted = slice(cols, positions) if tap_row == 0 else slice(0, positions - cols)
            outer = slice(positions - cols, positions) if tap_row == 0 else slice(0, cols)
            edge = slice(cols, 2 * cols) if tap_row == 0 else slice(0, cols)
            found = contract(act_ref[:, inner], taps_ref[:, shifted], ((1,), (1,)))
            found = found + contract(act_ref[:, outer], edge_ref[:, edge], ((1,), (1,)))
        for half in range(2):

            @pl.when(core == half)
            def _():
                for rest in range(blocks // 2):
                    store(near_ref, mine ^ rest, found, half * blocks // 2 + rest, tap_row)

            for top in range(2):

                @pl.when((core != half) & (other // quarter == top))
                def _():
                    for rest in range(blocks // 2):
                        ref = high_ref if rest // quarter != top else low_ref
                        at = (other ^ rest) % quarter
                        store(ref, at, found, half * blocks // 2 + rest, tap_row)


def conv_body(
    where_ref, latent_ref, above_ref, below_ref, stats_ref, gain_ref, bias_ref, weight_ref,
    extra_ref, out_ref, taps_ref, flat_ref,
):
    row_count, channels, cols = latent_ref.shape
    values = column_values(stats_ref, gain_ref, bias_ref)
    for place, ref, end in ((0, above_ref, 4), (row_count + 1, below_ref, 5)):
        keep = where_ref[end].astype(f32)
        put_taps(taps_ref, place, (activate(ref[...], values).astype(f32) * keep).astype(bf16), False)
    for row in range(row_count):
        put_taps(taps_ref, row + 1, activate(latent_ref[row], values), False)
    for tap_row in range(3):
        flat_ref[tap_row] = weight_ref[tap_row].reshape(3 * channels, channels).T
    extra = jnp.broadcast_to(extra_ref[...], (8, channels)).T[:, :1]
    for row in range(row_count):
        total = latent_ref[row].astype(f32) + extra
        for tap_row in range(3):
            start = (row + tap_row) * cols
            total = total + contract(
                flat_ref[tap_row], taps_ref[:, start : start + cols], ((1,), (0,))
            )
        out_ref[row] = total.astype(bf16)


def backward_body(
    latent_ref, taps_ref, edge_ref, stats_ref, gain_ref, bias_ref, weight_ref,
    grad_ref, sums_ref, flat_ref,
):
    row_count, channels, cols = latent_ref.shape
    values = column_values(stats_ref, gain_ref, bias_ref)
    for tap_row in range(3):
        flat_ref[tap_row] = jnp.concatenate([weight_ref[tap_row, j] for j in range(3)], axis=1)
    first = jnp.zeros((channels, LANES), f32)
    second = jnp.zeros((channels, LANES), f32)
    for row in range(row_count):
        total = jnp.zeros((channels, cols), f32)
        for tap_row in range(3):
            source = row + 1 - tap_row
            if 0 <= source < row_count:
                piece = taps_ref[:, source * cols : (source + 1) * cols]
            else:
                start = cols if source > 0 else 0
                piece = edge_ref[:, start : start + cols]
            total = total + contract(flat_ref[tap_row], piece, ((1,), (0,)))
        normed, shifted, sigmoid = normalized(latent_ref[row], values)
        grad = total * sigmoid * (1.0 + shifted * (1.0 - sigmoid)) * values[2]
        grad_ref[row] = grad
        first = first + fold_lanes(grad)
        second = second + fold_lanes(grad * normed)
    member = member_matrix(channels)
    first = contract(member, first, ((1,), (0,)), HIGHEST)
    second = contract(member, second, ((1,), (0,)), HIGHEST)
    sums_ref[...] = rows_of(lane_form(first), lane_form(second))


def latent_body(total, grad_ref, latent_ref, cot_ref, stats_ref, sums_ref, out_ref):
    row_count, channels, _ = latent_ref.shape
    sums = sums_ref[0:2] / total
    shape = (8, channels)
    table = rows_of(
        *[
            jnp.broadcast_to(row, shape)
            for row in (stats_ref[0:1], stats_ref[1:2], sums[0:1], sums[1:2])
        ]
    ).T
    mean, inverse, first, second = [table[:, i : i + 1] for i in range(4)]
    for row in range(row_count):
        normed = (latent_ref[row].astype(f32) - mean) * inverse
        change = inverse * (grad_ref[row] - first - normed * second)
        out_ref[row] = (cot_ref[row].astype(f32) + change).astype(bf16)


def place_body(shape, half_blocks, pieces, where_ref, *refs):
    zones, height, width = shape
    count = len(pieces)
    cells = refs[:count]
    core, mine, other, zone_index = [where_ref[i] for i in range(4)]
    spots = [
        (1 - core) * half_blocks + (other ^ rest) if crossed else core * half_blocks + (mine ^ rest)
        for crossed, rest in pieces
    ]
    out_ref, flat_ref, rows_ref, sem = refs[-4:]
    channels = out_ref.shape[1]
    tap_width = zones * width // 3
    whole, part = channels // height, channels % height

    def copies(index, act):
        block = spots[index]

        def copy(size):
            return pltpu.make_async_copy(
                rows_ref.at[index, :, pl.ds(0, size)],
                out_ref.at[:, pl.ds(pl.multiple_of(block * height, 8), size)],
                sem.at[index],
            )

        @pl.when(block < whole)
        def _():
            act(copy(height))

        if part:

            @pl.when(block == whole)
            def _():
                act(copy(part))

    for index in range(count):
        for zone in range(zones):
            left = pl.multiple_of((zone_index ^ zone) * width, LANES)
            flat_ref[index, :, pl.ds(left, width)] = cells[index][zone]
        for tap in range(9):
            left = (tap // 3) * tap_width + (tap % 3) * channels
            rows_ref[index, tap] = flat_ref[index, :, left : left + channels]
        copies(index, lambda copy: copy.start())
    for index in range(count):
        copies(index, lambda copy: copy.wait())


def spread_body(
    known, masks, where_ref, mine_ref, other_ref, table_ref, scale_ref, back_ref, steps_ref
):
    channels = steps_ref.shape[1]
    table_ref[...] = mine_ref[...]
    for core in range(2):

        @pl.when(where_ref[0] == core)
        def _():
            for row in known[core]:
                at = row ^ masks[core]
                table_ref[at : at + 1] = other_ref[row : row + 1]

    table = table_ref[...]
    bound = jnp.max(table[:, channels + NOTE : channels + NOTE + 1], axis=0, keepdims=True)
    bound = jnp.maximum(bound, 1e-25) * (1.0 / 30000.0)
    back_ref[...] = bound
    scale_ref[...] = 1.0 / bound
    steps_ref[...] = jnp.broadcast_to(table[:, channels : channels + 1], steps_ref.shape)


def gather_body(images, sums_ref, table_ref, out_ref):
    channels = sums_ref.shape[1]
    rows = [sums_ref[0:1], sums_ref[1:2]]
    rows += [table_ref[i : i + 1, :channels] for i in range(images)]
    out_ref[...] = rows_of(*[jnp.broadcast_to(row, out_ref.shape) for row in rows])


def total_body(*refs):
    refs[-1][...] = tree_sum([ref[...] for ref in refs[:-1]])


def time_body(count, embed_ref, total_ref, out_ref):
    columns = embed_ref[...].T
    terms = [columns[:, i : i + 1] * total_ref[2 + i : 3 + i] for i in range(count)]
    out_ref[...] = tree_sum(terms)


def swap_space(cells, mask):
    count = lax.axis_size("space")
    return lax.ppermute(cells, "space", [(i, i ^ mask) for i in range(count)])


def swap_image(cells, masks):
    images = lax.axis_size("dp")
    count = lax.axis_size("space")
    pairs = [
        (i * count + j, (i ^ masks[j % 2]) * count + j) for i in range(images) for j in range(count)
    ]
    return lax.ppermute(cells, ("dp", "space"), pairs)


def slab_program(
    latent, timesteps, norm_gain, norm_bias, conv_weight, conv_bias, time_weight, cotangent
):
    images, row_count, col_count, channels = latent.shape
    assert images == 1
    per_group = channels // GROUPS
    image_count = lax.axis_size("dp")
    slab_count = lax.axis_size("space")
    zones = slab_count // 2
    bits = image_count.bit_length() - 1
    blocks = 2 * image_count
    height = -(-channels // (8 * blocks)) * 8
    tap_width = -(-3 * channels // LANES) * LANES
    width = 3 * tap_width // zones
    local_count = row_count * col_count * per_group
    total_count = local_count * slab_count
    positions = row_count * col_count

    image_index = lax.axis_index("dp")
    slab_index = lax.axis_index("space")
    core = slab_index % 2
    zone_index = slab_index // 2

    lat = latent.transpose(0, 1, 3, 2)[0]
    cot = cotangent.transpose(0, 1, 3, 2)[0]
    gain, bias = norm_gain, norm_bias
    smem = pl.BlockSpec(memory_space=pltpu.SMEM)
    vmem = pl.BlockSpec(memory_space=pltpu.VMEM)
    anywhere = pl.BlockSpec(memory_space=pl.ANY)
    small = jax.ShapeDtypeStruct((8, channels), f32)

    down = [(i, i + 1) for i in range(slab_count - 1)]
    up = [(i + 1, i) for i in range(slab_count - 1)]

    flops = 2 * positions * channels * channels * 9
    taps = pltpu.VMEM((3 * channels, (row_count + 2) * col_count), bf16)
    flat = pltpu.VMEM((3, channels, 3 * channels), bf16)

    slab = pltpu.VMEM((row_count, channels, col_count), bf16)
    own = call(
        functools.partial(stats_body, local_count),
        small,
        (timesteps, lat, cot),
        specs=(smem, anywhere, anywhere),
        scratch=(slab, slab, pltpu.SemaphoreType.DMA((2, row_count))),
        moved=2 * lat.size * 2,
        flops=positions * channels * 60,
        limit=63 << 20,
    )
    partner = swap_space(own, 1)
    pair = call(
        functools.partial(merge_body, local_count, None), small, (own, partner), limit=4 << 20
    )
    parts = [pair]
    for mask in range(1, zones):
        parts.append(swap_space(pair, 2 * mask))
    above = lax.ppermute(cot[row_count - 1], "space", down)
    below = lax.ppermute(cot[0], "space", up)
    lat_above = lax.ppermute(lat[row_count - 1], "space", down)
    lat_below = lax.ppermute(lat[0], "space", up)
    stats = call(
        functools.partial(merge_body, 2 * local_count, total_count),
        small,
        tuple(parts),
        limit=4 << 20,
    )

    orders = [list(range(bits)), list(range(bits))[::-1]]

    def rest_index(which):
        index = 0
        for step in range(bits):
            shift = jnp.where(which == 0, orders[0][step], orders[1][step])
            index = index * 2 + ((image_index >> shift) & 1)
        return index

    mine, other = rest_index(core), rest_index(1 - core)
    inside = [slab_index > 0, slab_index < slab_count - 1]
    where = jnp.stack([core, mine, other, zone_index] + [x.astype(core.dtype) for x in inside])
    where = where.astype(jnp.int32)
    part_shape = jax.ShapeDtypeStruct((blocks // 4, zones, height, width), f32)
    share_shape = jax.ShapeDtypeStruct((blocks // 2, zones, height, width), f32)
    taps_shape = jax.ShapeDtypeStruct((3 * channels, positions), bf16)
    grad_taps, col_sums = call(
        taps_body, (taps_shape, small), (cot,), moved=10 * lat.size, limit=6 << 20
    )
    table_shape = jax.ShapeDtypeStruct((-(-image_count // 8) * 8, channels + 2 * NOTE), f32)
    factor, spread = float(positions * slab_count * image_count), math.sqrt(per_group)
    act, middle_rows, table = call(
        functools.partial(middle_body, factor, spread),
        (
            jax.ShapeDtypeStruct((channels, positions), bf16),
            jax.ShapeDtypeStruct((channels, 3 * channels), f32),
            table_shape,
        ),
        (lat, grad_taps, stats, gain, bias, col_sums),
        flops=flops // 3,
        moved=8 * lat.size,
        limit=8 << 20,
    )
    near, far_low, far_high, edge_taps = call(
        functools.partial(weight_body, (blocks, zones, height, width), col_count),
        (
            share_shape,
            part_shape,
            part_shape,
            jax.ShapeDtypeStruct((3 * channels, 2 * col_count), bf16),
        ),
        (where, act, grad_taps, above, below, middle_rows),
        specs=(smem,) + (vmem,) * 5,
        flops=flops,
        moved=8 * lat.size,
        limit=12 << 20,
    )
    unit = jax.ShapeDtypeStruct((1, 1), f32)
    steps_shape = jax.ShapeDtypeStruct((table_shape.shape[0], channels), f32)
    known = ([0], [0])
    scales = []
    for step in range(bits):
        masks = (1 << orders[0][step], 1 << orders[1][step])
        arrived = swap_image(table, masks)
        table, scale, back, steps = call(
            functools.partial(spread_body, known, masks),
            (table_shape, unit, unit, steps_shape),
            (where, table, arrived),
            specs=(smem,) + (vmem,) * 2,
            limit=4 << 20,
        )
        scales.append((scale[0, 0], back[0, 0]))
        known = tuple(rows + [row ^ mask for row in rows] for rows, mask in zip(known, masks))

    grad, sums = call(
        backward_body,
        (jax.ShapeDtypeStruct((row_count, channels, col_count), f32), small),
        (lat, grad_taps, edge_taps, stats, gain, bias, conv_weight),
        scratch=(flat,),
        flops=flops,
        moved=8 * lat.size,
        limit=8 << 20,
    )
    message = jax.ShapeDtypeStruct((-(-(2 + image_count) // 8) * 8, channels), f32)
    gathered = call(
        functools.partial(gather_body, image_count), message, (sums, table), limit=4 << 20
    )
    gathered = [gathered + swap_space(gathered, 1)]
    for mask in range(1, zones):
        gathered.append(swap_space(gathered[0], 2 * mask))
    totals = call(total_body, message, tuple(gathered), limit=4 << 20)
    line_scale, line_back = scales[-1]

    middle = blocks // 4
    far_in = swap_space(far_high, 1)
    near_in = swap_space(far_low, 1)
    sent = ((near[middle:] + far_in) * scales[0][0]).astype(f16)
    near, near_in, _ = lax.optimization_barrier((near, near_in, sent))
    keeping = near[:middle] + near_in
    for step in range(bits):
        masks = (1 << orders[0][step], 1 << orders[1][step])
        arrived = swap_image(sent, masks)
        back = scales[step][1]
        middle = keeping.shape[0] // 2
        if middle:
            total = keeping[middle:] + arrived[middle:].astype(f32) * back
            sent = (total * scales[step + 1][0]).astype(f16)
            keeping, arrived, _ = lax.optimization_barrier((keeping, arrived, sent))
            keeping = keeping[:middle] + arrived[:middle].astype(f32) * back
    sent = []
    for mask in range(1, zones):
        total = keeping[0, mask] + arrived[0, mask].astype(f32) * back
        sent.append((total * line_scale).astype(f16))
    keeping, arrived, *_ = lax.optimization_barrier((keeping, arrived, *sent))
    share = keeping[0, 0] + arrived[0, 0].astype(f32) * back
    for mask in range(1, zones):
        share = share + swap_space(sent[mask - 1], 2 * mask).astype(f32) * line_back
    share = (share * line_scale).astype(f16)
    collected = [share]
    for mask in range(1, zones):
        collected.append(swap_space(share, 2 * mask))
    pieces = [jnp.stack(collected)]
    for step in reversed(range(bits)):
        masks = (1 << orders[0][step], 1 << orders[1][step])
        arrived = []
        for piece in pieces:
            arrived.append(swap_image(piece, masks))
        pieces = pieces + arrived
    crossed = []
    for piece in pieces:
        crossed.append(swap_space(piece, 1))
    half_blocks = blocks // 2
    numbers = list(range(half_blocks))

    def place(chosen, before):
        count = len(chosen)
        cells = []
        for is_crossed, rest in chosen:
            piece = crossed[rest] if is_crossed else pieces[rest]
            cells.append(piece.astype(f32) * line_back)
        return pl.pallas_call(
            functools.partial(place_body, (zones, height, width), half_blocks, chosen),
            out_shape=jax.ShapeDtypeStruct((9, channels, channels), f32),
            in_specs=[smem] + [vmem] * count + [anywhere] * len(before),
            out_specs=anywhere,
            scratch_shapes=[
                pltpu.VMEM((count, height, zones * width), f32),
                pltpu.VMEM((count, 9, height, channels), f32),
                pltpu.SemaphoreType.DMA((count,)),
            ],
            input_output_aliases={1 + count: 0} if before else {},
            compiler_params=pltpu.CompilerParams(vmem_limit_bytes=12 << 20),
            cost_estimate=pl.CostEstimate(
                flops=0,
                bytes_accessed=8 * count * zones * height * width,
                transcendentals=0,
            ),
        )(where, *cells, *before)

    early = [(side, rest) for side in (False, True) for rest in numbers[:-1]]
    weight_grad = place(early, ())
    weight_grad = place([(False, numbers[-1]), (True, numbers[-1])], (weight_grad,))
    weight_grad = weight_grad.reshape(3, 3, channels, channels)

    half_count = channels // 2
    frequency = jnp.exp(-math.log(10000.0) * jnp.arange(half_count, dtype=f32) / half_count)
    angles = steps[:, :half_count] * frequency[None, :]
    embedding = jnp.concatenate([jnp.cos(angles), jnp.sin(angles)], axis=1).astype(bf16)
    time_bias = jnp.dot(embedding[:1], time_weight, preferred_element_type=f32)
    extra = time_bias + conv_bias.reshape(1, channels)
    time_grad = call(
        functools.partial(time_body, image_count),
        jax.ShapeDtypeStruct((channels, channels), f32),
        (embedding.astype(f32), totals),
        limit=4 << 20,
    )
    block_out = call(
        conv_body,
        jax.ShapeDtypeStruct((row_count, channels, col_count), bf16),
        (where, lat, lat_above, lat_below, stats, gain, bias, conv_weight, extra),
        specs=(smem,) + (vmem,) * 8,
        scratch=(taps, flat),
        flops=flops,
        moved=8 * lat.size,
        limit=14 << 20,
    )
    latent_grad = call(
        functools.partial(latent_body, total_count),
        jax.ShapeDtypeStruct((row_count, channels, col_count), bf16),
        (grad, lat, cot, stats, totals),
        flops=lat.size * 20,
        moved=10 * lat.size,
        limit=12 << 20,
    )

    block_out = block_out[None].transpose(0, 1, 3, 2)
    latent_grad = latent_grad[None].transpose(0, 1, 3, 2)
    return (block_out, latent_grad, weight_grad, time_grad)


def solution(mesh):
    return jax.shard_map(
        slab_program,
        mesh=mesh,
        in_specs=(
            P("dp", "space", None, None),
            P("dp"),
            P(),
            P(),
            P(),
            P(),
            P(),
            P("dp", "space", None, None),
        ),
        out_specs=(P("dp", "space", None, None), P("dp", "space", None, None), P(), P()),
        check_vma=False,
    )
```

```python
import functools
import math

import jax
import jax.numpy as jnp
from jax import lax
from jax.experimental import pallas as pl
from jax.experimental.pallas import tpu as pltpu
from jax.sharding import PartitionSpec as P


GROUPS = 32
epsilon = 1e-05
f32 = jnp.float32
bf16 = jnp.bfloat16
f16 = jnp.float16
HIGHEST = lax.Precision.HIGHEST
LANES = 128
NOTE = 32


def contract(a, b, dims, precision=None):
    return lax.dot_general(a, b, (dims, ((), ())), preferred_element_type=f32, precision=precision)


def spot(bits):
    image, slab = lax.axis_index("dp"), lax.axis_index("space")
    core = lax.rem(slab, 2)

    def index(which):
        found = 0
        for step in range(bits):
            shift = jnp.where(which == 0, step, bits - 1 - step)
            found = found * 2 + (lax.shift_right_logical(image, shift) & 1)
        return found

    return core, index(core), index(1 - core), lax.shift_right_logical(slab, 1)


def call(body, outs, args, specs=None, scratch=(), flops=0, moved=0, limit=40 << 20):
    vmem = pl.BlockSpec(memory_space=pltpu.VMEM)
    many = isinstance(outs, (list, tuple))
    return pl.pallas_call(
        body,
        out_shape=tuple(outs) if many else outs,
        in_specs=list(specs) if specs else [vmem] * len(args),
        out_specs=tuple([vmem] * len(outs)) if many else vmem,
        scratch_shapes=list(scratch),
        compiler_params=pltpu.CompilerParams(vmem_limit_bytes=limit),
        cost_estimate=pl.CostEstimate(flops=flops, bytes_accessed=moved, transcendentals=0),
    )(*args)


def member_matrix(channels):
    per_group = channels // GROUPS
    row = lax.broadcasted_iota(jnp.int32, (channels, channels), 0).astype(f32)
    col = lax.broadcasted_iota(jnp.int32, (channels, channels), 1).astype(f32)
    same = jnp.floor((row + 0.5) / per_group) == jnp.floor((col + 0.5) / per_group)
    return jnp.where(same, 1.0, 0.0).astype(f32)


def lane_form(cells):
    ones = jnp.ones((8, cells.shape[1]), f32)
    return contract(ones, cells, ((1,), (1,)), HIGHEST)


def rows_of(*rows):
    height = lax.broadcasted_iota(jnp.int32, rows[0].shape, 0)
    packed = jnp.zeros(rows[0].shape, f32)
    for number, row in enumerate(rows):
        packed = jnp.where(height == number, row, packed)
    return packed


def fold_lanes(cells):
    total = cells[:, :LANES]
    for start in range(LANES, cells.shape[1], LANES):
        total = total + cells[:, start : start + LANES]
    return total


def stats_body(count, latent_hbm, cot_hbm, out_ref, latent_ref, cot_ref, sem):
    row_count, channels, cols = latent_ref.shape
    loads = []
    for number, (source, target) in enumerate(((latent_hbm, latent_ref), (cot_hbm, cot_ref))):
        for row in range(row_count):
            load = pltpu.make_async_copy(source.at[row], target.at[row], sem.at[number, row])
            load.start()
            loads.append(load)
    member = member_matrix(channels)
    ones = jnp.ones((cols, LANES), bf16)
    sums = jnp.zeros((channels, LANES), f32)
    for row in range(row_count):
        loads[row].wait()
        sums = sums + contract(latent_ref[row], ones, ((1,), (0,)))
    mean = contract(member, sums, ((1,), (0,)), HIGHEST) / count
    squares = jnp.zeros((channels, LANES), f32)
    for row in range(row_count):
        centered = latent_ref[row].astype(f32) - mean[:, :1]
        squares = squares + fold_lanes(centered * centered)
    grouped = contract(member, squares, ((1,), (0,)), HIGHEST)
    top = jnp.zeros((channels, LANES), bf16)
    for row in range(row_count):
        loads[row_count + row].wait()
        size = jnp.abs(cot_ref[row])
        for start in range(0, cols, LANES):
            top = jnp.maximum(top, size[:, start : start + LANES])
    largest = jnp.broadcast_to(jnp.max(top.astype(f32)), (8, channels))
    out_ref[...] = rows_of(lane_form(mean) * (1.0 / LANES), lane_form(grouped), largest)


def tree_sum(parts):
    while len(parts) > 1:
        parts = [parts[i] + parts[i + 1] for i in range(0, len(parts), 2)]
    return parts[0]


def merge_body(count, total, *refs):
    parts, out_ref = [ref[...] for ref in refs[:-1]], refs[-1]
    mean = tree_sum([part[0:1] for part in parts]) / len(parts)
    squares = tree_sum([part[1:2] + count * (part[0:1] - mean) ** 2 for part in parts])
    if total:
        squares = lax.rsqrt(squares / total + epsilon)
    largest = functools.reduce(jnp.maximum, [part[2:3] for part in parts])
    rows = (mean, squares, largest)
    out_ref[...] = rows_of(*[jnp.broadcast_to(row, out_ref.shape) for row in rows])


def column_values(stats_ref, gain_ref, bias_ref):
    channels = gain_ref.shape[0]
    shape = (8, channels)
    table = rows_of(
        jnp.broadcast_to(stats_ref[0:1], shape),
        jnp.broadcast_to(stats_ref[1:2], shape),
        jnp.broadcast_to(gain_ref[...], shape),
        jnp.broadcast_to(bias_ref[...], shape),
    ).T
    return [table[:, i : i + 1] for i in range(4)]


def normalized(cells, values):
    mean, inverse, gain, bias = values
    normed = (cells.astype(f32) - mean) * inverse
    shifted = normed * gain + bias
    return normed, shifted, jax.nn.sigmoid(shifted)


def activate(cells, values):
    _, shifted, sigmoid = normalized(cells, values)
    return (shifted * sigmoid).astype(bf16)


def shifted_cols(cells):
    cols = cells.shape[1]
    lane = lax.broadcasted_iota(jnp.int32, cells.shape, 1)
    zero = jnp.zeros_like(cells)
    after = jnp.where(lane == cols - 1, zero, pltpu.roll(cells, cols - 1, 1))
    before = jnp.where(lane == 0, zero, pltpu.roll(cells, 1, 1))
    return after, before


def put_taps(buffer_ref, place, cells, flip):
    channels, cols = cells.shape
    wide = cells.astype(f32)
    after, before = shifted_cols(wide)
    order = (after, cells, before) if flip else (before, cells, after)
    start = place * cols if isinstance(place, int) else pl.multiple_of(place * cols, LANES)
    for tap, piece in enumerate(order):
        buffer_ref[tap * channels : (tap + 1) * channels, pl.ds(start, cols)] = piece.astype(bf16)


def taps_body(cot_ref, taps_ref, sums_ref):
    row_count, channels, cols = cot_ref.shape
    tall = jnp.ones((8, cols), bf16)
    sums = jnp.zeros((8, channels), f32)
    for row in range(row_count):
        put_taps(taps_ref, row, cot_ref[row], True)
        sums = sums + contract(tall, cot_ref[row], ((1,), (1,)))
    sums_ref[...] = sums


def middle_body(
    factor, spread, latent_ref, taps_ref, stats_ref, gain_ref, bias_ref, sums_ref, step_ref,
    act_ref, found_ref, table_ref,
):
    row_count, channels, cols = latent_ref.shape
    table_ref[...] = jnp.zeros(table_ref.shape, f32)
    table_ref[0:1, :channels] = sums_ref[0:1]
    table_ref[0:1, channels : channels + NOTE] = jnp.broadcast_to(step_ref[...], (1, NOTE))
    gain = jnp.max(jnp.abs(gain_ref[...][None, :]), axis=1, keepdims=True)
    bias = jnp.max(jnp.abs(bias_ref[...][None, :]), axis=1, keepdims=True)
    bound = stats_ref[2:3] * ((spread * gain + bias) * factor)
    table_ref[0:1, channels + NOTE : channels + 2 * NOTE] = bound[:, :NOTE]
    values = column_values(stats_ref, gain_ref, bias_ref)
    for row in range(row_count):
        act_ref[:, row * cols : (row + 1) * cols] = activate(latent_ref[row], values)
    found_ref[...] = contract(act_ref[...], taps_ref[...], ((1,), (1,)))


def weight_body(
    shape, cols, act_ref, taps_ref, outer_ref, inner_ref, middle_ref,
    near_ref, low_ref, high_ref, edge_ref,
):
    blocks, zones, height, width = shape
    channels, positions = act_ref.shape
    core, mine, other, zone_index = spot((blocks // 2).bit_length() - 1)
    quarter = blocks // 4
    put_taps(edge_ref, core, outer_ref[...], True)
    put_taps(edge_ref, 1 - core, inner_ref[...], True)
    tap_width = zones * width // 3

    def store(ref, place, found, block, tap_row):
        first = block * height
        size = max(min(height, channels - first), 0)
        for zone in range(zones):
            low = max(zone * width, tap_row * tap_width)
            high = min((zone + 1) * width, (tap_row + 1) * tap_width)
            if low >= high:
                continue
            at = zone_index ^ zone
            left, right = low - zone * width, high - zone * width
            source = low - tap_row * tap_width
            used = max(min(right - left, 3 * channels - source), 0)
            if size and used:
                ref[place, at, :size, left : left + used] = found[
                    first : first + size, source : source + used
                ]
            if used < right - left:
                ref[place, at, :, left + used : right] = jnp.zeros(
                    (height, right - left - used), f32
                )
            if size < height and used:
                ref[place, at, size:, left : left + used] = jnp.zeros((height - size, used), f32)

    for tap_row in (1, 0, 2):
        if tap_row == 1:
            found = middle_ref
        else:
            inner = slice(0, positions - cols) if tap_row == 0 else slice(cols, positions)
            shifted = slice(cols, positions) if tap_row == 0 else slice(0, positions - cols)
            outer = slice(positions - cols, positions) if tap_row == 0 else slice(0, cols)
            edge = slice(cols, 2 * cols) if tap_row == 0 else slice(0, cols)
            found = contract(act_ref[:, inner], taps_ref[:, shifted], ((1,), (1,)))
            found = found + contract(act_ref[:, outer], edge_ref[:, edge], ((1,), (1,)))
        for half in range(2):

            @pl.when(core == half)
            def _():
                for rest in range(blocks // 2):
                    store(near_ref, mine ^ rest, found, half * blocks // 2 + rest, tap_row)

            for top in range(2):

                @pl.when((core != half) & (other // quarter == top))
                def _():
                    for rest in range(blocks // 2):
                        ref = high_ref if rest // quarter != top else low_ref
                        at = (other ^ rest) % quarter
                        store(ref, at, found, half * blocks // 2 + rest, tap_row)


def conv_body(
    latent_ref, outer_ref, inner_ref, stats_ref, gain_ref, bias_ref, weight_ref,
    extra_ref, out_ref, taps_ref, flat_ref,
):
    row_count, channels, cols = latent_ref.shape
    values = column_values(stats_ref, gain_ref, bias_ref)
    slab, last = lax.axis_index("space"), lax.axis_size("space") - 1
    core = lax.rem(slab, 2)
    keep = jnp.where((slab == 0) | (slab == last), 0.0, 1.0).astype(f32)
    outer = (activate(outer_ref[...], values).astype(f32) * keep).astype(bf16)
    put_taps(taps_ref, core * (row_count + 1), outer, False)
    put_taps(taps_ref, (1 - core) * (row_count + 1), activate(inner_ref[...], values), False)
    for row in range(row_count):
        put_taps(taps_ref, row + 1, activate(latent_ref[row], values), False)
    for tap_row in range(3):
        flat_ref[tap_row] = weight_ref[tap_row].reshape(3 * channels, channels).T
    extra = jnp.broadcast_to(extra_ref[...], (8, channels)).T[:, :1]
    for row in range(row_count):
        total = latent_ref[row].astype(f32) + extra
        for tap_row in range(3):
            start = (row + tap_row) * cols
            total = total + contract(
                flat_ref[tap_row], taps_ref[:, start : start + cols], ((1,), (0,))
            )
        out_ref[row] = total.astype(bf16)


def backward_body(
    latent_ref, taps_ref, edge_ref, stats_ref, gain_ref, bias_ref, weight_ref,
    grad_ref, sums_ref, flat_ref,
):
    row_count, channels, cols = latent_ref.shape
    values = column_values(stats_ref, gain_ref, bias_ref)
    for tap_row in range(3):
        flat_ref[tap_row] = jnp.concatenate([weight_ref[tap_row, j] for j in range(3)], axis=1)
    first = jnp.zeros((channels, LANES), f32)
    second = jnp.zeros((channels, LANES), f32)
    for row in range(row_count):
        total = jnp.zeros((channels, cols), f32)
        for tap_row in range(3):
            source = row + 1 - tap_row
            if 0 <= source < row_count:
                piece = taps_ref[:, source * cols : (source + 1) * cols]
            else:
                start = cols if source > 0 else 0
                piece = edge_ref[:, start : start + cols]
            total = total + contract(flat_ref[tap_row], piece, ((1,), (0,)))
        normed, shifted, sigmoid = normalized(latent_ref[row], values)
        grad = total * sigmoid * (1.0 + shifted * (1.0 - sigmoid)) * values[2]
        grad_ref[row] = grad
        first = first + fold_lanes(grad)
        second = second + fold_lanes(grad * normed)
    member = member_matrix(channels)
    first = contract(member, first, ((1,), (0,)), HIGHEST)
    second = contract(member, second, ((1,), (0,)), HIGHEST)
    sums_ref[...] = rows_of(lane_form(first), lane_form(second))


def latent_body(total, grad_ref, latent_ref, cot_ref, stats_ref, sums_ref, out_ref):
    row_count, channels, _ = latent_ref.shape
    sums = sums_ref[0:2] / total
    shape = (8, channels)
    table = rows_of(
        *[
            jnp.broadcast_to(row, shape)
            for row in (stats_ref[0:1], stats_ref[1:2], sums[0:1], sums[1:2])
        ]
    ).T
    mean, inverse, first, second = [table[:, i : i + 1] for i in range(4)]
    for row in range(row_count):
        normed = (latent_ref[row].astype(f32) - mean) * inverse
        change = inverse * (grad_ref[row] - first - normed * second)
        out_ref[row] = (cot_ref[row].astype(f32) + change).astype(bf16)


def place_body(shape, half_blocks, pieces, *refs):
    zones, height, width = shape
    count = len(pieces)
    cells = refs[:count]
    core, mine, other, zone_index = spot(half_blocks.bit_length() - 1)
    spots = [
        (1 - core) * half_blocks + (other ^ rest) if crossed else core * half_blocks + (mine ^ rest)
        for crossed, rest in pieces
    ]
    out_ref, flat_ref, rows_ref, sem = refs[-4:]
    channels = out_ref.shape[1]
    tap_width = zones * width // 3
    whole, part = channels // height, channels % height

    def copies(index, act):
        block = spots[index]

        def copy(size):
            return pltpu.make_async_copy(
                rows_ref.at[index, :, pl.ds(0, size)],
                out_ref.at[:, pl.ds(pl.multiple_of(block * height, 8), size)],
                sem.at[index],
            )

        @pl.when(block < whole)
        def _():
            act(copy(height))

        if part:

            @pl.when(block == whole)
            def _():
                act(copy(part))

    for index in range(count):
        for zone in range(zones):
            left = pl.multiple_of((zone_index ^ zone) * width, LANES)
            flat_ref[index, :, pl.ds(left, width)] = cells[index][zone]
        for tap in range(9):
            left = (tap // 3) * tap_width + (tap % 3) * channels
            rows_ref[index, tap] = flat_ref[index, :, left : left + channels]
        copies(index, lambda copy: copy.start())
    for index in range(count):
        copies(index, lambda copy: copy.wait())


def spread_body(
    known, masks, mine_ref, other_ref, table_ref, scale_ref, back_ref, steps_ref
):
    channels = steps_ref.shape[1]
    table_ref[...] = mine_ref[...]
    for core in range(2):

        @pl.when(lax.rem(lax.axis_index("space"), 2) == core)
        def _():
            for row in known[core]:
                at = row ^ masks[core]
                table_ref[at : at + 1] = other_ref[row : row + 1]

    table = table_ref[...]
    bound = jnp.max(table[:, channels + NOTE : channels + NOTE + 1], axis=0, keepdims=True)
    bound = jnp.maximum(bound, 1e-25) * (1.0 / 30000.0)
    back_ref[...] = bound
    scale_ref[...] = 1.0 / bound
    steps_ref[...] = jnp.broadcast_to(table[:, channels : channels + 1], steps_ref.shape)


def gather_body(images, sums_ref, table_ref, out_ref):
    channels = sums_ref.shape[1]
    rows = [sums_ref[0:1], sums_ref[1:2]]
    rows += [table_ref[i : i + 1, :channels] for i in range(images)]
    out_ref[...] = rows_of(*[jnp.broadcast_to(row, out_ref.shape) for row in rows])


def total_body(*refs):
    refs[-1][...] = tree_sum([ref[...] for ref in refs[:-1]])


def time_body(count, embed_ref, total_ref, out_ref):
    columns = embed_ref[...].T
    terms = [columns[:, i : i + 1] * total_ref[2 + i : 3 + i] for i in range(count)]
    out_ref[...] = tree_sum(terms)


def swap_space(cells, mask):
    count = lax.axis_size("space")
    return lax.ppermute(cells, "space", [(i, i ^ mask) for i in range(count)])


def swap_image(cells, masks):
    images = lax.axis_size("dp")
    count = lax.axis_size("space")
    pairs = [
        (i * count + j, (i ^ masks[j % 2]) * count + j) for i in range(images) for j in range(count)
    ]
    return lax.ppermute(cells, ("dp", "space"), pairs)


def slab_program(
    latent, timesteps, norm_gain, norm_bias, conv_weight, conv_bias, time_weight, cotangent
):
    images, row_count, col_count, channels = latent.shape
    assert images == 1
    per_group = channels // GROUPS
    image_count = lax.axis_size("dp")
    slab_count = lax.axis_size("space")
    zones = slab_count // 2
    bits = image_count.bit_length() - 1
    blocks = 2 * image_count
    height = -(-channels // (8 * blocks)) * 8
    tap_width = -(-3 * channels // LANES) * LANES
    width = 3 * tap_width // zones
    local_count = row_count * col_count * per_group
    total_count = local_count * slab_count
    positions = row_count * col_count

    slab_index = lax.axis_index("space")
    core = slab_index % 2

    lat = latent.transpose(0, 1, 3, 2)[0]
    cot = cotangent.transpose(0, 1, 3, 2)[0]
    gain, bias = norm_gain, norm_bias
    vmem = pl.BlockSpec(memory_space=pltpu.VMEM)
    anywhere = pl.BlockSpec(memory_space=pl.ANY)
    small = jax.ShapeDtypeStruct((8, channels), f32)

    flops = 2 * positions * channels * channels * 9
    taps = pltpu.VMEM((3 * channels, (row_count + 2) * col_count), bf16)
    flat = pltpu.VMEM((3, channels, 3 * channels), bf16)

    slab = pltpu.VMEM((row_count, channels, col_count), bf16)
    own = call(
        functools.partial(stats_body, local_count),
        small,
        (lat, cot),
        specs=(anywhere, anywhere),
        scratch=(slab, slab, pltpu.SemaphoreType.DMA((2, row_count))),
        moved=2 * lat.size * 2,
        flops=positions * channels * 60,
        limit=63 << 20,
    )
    partner = swap_space(own, 1)
    pair = call(
        functools.partial(merge_body, local_count, None), small, (own, partner), limit=4 << 20
    )
    parts = [pair]
    for mask in range(1, zones):
        parts.append(swap_space(pair, 2 * mask))
    far_row = jnp.where(core == 0, 0, row_count - 1)
    between = [(i, i - 1 if i % 2 == 0 else i + 1) for i in range(1, slab_count - 1)]

    def edges(cells):
        outward = lax.dynamic_index_in_dim(cells, far_row, 0, keepdims=False)
        inward = lax.dynamic_index_in_dim(cells, row_count - 1 - far_row, 0, keepdims=False)
        outer = lax.ppermute(outward, "space", between)
        return outer, swap_space(inward, 1)

    outer, inner = edges(cot)
    lat_outer, lat_inner = edges(lat)
    stats = call(
        functools.partial(merge_body, 2 * local_count, total_count),
        small,
        tuple(parts),
        limit=4 << 20,
    )

    orders = [list(range(bits)), list(range(bits))[::-1]]

    part_shape = jax.ShapeDtypeStruct((blocks // 4, zones, height, width), f32)
    share_shape = jax.ShapeDtypeStruct((blocks // 2, zones, height, width), f32)
    taps_shape = jax.ShapeDtypeStruct((3 * channels, positions), bf16)
    grad_taps, col_sums = call(
        taps_body, (taps_shape, small), (cot,), moved=10 * lat.size, limit=6 << 20
    )
    table_shape = jax.ShapeDtypeStruct((-(-image_count // 8) * 8, channels + 2 * NOTE), f32)
    factor, spread = float(positions * slab_count * image_count), math.sqrt(per_group)
    act, middle_rows, table = call(
        functools.partial(middle_body, factor, spread),
        (
            jax.ShapeDtypeStruct((channels, positions), bf16),
            jax.ShapeDtypeStruct((channels, 3 * channels), f32),
            table_shape,
        ),
        (lat, grad_taps, stats, gain, bias, col_sums, timesteps.astype(f32).reshape(1, 1)),
        flops=flops // 3,
        moved=8 * lat.size,
        limit=8 << 20,
    )
    near, far_low, far_high, edge_taps = call(
        functools.partial(weight_body, (blocks, zones, height, width), col_count),
        (
            share_shape,
            part_shape,
            part_shape,
            jax.ShapeDtypeStruct((3 * channels, 2 * col_count), bf16),
        ),
        (act, grad_taps, outer, inner, middle_rows),
        flops=flops,
        moved=8 * lat.size,
        limit=12 << 20,
    )
    unit = jax.ShapeDtypeStruct((1, 1), f32)
    steps_shape = jax.ShapeDtypeStruct((table_shape.shape[0], channels), f32)
    known = ([0], [0])
    scales = []
    for step in range(bits):
        masks = (1 << orders[0][step], 1 << orders[1][step])
        arrived = swap_image(table, masks)
        table, scale, back, steps = call(
            functools.partial(spread_body, known, masks),
            (table_shape, unit, unit, steps_shape),
            (table, arrived),
            limit=4 << 20,
        )
        scales.append((scale[0, 0], back[0, 0]))
        known = tuple(rows + [row ^ mask for row in rows] for rows, mask in zip(known, masks))

    grad, sums = call(
        backward_body,
        (jax.ShapeDtypeStruct((row_count, channels, col_count), f32), small),
        (lat, grad_taps, edge_taps, stats, gain, bias, conv_weight),
        scratch=(flat,),
        flops=flops,
        moved=8 * lat.size,
        limit=8 << 20,
    )
    message = jax.ShapeDtypeStruct((-(-(2 + image_count) // 8) * 8, channels), f32)
    gathered = call(
        functools.partial(gather_body, image_count), message, (sums, table), limit=4 << 20
    )
    gathered = [gathered + swap_space(gathered, 1)]
    for mask in range(1, zones):
        gathered.append(swap_space(gathered[0], 2 * mask))
    totals = call(total_body, message, tuple(gathered), limit=4 << 20)
    line_scale, line_back = scales[-1]

    middle = blocks // 4
    far_in = swap_space(far_high, 1)
    near_in = swap_space(far_low, 1)
    sent = ((near[middle:] + far_in) * scales[0][0]).astype(f16)
    near, near_in, _ = lax.optimization_barrier((near, near_in, sent))
    keeping = near[:middle] + near_in
    for step in range(bits):
        masks = (1 << orders[0][step], 1 << orders[1][step])
        arrived = swap_image(sent, masks)
        back = scales[step][1]
        middle = keeping.shape[0] // 2
        if middle:
            total = keeping[middle:] + arrived[middle:].astype(f32) * back
            sent = (total * scales[step + 1][0]).astype(f16)
            keeping, arrived, _ = lax.optimization_barrier((keeping, arrived, sent))
            keeping = keeping[:middle] + arrived[:middle].astype(f32) * back
    sent = []
    for mask in range(1, zones):
        total = keeping[0, mask] + arrived[0, mask].astype(f32) * back
        sent.append((total * line_scale).astype(f16))
    keeping, arrived, *_ = lax.optimization_barrier((keeping, arrived, *sent))
    share = keeping[0, 0] + arrived[0, 0].astype(f32) * back
    for mask in range(1, zones):
        share = share + swap_space(sent[mask - 1], 2 * mask).astype(f32) * line_back
    share = (share * line_scale).astype(f16)
    collected = [share]
    for mask in range(1, zones):
        collected.append(swap_space(share, 2 * mask))
    pieces = [jnp.stack(collected)]
    for step in reversed(range(bits)):
        masks = (1 << orders[0][step], 1 << orders[1][step])
        arrived = []
        for piece in pieces:
            arrived.append(swap_image(piece, masks))
        pieces = pieces + arrived
    crossed = []
    for piece in pieces:
        crossed.append(swap_space(piece, 1))
    half_blocks = blocks // 2
    numbers = list(range(half_blocks))

    def place(chosen, before):
        count = len(chosen)
        cells = []
        for is_crossed, rest in chosen:
            piece = crossed[rest] if is_crossed else pieces[rest]
            cells.append(piece.astype(f32) * line_back)
        return pl.pallas_call(
            functools.partial(place_body, (zones, height, width), half_blocks, chosen),
            out_shape=jax.ShapeDtypeStruct((9, channels, channels), f32),
            in_specs=[vmem] * count + [anywhere] * len(before),
            out_specs=anywhere,
            scratch_shapes=[
                pltpu.VMEM((count, height, zones * width), f32),
                pltpu.VMEM((count, 9, height, channels), f32),
                pltpu.SemaphoreType.DMA((count,)),
            ],
            input_output_aliases={count: 0} if before else {},
            compiler_params=pltpu.CompilerParams(vmem_limit_bytes=12 << 20),
            cost_estimate=pl.CostEstimate(
                flops=0,
                bytes_accessed=8 * count * zones * height * width,
                transcendentals=0,
            ),
        )(*cells, *before)

    early = [(side, rest) for side in (False, True) for rest in numbers[:-1]]
    weight_grad = place(early, ())
    weight_grad = place([(False, numbers[-1]), (True, numbers[-1])], (weight_grad,))
    weight_grad = weight_grad.reshape(3, 3, channels, channels)

    half_count = channels // 2
    frequency = jnp.exp(-math.log(10000.0) * jnp.arange(half_count, dtype=f32) / half_count)
    angles = steps[:, :half_count] * frequency[None, :]
    embedding = jnp.concatenate([jnp.cos(angles), jnp.sin(angles)], axis=1).astype(bf16)
    time_bias = jnp.dot(embedding[:1], time_weight, preferred_element_type=f32)
    extra = time_bias + conv_bias.reshape(1, channels)
    time_grad = call(
        functools.partial(time_body, image_count),
        jax.ShapeDtypeStruct((channels, channels), f32),
        (embedding.astype(f32), totals),
        limit=4 << 20,
    )
    block_out = call(
        conv_body,
        jax.ShapeDtypeStruct((row_count, channels, col_count), bf16),
        (lat, lat_outer, lat_inner, stats, gain, bias, conv_weight, extra),
        scratch=(taps, flat),
        flops=flops,
        moved=8 * lat.size,
        limit=14 << 20,
    )
    latent_grad = call(
        functools.partial(latent_body, total_count),
        jax.ShapeDtypeStruct((row_count, channels, col_count), bf16),
        (grad, lat, cot, stats, totals),
        flops=lat.size * 20,
        moved=10 * lat.size,
        limit=12 << 20,
    )

    block_out = block_out[None].transpose(0, 1, 3, 2)
    latent_grad = latent_grad[None].transpose(0, 1, 3, 2)
    return (block_out, latent_grad, weight_grad, time_grad)


def solution(mesh):
    return jax.shard_map(
        slab_program,
        mesh=mesh,
        in_specs=(
            P("dp", "space", None, None),
            P("dp"),
            P(),
            P(),
            P(),
            P(),
            P(),
            P("dp", "space", None, None),
        ),
        out_specs=(P("dp", "space", None, None), P("dp", "space", None, None), P(), P()),
        check_vma=False,
    )
```

```python
import functools
import math

import jax
import jax.numpy as jnp
from jax import lax
from jax.experimental import pallas as pl
from jax.experimental.pallas import tpu as pltpu
from jax.sharding import PartitionSpec as P


GROUPS = 32
epsilon = 1e-05
f32 = jnp.float32
bf16 = jnp.bfloat16
f16 = jnp.float16
LANES = 128
NOTE = 32


def contract(a, b, dims, precision=None):
    return lax.dot_general(a, b, (dims, ((), ())), preferred_element_type=f32, precision=precision)


def spot(bits):
    image, slab = lax.axis_index("dp"), lax.axis_index("space")
    core = lax.rem(slab, 2)

    def index(which):
        found = 0
        for step in range(bits):
            shift = jnp.where(which == 0, step, bits - 1 - step)
            found = found * 2 + (lax.shift_right_logical(image, shift) & 1)
        return found

    return core, index(core), index(1 - core), lax.shift_right_logical(slab, 1)


def call(body, outs, args, specs=None, scratch=(), flops=0, moved=0, limit=40 << 20):
    vmem = pl.BlockSpec(memory_space=pltpu.VMEM)
    many = isinstance(outs, (list, tuple))
    return pl.pallas_call(
        body,
        out_shape=tuple(outs) if many else outs,
        in_specs=list(specs) if specs else [vmem] * len(args),
        out_specs=tuple([vmem] * len(outs)) if many else vmem,
        scratch_shapes=list(scratch),
        compiler_params=pltpu.CompilerParams(vmem_limit_bytes=limit),
        cost_estimate=pl.CostEstimate(flops=flops, bytes_accessed=moved, transcendentals=0),
    )(*args)


def group_sums(*columns):
    channels = columns[0].shape[0]
    per_group = channels // GROUPS
    row = lax.broadcasted_iota(jnp.int32, (channels, channels), 0).astype(f32)
    col = lax.broadcasted_iota(jnp.int32, (channels, channels), 1).astype(f32)
    same = jnp.floor((row + 0.5) / per_group) == jnp.floor((col + 0.5) / per_group)
    member = jnp.where(same, 1.0, 0.0).astype(bf16)
    lane = lax.broadcasted_iota(jnp.int32, (channels, LANES), 1)
    cells = jnp.zeros((channels, LANES), f32)
    for number, column in enumerate(columns):
        rest = column
        for part in range(3):
            taken = rest.astype(bf16).astype(f32)
            cells = jnp.where(lane == 3 * number + part, taken, cells)
            rest = rest - taken
    found = contract(member, cells.astype(bf16), ((1,), (0,)))
    pick = [found[:, i : i + 1] for i in range(3 * len(columns))]
    return [pick[3 * i] + pick[3 * i + 1] + pick[3 * i + 2] for i in range(len(columns))]


def as_rows(*columns):
    channels = columns[0].shape[0]
    lane = lax.broadcasted_iota(jnp.int32, (channels, LANES), 1)
    cells = jnp.zeros((channels, LANES), f32)
    for number, column in enumerate(columns):
        cells = jnp.where(lane == number, column, cells)
    return cells.T[:8]


def lane_sum(cells):
    return jnp.sum(cells, axis=1, keepdims=True)


def rows_of(*rows):
    height = lax.broadcasted_iota(jnp.int32, rows[0].shape, 0)
    packed = jnp.zeros(rows[0].shape, f32)
    for number, row in enumerate(rows):
        packed = jnp.where(height == number, row, packed)
    return packed


def fold_lanes(cells):
    total = cells[:, :LANES]
    for start in range(LANES, cells.shape[1], LANES):
        total = total + cells[:, start : start + LANES]
    return total


def stats_body(count, latent_hbm, cot_hbm, out_ref, latent_ref, cot_ref, sem):
    row_count, channels, cols = latent_ref.shape
    loads = []
    for number, (source, target) in enumerate(((latent_hbm, latent_ref), (cot_hbm, cot_ref))):
        for row in range(row_count):
            load = pltpu.make_async_copy(source.at[row], target.at[row], sem.at[number, row])
            load.start()
            loads.append(load)
    ones = jnp.ones((cols, LANES), bf16)
    sums = jnp.zeros((channels, LANES), f32)
    for row in range(row_count):
        loads[row].wait()
        sums = sums + contract(latent_ref[row], ones, ((1,), (0,)))
    mean = group_sums(sums[:, :1])[0] / count
    squares = jnp.zeros((channels, LANES), f32)
    for row in range(row_count):
        centered = latent_ref[row].astype(f32) - mean
        squares = squares + fold_lanes(centered * centered)
    grouped = group_sums(lane_sum(squares))[0]
    top = jnp.zeros((channels, LANES), bf16)
    for row in range(row_count):
        loads[row_count + row].wait()
        size = jnp.abs(cot_ref[row])
        for start in range(0, cols, LANES):
            top = jnp.maximum(top, size[:, start : start + LANES])
    largest = jnp.max(top.astype(f32), axis=(0, 1), keepdims=True)
    out_ref[...] = as_rows(mean, grouped, jnp.broadcast_to(largest, mean.shape))


def tree_sum(parts):
    while len(parts) > 1:
        parts = [parts[i] + parts[i + 1] for i in range(0, len(parts), 2)]
    return parts[0]


def merge_body(count, total, *refs):
    parts, out_ref = [ref[...] for ref in refs[:-1]], refs[-1]
    mean = tree_sum([part[0:1] for part in parts]) / len(parts)
    squares = tree_sum([part[1:2] + count * (part[0:1] - mean) ** 2 for part in parts])
    if total:
        squares = lax.rsqrt(squares / total + epsilon)
    largest = functools.reduce(jnp.maximum, [part[2:3] for part in parts])
    rows = (mean, squares, largest)
    out_ref[...] = rows_of(*[jnp.broadcast_to(row, out_ref.shape) for row in rows])


def column_values(stats_ref, gain_ref, bias_ref):
    channels = gain_ref.shape[0]
    shape = (8, channels)
    table = rows_of(
        jnp.broadcast_to(stats_ref[0:1], shape),
        jnp.broadcast_to(stats_ref[1:2], shape),
        jnp.broadcast_to(gain_ref[...], shape),
        jnp.broadcast_to(bias_ref[...], shape),
    ).T
    return [table[:, i : i + 1] for i in range(4)]


def normalized(cells, values):
    mean, inverse, gain, bias = values
    normed = (cells.astype(f32) - mean) * inverse
    shifted = normed * gain + bias
    return normed, shifted, jax.nn.sigmoid(shifted)


def activate(cells, values):
    _, shifted, sigmoid = normalized(cells, values)
    return (shifted * sigmoid).astype(bf16)


def shifted_cols(cells):
    cols = cells.shape[1]
    lane = lax.broadcasted_iota(jnp.int32, cells.shape, 1)
    zero = jnp.zeros_like(cells)
    after = jnp.where(lane == cols - 1, zero, pltpu.roll(cells, cols - 1, 1))
    before = jnp.where(lane == 0, zero, pltpu.roll(cells, 1, 1))
    return after, before


def put_taps(buffer_ref, place, cells, flip):
    channels, cols = cells.shape
    wide = cells.astype(f32)
    after, before = shifted_cols(wide)
    order = (after, cells, before) if flip else (before, cells, after)
    start = place * cols if isinstance(place, int) else pl.multiple_of(place * cols, LANES)
    for tap, piece in enumerate(order):
        buffer_ref[tap * channels : (tap + 1) * channels, pl.ds(start, cols)] = piece.astype(bf16)


def taps_body(cot_ref, taps_ref, sums_ref):
    row_count, channels, cols = cot_ref.shape
    tall = jnp.ones((8, cols), bf16)
    sums = jnp.zeros((8, channels), f32)
    for row in range(row_count):
        put_taps(taps_ref, row, cot_ref[row], True)
        sums = sums + contract(tall, cot_ref[row], ((1,), (1,)))
    sums_ref[...] = sums


def middle_body(
    factor, spread, latent_ref, taps_ref, stats_ref, gain_ref, bias_ref, sums_ref, step_ref,
    act_ref, found_ref, table_ref,
):
    row_count, channels, cols = latent_ref.shape
    table_ref[...] = jnp.zeros(table_ref.shape, f32)
    table_ref[0:1, :channels] = sums_ref[0:1]
    table_ref[0:1, channels : channels + NOTE] = jnp.broadcast_to(step_ref[...], (1, NOTE))
    gain = jnp.max(jnp.abs(gain_ref[...][None, :]), axis=1, keepdims=True)
    bias = jnp.max(jnp.abs(bias_ref[...][None, :]), axis=1, keepdims=True)
    bound = stats_ref[2:3] * ((spread * gain + bias) * factor)
    table_ref[0:1, channels + NOTE : channels + 2 * NOTE] = bound[:, :NOTE]
    values = column_values(stats_ref, gain_ref, bias_ref)
    for row in range(row_count):
        act_ref[:, row * cols : (row + 1) * cols] = activate(latent_ref[row], values)
    found_ref[...] = contract(act_ref[...], taps_ref[...], ((1,), (1,)))


def weight_body(
    shape, cols, act_ref, taps_ref, outer_ref, inner_ref, middle_ref,
    near_ref, low_ref, high_ref, edge_ref,
):
    blocks, zones, height, width = shape
    channels, positions = act_ref.shape
    core, mine, other, zone_index = spot((blocks // 2).bit_length() - 1)
    quarter = blocks // 4
    put_taps(edge_ref, core, outer_ref[...], True)
    put_taps(edge_ref, 1 - core, inner_ref[...], True)
    tap_width = zones * width // 3

    def store(ref, place, found, block, tap_row):
        first = block * height
        size = max(min(height, channels - first), 0)
        for zone in range(zones):
            low = max(zone * width, tap_row * tap_width)
            high = min((zone + 1) * width, (tap_row + 1) * tap_width)
            if low >= high:
                continue
            at = zone_index ^ zone
            left, right = low - zone * width, high - zone * width
            source = low - tap_row * tap_width
            used = max(min(right - left, 3 * channels - source), 0)
            if size and used:
                ref[place, at, :size, left : left + used] = found[
                    first : first + size, source : source + used
                ]
            if used < right - left:
                ref[place, at, :, left + used : right] = jnp.zeros(
                    (height, right - left - used), f32
                )
            if size < height and used:
                ref[place, at, size:, left : left + used] = jnp.zeros((height - size, used), f32)

    for tap_row in (1, 0, 2):
        if tap_row == 1:
            found = middle_ref
        else:
            inner = slice(0, positions - cols) if tap_row == 0 else slice(cols, positions)
            shifted = slice(cols, positions) if tap_row == 0 else slice(0, positions - cols)
            outer = slice(positions - cols, positions) if tap_row == 0 else slice(0, cols)
            edge = slice(cols, 2 * cols) if tap_row == 0 else slice(0, cols)
            found = contract(act_ref[:, inner], taps_ref[:, shifted], ((1,), (1,)))
            found = found + contract(act_ref[:, outer], edge_ref[:, edge], ((1,), (1,)))
        for half in range(2):

            @pl.when(core == half)
            def _():
                for rest in range(blocks // 2):
                    store(near_ref, mine ^ rest, found, half * blocks // 2 + rest, tap_row)

            for top in range(2):

                @pl.when((core != half) & (other // quarter == top))
                def _():
                    for rest in range(blocks // 2):
                        ref = high_ref if rest // quarter != top else low_ref
                        at = (other ^ rest) % quarter
                        store(ref, at, found, half * blocks // 2 + rest, tap_row)


def conv_body(
    act_ref, latent_ref, outer_ref, inner_ref, stats_ref, gain_ref, bias_ref, weight_ref,
    extra_ref, out_ref, taps_ref, flat_ref,
):
    row_count, channels, cols = latent_ref.shape
    values = column_values(stats_ref, gain_ref, bias_ref)
    slab, last = lax.axis_index("space"), lax.axis_size("space") - 1
    core = lax.rem(slab, 2)
    keep = jnp.where((slab == 0) | (slab == last), 0.0, 1.0).astype(f32)
    outer = (activate(outer_ref[...], values).astype(f32) * keep).astype(bf16)
    put_taps(taps_ref, core * (row_count + 1), outer, False)
    put_taps(taps_ref, (1 - core) * (row_count + 1), activate(inner_ref[...], values), False)
    for row in range(row_count):
        put_taps(taps_ref, row + 1, act_ref[:, row * cols : (row + 1) * cols], False)
    for tap_row in range(3):
        flat_ref[tap_row] = weight_ref[tap_row].reshape(3 * channels, channels).T
    extra = jnp.broadcast_to(extra_ref[...], (8, channels)).T[:, :1]
    for row in range(row_count):
        total = latent_ref[row].astype(f32) + extra
        for tap_row in range(3):
            start = (row + tap_row) * cols
            total = total + contract(
                flat_ref[tap_row], taps_ref[:, start : start + cols], ((1,), (0,))
            )
        out_ref[row] = total.astype(bf16)


def backward_body(
    latent_ref, taps_ref, edge_ref, stats_ref, gain_ref, bias_ref, weight_ref,
    grad_ref, sums_ref, flat_ref,
):
    row_count, channels, cols = latent_ref.shape
    values = column_values(stats_ref, gain_ref, bias_ref)
    for tap_row in range(3):
        flat_ref[tap_row] = jnp.concatenate([weight_ref[tap_row, j] for j in range(3)], axis=1)
    first = jnp.zeros((channels, LANES), f32)
    second = jnp.zeros((channels, LANES), f32)
    for row in range(row_count):
        total = jnp.zeros((channels, cols), f32)
        for tap_row in range(3):
            source = row + 1 - tap_row
            if 0 <= source < row_count:
                piece = taps_ref[:, source * cols : (source + 1) * cols]
            else:
                start = cols if source > 0 else 0
                piece = edge_ref[:, start : start + cols]
            total = total + contract(flat_ref[tap_row], piece, ((1,), (0,)))
        normed, shifted, sigmoid = normalized(latent_ref[row], values)
        grad = total * sigmoid * (1.0 + shifted * (1.0 - sigmoid)) * values[2]
        grad_ref[row] = grad
        first = first + fold_lanes(grad)
        second = second + fold_lanes(grad * normed)
    sums_ref[...] = as_rows(*group_sums(lane_sum(first), lane_sum(second)))


def latent_body(total, grad_ref, latent_ref, cot_ref, stats_ref, sums_ref, out_ref):
    row_count, channels, _ = latent_ref.shape
    sums = sums_ref[0:2] / total
    shape = (8, channels)
    table = rows_of(
        *[
            jnp.broadcast_to(row, shape)
            for row in (stats_ref[0:1], stats_ref[1:2], sums[0:1], sums[1:2])
        ]
    ).T
    mean, inverse, first, second = [table[:, i : i + 1] for i in range(4)]
    for row in range(row_count):
        normed = (latent_ref[row].astype(f32) - mean) * inverse
        change = inverse * (grad_ref[row] - first - normed * second)
        out_ref[row] = (cot_ref[row].astype(f32) + change).astype(bf16)


def place_body(shape, half_blocks, pieces, *refs):
    zones, height, width = shape
    count = len(pieces)
    cells = refs[:count]
    core, mine, other, zone_index = spot(half_blocks.bit_length() - 1)
    spots = [
        (1 - core) * half_blocks + (other ^ rest) if crossed else core * half_blocks + (mine ^ rest)
        for crossed, rest in pieces
    ]
    out_ref, flat_ref, rows_ref, sem = refs[-4:]
    channels = out_ref.shape[1]
    tap_width = zones * width // 3
    whole, part = channels // height, channels % height

    def copies(index, act):
        block = spots[index]

        def copy(size):
            return pltpu.make_async_copy(
                rows_ref.at[index, :, pl.ds(0, size)],
                out_ref.at[:, pl.ds(pl.multiple_of(block * height, 8), size)],
                sem.at[index],
            )

        @pl.when(block < whole)
        def _():
            act(copy(height))

        if part:

            @pl.when(block == whole)
            def _():
                act(copy(part))

    for index in range(count):
        for zone in range(zones):
            left = pl.multiple_of((zone_index ^ zone) * width, LANES)
            flat_ref[index, :, pl.ds(left, width)] = cells[index][zone]
        for tap in range(9):
            left = (tap // 3) * tap_width + (tap % 3) * channels
            rows_ref[index, tap] = flat_ref[index, :, left : left + channels]
        copies(index, lambda copy: copy.start())
    for index in range(count):
        copies(index, lambda copy: copy.wait())


def spread_body(
    known, masks, mine_ref, other_ref, table_ref, scale_ref, back_ref, steps_ref
):
    channels = steps_ref.shape[1]
    table_ref[...] = mine_ref[...]
    for core in range(2):

        @pl.when(lax.rem(lax.axis_index("space"), 2) == core)
        def _():
            for row in known[core]:
                at = row ^ masks[core]
                table_ref[at : at + 1] = other_ref[row : row + 1]

    table = table_ref[...]
    bound = jnp.max(table[:, channels + NOTE : channels + NOTE + 1], axis=0, keepdims=True)
    bound = jnp.maximum(bound, 1e-25) * (1.0 / 30000.0)
    back_ref[...] = bound
    scale_ref[...] = 1.0 / bound
    steps_ref[...] = jnp.broadcast_to(table[:, channels : channels + 1], steps_ref.shape)


def gather_body(images, sums_ref, table_ref, out_ref):
    channels = sums_ref.shape[1]
    rows = [sums_ref[0:1], sums_ref[1:2]]
    rows += [table_ref[i : i + 1, :channels] for i in range(images)]
    out_ref[...] = rows_of(*[jnp.broadcast_to(row, out_ref.shape) for row in rows])


def total_body(*refs):
    refs[-1][...] = tree_sum([ref[...] for ref in refs[:-1]])


def time_body(count, embed_ref, total_ref, out_ref):
    columns = embed_ref[...].T
    terms = [columns[:, i : i + 1] * total_ref[2 + i : 3 + i] for i in range(count)]
    out_ref[...] = tree_sum(terms)


def swap_space(cells, mask):
    count = lax.axis_size("space")
    return lax.ppermute(cells, "space", [(i, i ^ mask) for i in range(count)])


def swap_image(cells, masks):
    images = lax.axis_size("dp")
    count = lax.axis_size("space")
    pairs = [
        (i * count + j, (i ^ masks[j % 2]) * count + j) for i in range(images) for j in range(count)
    ]
    return lax.ppermute(cells, ("dp", "space"), pairs)


def slab_program(
    latent, timesteps, norm_gain, norm_bias, conv_weight, conv_bias, time_weight, cotangent
):
    images, row_count, col_count, channels = latent.shape
    assert images == 1
    per_group = channels // GROUPS
    image_count = lax.axis_size("dp")
    slab_count = lax.axis_size("space")
    zones = slab_count // 2
    bits = image_count.bit_length() - 1
    blocks = 2 * image_count
    height = -(-channels // (8 * blocks)) * 8
    tap_width = -(-3 * channels // LANES) * LANES
    width = 3 * tap_width // zones
    local_count = row_count * col_count * per_group
    total_count = local_count * slab_count
    positions = row_count * col_count

    slab_index = lax.axis_index("space")
    core = slab_index % 2

    lat = latent.transpose(0, 1, 3, 2)[0]
    cot = cotangent.transpose(0, 1, 3, 2)[0]
    gain, bias = norm_gain, norm_bias
    vmem = pl.BlockSpec(memory_space=pltpu.VMEM)
    anywhere = pl.BlockSpec(memory_space=pl.ANY)
    small = jax.ShapeDtypeStruct((8, channels), f32)

    flops = 2 * positions * channels * channels * 9
    taps = pltpu.VMEM((3 * channels, (row_count + 2) * col_count), bf16)
    flat = pltpu.VMEM((3, channels, 3 * channels), bf16)

    slab = pltpu.VMEM((row_count, channels, col_count), bf16)
    own = call(
        functools.partial(stats_body, local_count),
        small,
        (lat, cot),
        specs=(anywhere, anywhere),
        scratch=(slab, slab, pltpu.SemaphoreType.DMA((2, row_count))),
        moved=2 * lat.size * 2,
        flops=positions * channels * 60,
        limit=60 << 20,
    )
    partner = swap_space(own, 1)
    pair = call(
        functools.partial(merge_body, local_count, None), small, (own, partner), limit=4 << 20
    )
    parts = [pair]
    for mask in range(1, zones):
        parts.append(swap_space(pair, 2 * mask))
    far_row = jnp.where(core == 0, 0, row_count - 1)
    between = [(i, i - 1 if i % 2 == 0 else i + 1) for i in range(1, slab_count - 1)]

    def edges(cells):
        outward = lax.dynamic_index_in_dim(cells, far_row, 0, keepdims=False)
        inward = lax.dynamic_index_in_dim(cells, row_count - 1 - far_row, 0, keepdims=False)
        outer = lax.ppermute(outward, "space", between)
        return outer, swap_space(inward, 1)

    outer, inner = edges(cot)
    lat_outer, lat_inner = edges(lat)
    stats = call(
        functools.partial(merge_body, 2 * local_count, total_count),
        small,
        tuple(parts),
        limit=4 << 20,
    )

    orders = [list(range(bits)), list(range(bits))[::-1]]

    part_shape = jax.ShapeDtypeStruct((blocks // 4, zones, height, width), f32)
    share_shape = jax.ShapeDtypeStruct((blocks // 2, zones, height, width), f32)
    taps_shape = jax.ShapeDtypeStruct((3 * channels, positions), bf16)
    grad_taps, col_sums = call(
        taps_body, (taps_shape, small), (cot,), moved=10 * lat.size, limit=6 << 20
    )
    table_shape = jax.ShapeDtypeStruct((-(-image_count // 8) * 8, channels + 2 * NOTE), f32)
    factor, spread = float(positions * slab_count * image_count), math.sqrt(per_group)
    act, middle_rows, table = call(
        functools.partial(middle_body, factor, spread),
        (
            jax.ShapeDtypeStruct((channels, positions), bf16),
            jax.ShapeDtypeStruct((channels, 3 * channels), f32),
            table_shape,
        ),
        (lat, grad_taps, stats, gain, bias, col_sums, timesteps.astype(f32).reshape(1, 1)),
        flops=flops // 3,
        moved=8 * lat.size,
        limit=8 << 20,
    )
    near, far_low, far_high, edge_taps = call(
        functools.partial(weight_body, (blocks, zones, height, width), col_count),
        (
            share_shape,
            part_shape,
            part_shape,
            jax.ShapeDtypeStruct((3 * channels, 2 * col_count), bf16),
        ),
        (act, grad_taps, outer, inner, middle_rows),
        flops=flops,
        moved=8 * lat.size,
        limit=12 << 20,
    )
    unit = jax.ShapeDtypeStruct((1, 1), f32)
    steps_shape = jax.ShapeDtypeStruct((table_shape.shape[0], channels), f32)
    known = ([0], [0])
    scales = []
    for step in range(bits):
        masks = (1 << orders[0][step], 1 << orders[1][step])
        arrived = swap_image(table, masks)
        table, scale, back, steps = call(
            functools.partial(spread_body, known, masks),
            (table_shape, unit, unit, steps_shape),
            (table, arrived),
            limit=4 << 20,
        )
        scales.append((scale[0, 0], back[0, 0]))
        known = tuple(rows + [row ^ mask for row in rows] for rows, mask in zip(known, masks))

    grad, sums = call(
        backward_body,
        (jax.ShapeDtypeStruct((row_count, channels, col_count), f32), small),
        (lat, grad_taps, edge_taps, stats, gain, bias, conv_weight),
        scratch=(flat,),
        flops=flops,
        moved=8 * lat.size,
        limit=8 << 20,
    )
    message = jax.ShapeDtypeStruct((-(-(2 + image_count) // 8) * 8, channels), f32)
    gathered = call(
        functools.partial(gather_body, image_count), message, (sums, table), limit=4 << 20
    )
    gathered = [gathered + swap_space(gathered, 1)]
    for mask in range(1, zones):
        gathered.append(swap_space(gathered[0], 2 * mask))
    totals = call(total_body, message, tuple(gathered), limit=4 << 20)
    line_scale, line_back = scales[-1]

    middle = blocks // 4
    far_in = swap_space(far_high, 1)
    near_in = swap_space(far_low, 1)
    sent = ((near[middle:] + far_in) * scales[0][0]).astype(f16)
    near, near_in, _ = lax.optimization_barrier((near, near_in, sent))
    keeping = near[:middle] + near_in
    for step in range(bits):
        masks = (1 << orders[0][step], 1 << orders[1][step])
        arrived = swap_image(sent, masks)
        back = scales[step][1]
        middle = keeping.shape[0] // 2
        if middle:
            total = keeping[middle:] + arrived[middle:].astype(f32) * back
            sent = (total * scales[step + 1][0]).astype(f16)
            keeping, arrived, _ = lax.optimization_barrier((keeping, arrived, sent))
            keeping = keeping[:middle] + arrived[:middle].astype(f32) * back
    sent = []
    for mask in range(1, zones):
        total = keeping[0, mask] + arrived[0, mask].astype(f32) * back
        sent.append((total * line_scale).astype(f16))
    keeping, arrived, *_ = lax.optimization_barrier((keeping, arrived, *sent))
    share = keeping[0, 0] + arrived[0, 0].astype(f32) * back
    for mask in range(1, zones):
        share = share + swap_space(sent[mask - 1], 2 * mask).astype(f32) * line_back
    share = (share * line_scale).astype(f16)
    collected = [share]
    for mask in range(1, zones):
        collected.append(swap_space(share, 2 * mask))
    pieces = [jnp.stack(collected)]
    for step in reversed(range(bits)):
        masks = (1 << orders[0][step], 1 << orders[1][step])
        arrived = []
        for piece in pieces:
            arrived.append(swap_image(piece, masks))
        pieces = pieces + arrived
    crossed = []
    for piece in pieces:
        crossed.append(swap_space(piece, 1))
    half_blocks = blocks // 2
    numbers = list(range(half_blocks))

    def place(chosen, before):
        count = len(chosen)
        cells = []
        for is_crossed, rest in chosen:
            piece = crossed[rest] if is_crossed else pieces[rest]
            cells.append(piece.astype(f32) * line_back)
        return pl.pallas_call(
            functools.partial(place_body, (zones, height, width), half_blocks, chosen),
            out_shape=jax.ShapeDtypeStruct((9, channels, channels), f32),
            in_specs=[vmem] * count + [anywhere] * len(before),
            out_specs=anywhere,
            scratch_shapes=[
                pltpu.VMEM((count, height, zones * width), f32),
                pltpu.VMEM((count, 9, height, channels), f32),
                pltpu.SemaphoreType.DMA((count,)),
            ],
            input_output_aliases={count: 0} if before else {},
            compiler_params=pltpu.CompilerParams(vmem_limit_bytes=12 << 20),
            cost_estimate=pl.CostEstimate(
                flops=0,
                bytes_accessed=8 * count * zones * height * width,
                transcendentals=0,
            ),
        )(*cells, *before)

    early = [(side, rest) for side in (False, True) for rest in numbers[:-1]]
    weight_grad = place(early, ())
    weight_grad = place([(False, numbers[-1]), (True, numbers[-1])], (weight_grad,))
    weight_grad = weight_grad.reshape(3, 3, channels, channels)

    half_count = channels // 2
    frequency = jnp.exp(-math.log(10000.0) * jnp.arange(half_count, dtype=f32) / half_count)
    angles = steps[:, :half_count] * frequency[None, :]
    embedding = jnp.concatenate([jnp.cos(angles), jnp.sin(angles)], axis=1).astype(bf16)
    time_bias = jnp.dot(embedding[:1], time_weight, preferred_element_type=f32)
    extra = time_bias + conv_bias.reshape(1, channels)
    time_grad = call(
        functools.partial(time_body, image_count),
        jax.ShapeDtypeStruct((channels, channels), f32),
        (embedding.astype(f32), totals),
        limit=4 << 20,
    )
    block_out = call(
        conv_body,
        jax.ShapeDtypeStruct((row_count, channels, col_count), bf16),
        (act, lat, lat_outer, lat_inner, stats, gain, bias, conv_weight, extra),
        scratch=(taps, flat),
        flops=flops,
        moved=8 * lat.size,
        limit=14 << 20,
    )
    latent_grad = call(
        functools.partial(latent_body, total_count),
        jax.ShapeDtypeStruct((row_count, channels, col_count), bf16),
        (grad, lat, cot, stats, totals),
        flops=lat.size * 20,
        moved=10 * lat.size,
        limit=12 << 20,
    )

    block_out = block_out[None].transpose(0, 1, 3, 2)
    latent_grad = latent_grad[None].transpose(0, 1, 3, 2)
    return (block_out, latent_grad, weight_grad, time_grad)


def solution(mesh):
    return jax.shard_map(
        slab_program,
        mesh=mesh,
        in_specs=(
            P("dp", "space", None, None),
            P("dp"),
            P(),
            P(),
            P(),
            P(),
            P(),
            P("dp", "space", None, None),
        ),
        out_specs=(P("dp", "space", None, None), P("dp", "space", None, None), P(), P()),
        check_vma=False,
    )
```

```python
import functools
import math

import jax
import jax.numpy as jnp
from jax import lax
from jax.experimental import pallas as pl
from jax.experimental.pallas import tpu as pltpu
from jax.sharding import PartitionSpec as P


GROUPS = 32
epsilon = 1e-05
f32 = jnp.float32
bf16 = jnp.bfloat16
f16 = jnp.float16
LANES = 128
NOTE = 32


def contract(a, b, dims, precision=None):
    return lax.dot_general(a, b, (dims, ((), ())), preferred_element_type=f32, precision=precision)


def spot(bits):
    image, slab = lax.axis_index("dp"), lax.axis_index("space")
    core = lax.rem(slab, 2)

    def index(which):
        found = 0
        for step in range(bits):
            shift = jnp.where(which == 0, step, bits - 1 - step)
            found = found * 2 + (lax.shift_right_logical(image, shift) & 1)
        return found

    return core, index(core), index(1 - core), lax.shift_right_logical(slab, 1)


def call(body, outs, args, specs=None, scratch=(), flops=0, moved=0, limit=40 << 20):
    vmem = pl.BlockSpec(memory_space=pltpu.VMEM)
    many = isinstance(outs, (list, tuple))
    return pl.pallas_call(
        body,
        out_shape=tuple(outs) if many else outs,
        in_specs=list(specs) if specs else [vmem] * len(args),
        out_specs=tuple([vmem] * len(outs)) if many else vmem,
        scratch_shapes=list(scratch),
        compiler_params=pltpu.CompilerParams(vmem_limit_bytes=limit),
        cost_estimate=pl.CostEstimate(flops=flops, bytes_accessed=moved, transcendentals=0),
    )(*args)


def group_sums(*columns):
    channels = columns[0].shape[0]
    per_group = channels // GROUPS
    row = lax.broadcasted_iota(jnp.int32, (channels, channels), 0).astype(f32)
    col = lax.broadcasted_iota(jnp.int32, (channels, channels), 1).astype(f32)
    same = jnp.floor((row + 0.5) / per_group) == jnp.floor((col + 0.5) / per_group)
    member = jnp.where(same, 1.0, 0.0).astype(bf16)
    lane = lax.broadcasted_iota(jnp.int32, (channels, LANES), 1)
    cells = jnp.zeros((channels, LANES), f32)
    for number, column in enumerate(columns):
        rest = column
        for part in range(3):
            taken = rest.astype(bf16).astype(f32)
            cells = jnp.where(lane == 3 * number + part, taken, cells)
            rest = rest - taken
    found = contract(member, cells.astype(bf16), ((1,), (0,)))
    pick = [found[:, i : i + 1] for i in range(3 * len(columns))]
    return [pick[3 * i] + pick[3 * i + 1] + pick[3 * i + 2] for i in range(len(columns))]


def as_rows(*columns):
    channels = columns[0].shape[0]
    lane = lax.broadcasted_iota(jnp.int32, (channels, LANES), 1)
    cells = jnp.zeros((channels, LANES), f32)
    for number, column in enumerate(columns):
        cells = jnp.where(lane == number, column, cells)
    return cells.T[:8]


def lane_sum(cells):
    return jnp.sum(cells, axis=1, keepdims=True)


def rows_of(*rows):
    height = lax.broadcasted_iota(jnp.int32, rows[0].shape, 0)
    packed = jnp.zeros(rows[0].shape, f32)
    for number, row in enumerate(rows):
        packed = jnp.where(height == number, row, packed)
    return packed


def fold_lanes(cells):
    total = cells[:, :LANES]
    for start in range(LANES, cells.shape[1], LANES):
        total = total + cells[:, start : start + LANES]
    return total


def stats_body(count, latent_hbm, cot_hbm, out_ref, latent_ref, cot_ref, sem):
    row_count, channels, cols = latent_ref.shape
    loads = []
    for number, (source, target) in enumerate(((latent_hbm, latent_ref), (cot_hbm, cot_ref))):
        for row in range(row_count):
            load = pltpu.make_async_copy(source.at[row], target.at[row], sem.at[number, row])
            load.start()
            loads.append(load)
    ones = jnp.ones((cols, LANES), bf16)
    sums = jnp.zeros((channels, LANES), f32)
    for row in range(row_count):
        loads[row].wait()
        sums = sums + contract(latent_ref[row], ones, ((1,), (0,)))
    mean = group_sums(sums[:, :1])[0] / count
    squares = jnp.zeros((channels, LANES), f32)
    for row in range(row_count):
        centered = latent_ref[row].astype(f32) - mean
        squares = squares + fold_lanes(centered * centered)
    grouped = group_sums(lane_sum(squares))[0]
    top = jnp.zeros((channels, LANES), bf16)
    for row in range(row_count):
        loads[row_count + row].wait()
        size = jnp.abs(cot_ref[row])
        for start in range(0, cols, LANES):
            top = jnp.maximum(top, size[:, start : start + LANES])
    largest = jnp.max(top.astype(f32), axis=(0, 1), keepdims=True)
    out_ref[...] = as_rows(mean, grouped, jnp.broadcast_to(largest, mean.shape))


def tree_sum(parts):
    while len(parts) > 1:
        parts = [parts[i] + parts[i + 1] for i in range(0, len(parts), 2)]
    return parts[0]


def merge_body(count, total, *refs):
    parts, out_ref = [ref[...] for ref in refs[:-1]], refs[-1]
    mean = tree_sum([part[0:1] for part in parts]) / len(parts)
    squares = tree_sum([part[1:2] + count * (part[0:1] - mean) ** 2 for part in parts])
    if total:
        squares = lax.rsqrt(squares / total + epsilon)
    largest = functools.reduce(jnp.maximum, [part[2:3] for part in parts])
    rows = (mean, squares, largest)
    out_ref[...] = rows_of(*[jnp.broadcast_to(row, out_ref.shape) for row in rows])


def column_values(stats_ref, gain_ref, bias_ref):
    channels = gain_ref.shape[0]
    shape = (8, channels)
    table = rows_of(
        jnp.broadcast_to(stats_ref[0:1], shape),
        jnp.broadcast_to(stats_ref[1:2], shape),
        jnp.broadcast_to(gain_ref[...], shape),
        jnp.broadcast_to(bias_ref[...], shape),
    ).T
    return [table[:, i : i + 1] for i in range(4)]


def normalized(cells, values):
    mean, inverse, gain, bias = values
    normed = (cells.astype(f32) - mean) * inverse
    shifted = normed * gain + bias
    return normed, shifted, jax.nn.sigmoid(shifted)


def activate(cells, values):
    _, shifted, sigmoid = normalized(cells, values)
    return (shifted * sigmoid).astype(bf16)


def shifted_cols(cells):
    cols = cells.shape[1]
    lane = lax.broadcasted_iota(jnp.int32, cells.shape, 1)
    zero = jnp.zeros_like(cells)
    after = jnp.where(lane == cols - 1, zero, pltpu.roll(cells, cols - 1, 1))
    before = jnp.where(lane == 0, zero, pltpu.roll(cells, 1, 1))
    return after, before


def put_taps(buffer_ref, place, cells, flip):
    channels, cols = cells.shape
    wide = cells.astype(f32)
    after, before = shifted_cols(wide)
    order = (after, cells, before) if flip else (before, cells, after)
    start = place * cols if isinstance(place, int) else pl.multiple_of(place * cols, LANES)
    for tap, piece in enumerate(order):
        buffer_ref[tap * channels : (tap + 1) * channels, pl.ds(start, cols)] = piece.astype(bf16)


def taps_body(cot_ref, taps_ref, sums_ref):
    row_count, channels, cols = cot_ref.shape
    tall = jnp.ones((8, cols), bf16)
    sums = jnp.zeros((8, channels), f32)
    for row in range(row_count):
        put_taps(taps_ref, row, cot_ref[row], True)
        sums = sums + contract(tall, cot_ref[row], ((1,), (1,)))
    sums_ref[...] = sums


def middle_body(
    factor, spread, latent_ref, taps_ref, stats_ref, gain_ref, bias_ref, sums_ref, step_ref,
    act_ref, found_ref, table_ref,
):
    row_count, channels, cols = latent_ref.shape
    table_ref[...] = jnp.zeros(table_ref.shape, f32)
    table_ref[0:1, :channels] = sums_ref[0:1]
    table_ref[0:1, channels : channels + NOTE] = jnp.broadcast_to(step_ref[...], (1, NOTE))
    gain = jnp.max(jnp.abs(gain_ref[...][None, :]), axis=1, keepdims=True)
    bias = jnp.max(jnp.abs(bias_ref[...][None, :]), axis=1, keepdims=True)
    bound = stats_ref[2:3] * ((spread * gain + bias) * factor)
    table_ref[0:1, channels + NOTE : channels + 2 * NOTE] = bound[:, :NOTE]
    values = column_values(stats_ref, gain_ref, bias_ref)
    for row in range(row_count):
        act_ref[:, row * cols : (row + 1) * cols] = activate(latent_ref[row], values)
    found_ref[...] = contract(act_ref[...], taps_ref[...], ((1,), (1,)))


def weight_body(
    shape, cols, act_ref, taps_ref, outer_ref, inner_ref, middle_ref,
    near_ref, low_ref, high_ref, edge_ref,
):
    blocks, zones, height, width = shape
    channels, positions = act_ref.shape
    core, mine, other, zone_index = spot((blocks // 2).bit_length() - 1)
    quarter = blocks // 4
    put_taps(edge_ref, core, outer_ref[...], True)
    put_taps(edge_ref, 1 - core, inner_ref[...], True)
    tap_width = zones * width // 3

    def store(ref, place, found, block, tap_row):
        first = block * height
        size = max(min(height, channels - first), 0)
        for zone in range(zones):
            low = max(zone * width, tap_row * tap_width)
            high = min((zone + 1) * width, (tap_row + 1) * tap_width)
            if low >= high:
                continue
            at = zone_index ^ zone
            left, right = low - zone * width, high - zone * width
            source = low - tap_row * tap_width
            used = max(min(right - left, 3 * channels - source), 0)
            if size and used:
                ref[place, at, :size, left : left + used] = found[
                    first : first + size, source : source + used
                ]
            if used < right - left:
                ref[place, at, :, left + used : right] = jnp.zeros(
                    (height, right - left - used), f32
                )
            if size < height and used:
                ref[place, at, size:, left : left + used] = jnp.zeros((height - size, used), f32)

    for tap_row in (1, 0, 2):
        if tap_row == 1:
            found = middle_ref
        else:
            inner = slice(0, positions - cols) if tap_row == 0 else slice(cols, positions)
            shifted = slice(cols, positions) if tap_row == 0 else slice(0, positions - cols)
            outer = slice(positions - cols, positions) if tap_row == 0 else slice(0, cols)
            edge = slice(cols, 2 * cols) if tap_row == 0 else slice(0, cols)
            found = contract(act_ref[:, inner], taps_ref[:, shifted], ((1,), (1,)))
            found = found + contract(act_ref[:, outer], edge_ref[:, edge], ((1,), (1,)))
        for half in range(2):

            @pl.when(core == half)
            def _():
                for rest in range(blocks // 2):
                    store(near_ref, mine ^ rest, found, half * blocks // 2 + rest, tap_row)

            for top in range(2):

                @pl.when((core != half) & (other // quarter == top))
                def _():
                    for rest in range(blocks // 2):
                        ref = high_ref if rest // quarter != top else low_ref
                        at = (other ^ rest) % quarter
                        store(ref, at, found, half * blocks // 2 + rest, tap_row)


def conv_body(
    act_ref, latent_ref, outer_ref, inner_ref, stats_ref, gain_ref, bias_ref, weight_ref,
    extra_ref, out_ref, taps_ref, flat_ref,
):
    row_count, channels, cols = latent_ref.shape
    values = column_values(stats_ref, gain_ref, bias_ref)
    slab, last = lax.axis_index("space"), lax.axis_size("space") - 1
    core = lax.rem(slab, 2)
    keep = jnp.where((slab == 0) | (slab == last), 0.0, 1.0).astype(f32)
    outer = (activate(outer_ref[...], values).astype(f32) * keep).astype(bf16)
    put_taps(taps_ref, core * (row_count + 1), outer, False)
    put_taps(taps_ref, (1 - core) * (row_count + 1), activate(inner_ref[...], values), False)
    for row in range(row_count):
        put_taps(taps_ref, row + 1, act_ref[:, row * cols : (row + 1) * cols], False)
    for tap_row in range(3):
        flat_ref[tap_row] = weight_ref[tap_row].reshape(3 * channels, channels).T
    extra = jnp.broadcast_to(extra_ref[...], (8, channels)).T[:, :1]
    for row in range(row_count):
        total = latent_ref[row].astype(f32) + extra
        for tap_row in range(3):
            start = (row + tap_row) * cols
            total = total + contract(
                flat_ref[tap_row], taps_ref[:, start : start + cols], ((1,), (0,))
            )
        out_ref[row] = total.astype(bf16)


def backward_body(
    latent_ref, taps_ref, edge_ref, stats_ref, gain_ref, bias_ref, weight_ref,
    grad_ref, sums_ref, flat_ref,
):
    row_count, channels, cols = latent_ref.shape
    values = column_values(stats_ref, gain_ref, bias_ref)
    for tap_row in range(3):
        flat_ref[tap_row] = jnp.concatenate([weight_ref[tap_row, j] for j in range(3)], axis=1)
    first = jnp.zeros((channels, LANES), f32)
    second = jnp.zeros((channels, LANES), f32)
    for row in range(row_count):
        total = jnp.zeros((channels, cols), f32)
        for tap_row in range(3):
            source = row + 1 - tap_row
            if 0 <= source < row_count:
                piece = taps_ref[:, source * cols : (source + 1) * cols]
            else:
                start = cols if source > 0 else 0
                piece = edge_ref[:, start : start + cols]
            total = total + contract(flat_ref[tap_row], piece, ((1,), (0,)))
        normed, shifted, sigmoid = normalized(latent_ref[row], values)
        grad = total * sigmoid * (1.0 + shifted * (1.0 - sigmoid)) * values[2]
        grad_ref[row] = grad
        first = first + fold_lanes(grad)
        second = second + fold_lanes(grad * normed)
    sums_ref[...] = as_rows(*group_sums(lane_sum(first), lane_sum(second)))


def latent_body(total, grad_ref, latent_ref, cot_ref, stats_ref, sums_ref, out_ref):
    row_count, channels, _ = latent_ref.shape
    sums = sums_ref[0:2] / total
    shape = (8, channels)
    table = rows_of(
        *[
            jnp.broadcast_to(row, shape)
            for row in (stats_ref[0:1], stats_ref[1:2], sums[0:1], sums[1:2])
        ]
    ).T
    mean, inverse, first, second = [table[:, i : i + 1] for i in range(4)]
    for row in range(row_count):
        normed = (latent_ref[row].astype(f32) - mean) * inverse
        change = inverse * (grad_ref[row] - first - normed * second)
        out_ref[row] = (cot_ref[row].astype(f32) + change).astype(bf16)


def place_body(shape, half_blocks, pieces, *refs):
    zones, height, width = shape
    count = len(pieces)
    cells = refs[:count]
    core, mine, other, zone_index = spot(half_blocks.bit_length() - 1)
    spots = [
        (1 - core) * half_blocks + (other ^ rest) if crossed else core * half_blocks + (mine ^ rest)
        for crossed, rest in pieces
    ]
    out_ref, flat_ref, rows_ref, sem = refs[-4:]
    channels = out_ref.shape[1]
    tap_width = zones * width // 3
    whole, part = channels // height, channels % height

    def copies(index, act):
        block = spots[index]

        def copy(size):
            return pltpu.make_async_copy(
                rows_ref.at[index, :, pl.ds(0, size)],
                out_ref.at[:, pl.ds(pl.multiple_of(block * height, 8), size)],
                sem.at[index],
            )

        @pl.when(block < whole)
        def _():
            act(copy(height))

        if part:

            @pl.when(block == whole)
            def _():
                act(copy(part))

    for index in range(count):
        for zone in range(zones):
            left = pl.multiple_of((zone_index ^ zone) * width, LANES)
            flat_ref[index, :, pl.ds(left, width)] = cells[index][zone]
        for tap in range(9):
            left = (tap // 3) * tap_width + (tap % 3) * channels
            rows_ref[index, tap] = flat_ref[index, :, left : left + channels]
        copies(index, lambda copy: copy.start())
    for index in range(count):
        copies(index, lambda copy: copy.wait())


def spread_body(
    known, masks, mine_ref, other_ref, table_ref, scale_ref, back_ref, steps_ref
):
    channels = steps_ref.shape[1]
    table_ref[...] = mine_ref[...]
    for core in range(2):

        @pl.when(lax.rem(lax.axis_index("space"), 2) == core)
        def _():
            for row in known[core]:
                at = row ^ masks[core]
                table_ref[at : at + 1] = other_ref[row : row + 1]

    table = table_ref[...]
    bound = jnp.max(table[:, channels + NOTE : channels + NOTE + 1], axis=0, keepdims=True)
    bound = jnp.maximum(bound, 1e-25) * (1.0 / 30000.0)
    back_ref[...] = bound
    scale_ref[...] = 1.0 / bound
    steps_ref[...] = jnp.broadcast_to(table[:, channels : channels + 1], steps_ref.shape)


def gather_body(images, sums_ref, table_ref, out_ref):
    channels = sums_ref.shape[1]
    rows = [sums_ref[0:1], sums_ref[1:2]]
    rows += [table_ref[i : i + 1, :channels] for i in range(images)]
    out_ref[...] = rows_of(*[jnp.broadcast_to(row, out_ref.shape) for row in rows])


def total_body(*refs):
    refs[-1][...] = tree_sum([ref[...] for ref in refs[:-1]])


def time_body(count, embed_ref, total_ref, out_ref):
    columns = embed_ref[...].T
    terms = [columns[:, i : i + 1] * total_ref[2 + i : 3 + i] for i in range(count)]
    out_ref[...] = tree_sum(terms)


def swap_space(cells, mask):
    count = lax.axis_size("space")
    return lax.ppermute(cells, "space", [(i, i ^ mask) for i in range(count)])


def swap_image(cells, masks):
    images = lax.axis_size("dp")
    count = lax.axis_size("space")
    pairs = [
        (i * count + j, (i ^ masks[j % 2]) * count + j) for i in range(images) for j in range(count)
    ]
    return lax.ppermute(cells, ("dp", "space"), pairs)


def slab_program(
    latent, timesteps, norm_gain, norm_bias, conv_weight, conv_bias, time_weight, cotangent
):
    images, row_count, col_count, channels = latent.shape
    assert images == 1
    per_group = channels // GROUPS
    image_count = lax.axis_size("dp")
    slab_count = lax.axis_size("space")
    zones = slab_count // 2
    bits = image_count.bit_length() - 1
    blocks = 2 * image_count
    height = -(-channels // (8 * blocks)) * 8
    tap_width = -(-3 * channels // LANES) * LANES
    width = 3 * tap_width // zones
    local_count = row_count * col_count * per_group
    total_count = local_count * slab_count
    positions = row_count * col_count

    slab_index = lax.axis_index("space")
    core = slab_index % 2

    lat = latent.transpose(0, 1, 3, 2)[0]
    cot = cotangent.transpose(0, 1, 3, 2)[0]
    gain, bias = norm_gain, norm_bias
    vmem = pl.BlockSpec(memory_space=pltpu.VMEM)
    anywhere = pl.BlockSpec(memory_space=pl.ANY)
    small = jax.ShapeDtypeStruct((8, channels), f32)

    flops = 2 * positions * channels * channels * 9
    taps = pltpu.VMEM((3 * channels, (row_count + 2) * col_count), bf16)
    flat = pltpu.VMEM((3, channels, 3 * channels), bf16)

    slab = pltpu.VMEM((row_count, channels, col_count), bf16)
    own = call(
        functools.partial(stats_body, local_count),
        small,
        (lat, cot),
        specs=(anywhere, anywhere),
        scratch=(slab, slab, pltpu.SemaphoreType.DMA((2, row_count))),
        moved=2 * lat.size * 2,
        flops=positions * channels * 60,
        limit=60 << 20,
    )
    partner = swap_space(own, 1)
    pair = call(
        functools.partial(merge_body, local_count, None),
        small,
        (jnp.maximum(own, jnp.finfo(f32).min), partner),
        limit=4 << 20,
    )
    parts = [pair]
    for mask in range(1, zones):
        parts.append(swap_space(pair, 2 * mask))
    far_row = jnp.where(core == 0, 0, row_count - 1)
    between = [(i, i - 1 if i % 2 == 0 else i + 1) for i in range(1, slab_count - 1)]

    def edges(cells):
        outward = lax.dynamic_index_in_dim(cells, far_row, 0, keepdims=False)
        inward = lax.dynamic_index_in_dim(cells, row_count - 1 - far_row, 0, keepdims=False)
        outer = lax.ppermute(outward, "space", between)
        return outer, swap_space(inward, 1)

    outer, inner = edges(cot)
    lat_outer, lat_inner = edges(lat)
    stats = call(
        functools.partial(merge_body, 2 * local_count, total_count),
        small,
        tuple(parts),
        limit=4 << 20,
    )

    orders = [list(range(bits)), list(range(bits))[::-1]]

    part_shape = jax.ShapeDtypeStruct((blocks // 4, zones, height, width), f32)
    share_shape = jax.ShapeDtypeStruct((blocks // 2, zones, height, width), f32)
    taps_shape = jax.ShapeDtypeStruct((3 * channels, positions), bf16)
    grad_taps, col_sums = call(
        taps_body, (taps_shape, small), (cot,), moved=10 * lat.size, limit=6 << 20
    )
    table_shape = jax.ShapeDtypeStruct((-(-image_count // 8) * 8, channels + 2 * NOTE), f32)
    factor, spread = float(positions * slab_count * image_count), math.sqrt(per_group)
    act, middle_rows, table = call(
        functools.partial(middle_body, factor, spread),
        (
            jax.ShapeDtypeStruct((channels, positions), bf16),
            jax.ShapeDtypeStruct((channels, 3 * channels), f32),
            table_shape,
        ),
        (lat, grad_taps, stats, gain, bias, col_sums, timesteps.astype(f32).reshape(1, 1)),
        flops=flops // 3,
        moved=8 * lat.size,
        limit=8 << 20,
    )
    near, far_low, far_high, edge_taps = call(
        functools.partial(weight_body, (blocks, zones, height, width), col_count),
        (
            share_shape,
            part_shape,
            part_shape,
            jax.ShapeDtypeStruct((3 * channels, 2 * col_count), bf16),
        ),
        (act, grad_taps, outer, inner, middle_rows),
        flops=flops,
        moved=8 * lat.size,
        limit=12 << 20,
    )
    unit = jax.ShapeDtypeStruct((1, 1), f32)
    steps_shape = jax.ShapeDtypeStruct((table_shape.shape[0], channels), f32)
    known = ([0], [0])
    scales = []
    for step in range(bits):
        masks = (1 << orders[0][step], 1 << orders[1][step])
        arrived = swap_image(table, masks)
        table, scale, back, steps = call(
            functools.partial(spread_body, known, masks),
            (table_shape, unit, unit, steps_shape),
            (table, arrived),
            limit=4 << 20,
        )
        scales.append((scale[0, 0], back[0, 0]))
        known = tuple(rows + [row ^ mask for row in rows] for rows, mask in zip(known, masks))

    grad, sums = call(
        backward_body,
        (jax.ShapeDtypeStruct((row_count, channels, col_count), f32), small),
        (lat, grad_taps, edge_taps, stats, gain, bias, conv_weight),
        scratch=(flat,),
        flops=flops,
        moved=8 * lat.size,
        limit=8 << 20,
    )
    message = jax.ShapeDtypeStruct((-(-(2 + image_count) // 8) * 8, channels), f32)
    gathered = call(
        functools.partial(gather_body, image_count), message, (sums, table), limit=4 << 20
    )
    gathered = [gathered + swap_space(gathered, 1)]
    for mask in range(1, zones):
        gathered.append(swap_space(gathered[0], 2 * mask))
    totals = call(total_body, message, tuple(gathered), limit=4 << 20)
    line_scale, line_back = scales[-1]

    middle = blocks // 4
    far_in = swap_space(far_high, 1)
    near_in = swap_space(far_low, 1)
    sent = ((near[middle:] + far_in) * scales[0][0]).astype(f16)
    near, near_in, _ = lax.optimization_barrier((near, near_in, sent))
    keeping = near[:middle] + near_in
    for step in range(bits):
        masks = (1 << orders[0][step], 1 << orders[1][step])
        arrived = swap_image(sent, masks)
        back = scales[step][1]
        middle = keeping.shape[0] // 2
        if middle:
            total = keeping[middle:] + arrived[middle:].astype(f32) * back
            sent = (total * scales[step + 1][0]).astype(f16)
            keeping, arrived, _ = lax.optimization_barrier((keeping, arrived, sent))
            keeping = keeping[:middle] + arrived[:middle].astype(f32) * back
    sent = []
    for mask in range(1, zones):
        total = keeping[0, mask] + arrived[0, mask].astype(f32) * back
        sent.append((total * line_scale).astype(f16))
    keeping, arrived, *_ = lax.optimization_barrier((keeping, arrived, *sent))
    share = keeping[0, 0] + arrived[0, 0].astype(f32) * back
    for mask in range(1, zones):
        share = share + swap_space(sent[mask - 1], 2 * mask).astype(f32) * line_back
    share = (share * line_scale).astype(f16)
    collected = [share]
    for mask in range(1, zones):
        collected.append(swap_space(share, 2 * mask))
    pieces = [jnp.stack(collected)]
    for step in reversed(range(bits)):
        masks = (1 << orders[0][step], 1 << orders[1][step])
        arrived = []
        for piece in pieces:
            arrived.append(swap_image(piece, masks))
        pieces = pieces + arrived
    crossed = []
    for piece in pieces:
        crossed.append(swap_space(piece, 1))
    half_blocks = blocks // 2
    numbers = list(range(half_blocks))

    def place(chosen, before):
        count = len(chosen)
        cells = []
        for is_crossed, rest in chosen:
            piece = crossed[rest] if is_crossed else pieces[rest]
            cells.append(piece.astype(f32) * line_back)
        return pl.pallas_call(
            functools.partial(place_body, (zones, height, width), half_blocks, chosen),
            out_shape=jax.ShapeDtypeStruct((9, channels, channels), f32),
            in_specs=[vmem] * count + [anywhere] * len(before),
            out_specs=anywhere,
            scratch_shapes=[
                pltpu.VMEM((count, height, zones * width), f32),
                pltpu.VMEM((count, 9, height, channels), f32),
                pltpu.SemaphoreType.DMA((count,)),
            ],
            input_output_aliases={count: 0} if before else {},
            compiler_params=pltpu.CompilerParams(vmem_limit_bytes=12 << 20),
            cost_estimate=pl.CostEstimate(
                flops=0,
                bytes_accessed=8 * count * zones * height * width,
                transcendentals=0,
            ),
        )(*cells, *before)

    early = [(side, rest) for side in (False, True) for rest in numbers[:-1]]
    weight_grad = place(early, ())
    weight_grad = place([(False, numbers[-1]), (True, numbers[-1])], (weight_grad,))
    weight_grad = weight_grad.reshape(3, 3, channels, channels)

    half_count = channels // 2
    frequency = jnp.exp(-math.log(10000.0) * jnp.arange(half_count, dtype=f32) / half_count)
    angles = steps[:, :half_count] * frequency[None, :]
    embedding = jnp.concatenate([jnp.cos(angles), jnp.sin(angles)], axis=1).astype(bf16)
    time_bias = jnp.dot(embedding[:1], time_weight, preferred_element_type=f32)
    extra = time_bias + conv_bias.reshape(1, channels)
    time_grad = call(
        functools.partial(time_body, image_count),
        jax.ShapeDtypeStruct((channels, channels), f32),
        (embedding.astype(f32), totals),
        limit=4 << 20,
    )
    block_out = call(
        conv_body,
        jax.ShapeDtypeStruct((row_count, channels, col_count), bf16),
        (act, lat, lat_outer, lat_inner, stats, gain, bias, conv_weight, extra),
        scratch=(taps, flat),
        flops=flops,
        moved=8 * lat.size,
        limit=14 << 20,
    )
    latent_grad = call(
        functools.partial(latent_body, total_count),
        jax.ShapeDtypeStruct((row_count, channels, col_count), bf16),
        (grad, lat, cot, stats, totals),
        flops=lat.size * 20,
        moved=10 * lat.size,
        limit=12 << 20,
    )

    block_out = block_out[None].transpose(0, 1, 3, 2)
    latent_grad = latent_grad[None].transpose(0, 1, 3, 2)
    return (block_out, latent_grad, weight_grad, time_grad)


def solution(mesh):
    return jax.shard_map(
        slab_program,
        mesh=mesh,
        in_specs=(
            P("dp", "space", None, None),
            P("dp"),
            P(),
            P(),
            P(),
            P(),
            P(),
            P("dp", "space", None, None),
        ),
        out_specs=(P("dp", "space", None, None), P("dp", "space", None, None), P(), P()),
        check_vma=False,
    )
```

```python
import functools
import math

import jax
import jax.numpy as jnp
from jax import lax
from jax.experimental import pallas as pl
from jax.experimental.pallas import tpu as pltpu
from jax.sharding import PartitionSpec as P


GROUPS = 32
epsilon = 1e-05
f32 = jnp.float32
bf16 = jnp.bfloat16
f16 = jnp.float16
LANES = 128
NOTE = 32


def contract(a, b, dims, precision=None):
    return lax.dot_general(a, b, (dims, ((), ())), preferred_element_type=f32, precision=precision)


def spot(bits):
    image, slab = lax.axis_index("dp"), lax.axis_index("space")
    core = lax.rem(slab, 2)

    def index(which):
        found = 0
        for step in range(bits):
            shift = jnp.where(which == 0, step, bits - 1 - step)
            found = found * 2 + (lax.shift_right_logical(image, shift) & 1)
        return found

    return core, index(core), index(1 - core), lax.shift_right_logical(slab, 1)


def call(body, outs, args, specs=None, scratch=(), flops=0, moved=0, limit=40 << 20):
    vmem = pl.BlockSpec(memory_space=pltpu.VMEM)
    many = isinstance(outs, (list, tuple))
    return pl.pallas_call(
        body,
        out_shape=tuple(outs) if many else outs,
        in_specs=list(specs) if specs else [vmem] * len(args),
        out_specs=tuple([vmem] * len(outs)) if many else vmem,
        scratch_shapes=list(scratch),
        compiler_params=pltpu.CompilerParams(vmem_limit_bytes=limit),
        cost_estimate=pl.CostEstimate(flops=flops, bytes_accessed=moved, transcendentals=0),
    )(*args)


def group_sums(*columns):
    channels = columns[0].shape[0]
    per_group = channels // GROUPS
    row = lax.broadcasted_iota(jnp.int32, (channels, channels), 0).astype(f32)
    col = lax.broadcasted_iota(jnp.int32, (channels, channels), 1).astype(f32)
    same = jnp.floor((row + 0.5) / per_group) == jnp.floor((col + 0.5) / per_group)
    member = jnp.where(same, 1.0, 0.0).astype(bf16)
    lane = lax.broadcasted_iota(jnp.int32, (channels, LANES), 1)
    cells = jnp.zeros((channels, LANES), f32)
    for number, column in enumerate(columns):
        rest = column
        for part in range(3):
            taken = rest.astype(bf16).astype(f32)
            cells = jnp.where(lane == 3 * number + part, taken, cells)
            rest = rest - taken
    found = contract(member, cells.astype(bf16), ((1,), (0,)))
    pick = [found[:, i : i + 1] for i in range(3 * len(columns))]
    return [pick[3 * i] + pick[3 * i + 1] + pick[3 * i + 2] for i in range(len(columns))]


def as_rows(*columns):
    channels = columns[0].shape[0]
    lane = lax.broadcasted_iota(jnp.int32, (channels, LANES), 1)
    cells = jnp.zeros((channels, LANES), f32)
    for number, column in enumerate(columns):
        cells = jnp.where(lane == number, column, cells)
    return cells.T[:8]


def lane_sum(cells):
    return jnp.sum(cells, axis=1, keepdims=True)


def rows_of(*rows):
    height = lax.broadcasted_iota(jnp.int32, rows[0].shape, 0)
    packed = jnp.zeros(rows[0].shape, f32)
    for number, row in enumerate(rows):
        packed = jnp.where(height == number, row, packed)
    return packed


def fold_lanes(cells):
    total = cells[:, :LANES]
    for start in range(LANES, cells.shape[1], LANES):
        total = total + cells[:, start : start + LANES]
    return total


def stats_body(count, latent_hbm, cot_hbm, out_ref, latent_ref, cot_ref, sem):
    row_count, channels, cols = latent_ref.shape
    loads = []
    for number, (source, target) in enumerate(((latent_hbm, latent_ref), (cot_hbm, cot_ref))):
        for row in range(row_count):
            load = pltpu.make_async_copy(source.at[row], target.at[row], sem.at[number, row])
            load.start()
            loads.append(load)
    ones = jnp.ones((cols, LANES), bf16)
    sums = jnp.zeros((channels, LANES), f32)
    for row in range(row_count):
        loads[row].wait()
        sums = sums + contract(latent_ref[row], ones, ((1,), (0,)))
    mean = group_sums(sums[:, :1])[0] / count
    squares = jnp.zeros((channels, LANES), f32)
    for row in range(row_count):
        centered = latent_ref[row].astype(f32) - mean
        squares = squares + fold_lanes(centered * centered)
    grouped = group_sums(lane_sum(squares))[0]
    top = jnp.zeros((channels, LANES), bf16)
    for row in range(row_count):
        loads[row_count + row].wait()
        size = jnp.abs(cot_ref[row])
        for start in range(0, cols, LANES):
            top = jnp.maximum(top, size[:, start : start + LANES])
    largest = jnp.max(top.astype(f32), axis=(0, 1), keepdims=True)
    out_ref[...] = as_rows(mean, grouped, jnp.broadcast_to(largest, mean.shape))


def tree_sum(parts):
    while len(parts) > 1:
        parts = [parts[i] + parts[i + 1] for i in range(0, len(parts), 2)]
    return parts[0]


def merge_body(count, total, *refs):
    parts, out_ref = [ref[...] for ref in refs[:-1]], refs[-1]
    mean = tree_sum([part[0:1] for part in parts]) / len(parts)
    squares = tree_sum([part[1:2] + count * (part[0:1] - mean) ** 2 for part in parts])
    if total:
        squares = lax.rsqrt(squares / total + epsilon)
    largest = functools.reduce(jnp.maximum, [part[2:3] for part in parts])
    rows = (mean, squares, largest)
    out_ref[...] = rows_of(*[jnp.broadcast_to(row, out_ref.shape) for row in rows])


def column_values(stats_ref, gain_ref, bias_ref):
    channels = gain_ref.shape[0]
    shape = (8, channels)
    table = rows_of(
        jnp.broadcast_to(stats_ref[0:1], shape),
        jnp.broadcast_to(stats_ref[1:2], shape),
        jnp.broadcast_to(gain_ref[...], shape),
        jnp.broadcast_to(bias_ref[...], shape),
    ).T
    return [table[:, i : i + 1] for i in range(4)]


def normalized(cells, values):
    mean, inverse, gain, bias = values
    normed = (cells.astype(f32) - mean) * inverse
    shifted = normed * gain + bias
    return normed, shifted, jax.nn.sigmoid(shifted)


def activate(cells, values):
    _, shifted, sigmoid = normalized(cells, values)
    return (shifted * sigmoid).astype(bf16)


def shifted_cols(cells):
    cols = cells.shape[1]
    lane = lax.broadcasted_iota(jnp.int32, cells.shape, 1)
    zero = jnp.zeros_like(cells)
    after = jnp.where(lane == cols - 1, zero, pltpu.roll(cells, cols - 1, 1))
    before = jnp.where(lane == 0, zero, pltpu.roll(cells, 1, 1))
    return after, before


def put_taps(buffer_ref, place, cells, flip):
    channels, cols = cells.shape
    wide = cells.astype(f32)
    after, before = shifted_cols(wide)
    order = (after, cells, before) if flip else (before, cells, after)
    start = place * cols if isinstance(place, int) else pl.multiple_of(place * cols, LANES)
    for tap, piece in enumerate(order):
        buffer_ref[tap * channels : (tap + 1) * channels, pl.ds(start, cols)] = piece.astype(bf16)


def taps_body(cot_ref, taps_ref, sums_ref):
    row_count, channels, cols = cot_ref.shape
    tall = jnp.ones((8, cols), bf16)
    sums = jnp.zeros((8, channels), f32)
    for row in range(row_count):
        put_taps(taps_ref, row, cot_ref[row], True)
        sums = sums + contract(tall, cot_ref[row], ((1,), (1,)))
    sums_ref[...] = sums


def middle_body(
    factor, spread, latent_ref, taps_ref, stats_ref, gain_ref, bias_ref, sums_ref, step_ref,
    act_ref, found_ref, table_ref,
):
    row_count, channels, cols = latent_ref.shape
    table_ref[...] = jnp.zeros(table_ref.shape, f32)
    table_ref[0:1, :channels] = sums_ref[0:1]
    table_ref[0:1, channels : channels + NOTE] = jnp.broadcast_to(step_ref[...], (1, NOTE))
    gain = jnp.max(jnp.abs(gain_ref[...][None, :]), axis=1, keepdims=True)
    bias = jnp.max(jnp.abs(bias_ref[...][None, :]), axis=1, keepdims=True)
    bound = stats_ref[2:3] * ((spread * gain + bias) * factor)
    table_ref[0:1, channels + NOTE : channels + 2 * NOTE] = bound[:, :NOTE]
    values = column_values(stats_ref, gain_ref, bias_ref)
    for row in range(row_count):
        act_ref[:, row * cols : (row + 1) * cols] = activate(latent_ref[row], values)
    found_ref[...] = contract(act_ref[...], taps_ref[...], ((1,), (1,)))


def weight_body(
    shape, cols, act_ref, taps_ref, outer_ref, inner_ref, middle_ref,
    near_ref, low_ref, high_ref, edge_ref,
):
    blocks, zones, height, width = shape
    channels, positions = act_ref.shape
    core, mine, other, zone_index = spot((blocks // 2).bit_length() - 1)
    quarter = blocks // 4
    put_taps(edge_ref, core, outer_ref[...], True)
    put_taps(edge_ref, 1 - core, inner_ref[...], True)
    tap_width = zones * width // 3

    def store(ref, place, found, block, tap_row):
        first = block * height
        size = max(min(height, channels - first), 0)
        for zone in range(zones):
            low = max(zone * width, tap_row * tap_width)
            high = min((zone + 1) * width, (tap_row + 1) * tap_width)
            if low >= high:
                continue
            at = zone_index ^ zone
            left, right = low - zone * width, high - zone * width
            source = low - tap_row * tap_width
            used = max(min(right - left, 3 * channels - source), 0)
            if size and used:
                ref[place, at, :size, left : left + used] = found[
                    first : first + size, source : source + used
                ]
            if used < right - left:
                ref[place, at, :, left + used : right] = jnp.zeros(
                    (height, right - left - used), f32
                )
            if size < height and used:
                ref[place, at, size:, left : left + used] = jnp.zeros((height - size, used), f32)

    for tap_row in (1, 0, 2):
        if tap_row == 1:
            found = middle_ref
        else:
            inner = slice(0, positions - cols) if tap_row == 0 else slice(cols, positions)
            shifted = slice(cols, positions) if tap_row == 0 else slice(0, positions - cols)
            outer = slice(positions - cols, positions) if tap_row == 0 else slice(0, cols)
            edge = slice(cols, 2 * cols) if tap_row == 0 else slice(0, cols)
            found = contract(act_ref[:, inner], taps_ref[:, shifted], ((1,), (1,)))
            found = found + contract(act_ref[:, outer], edge_ref[:, edge], ((1,), (1,)))
        for half in range(2):

            @pl.when(core == half)
            def _():
                for rest in range(blocks // 2):
                    store(near_ref, mine ^ rest, found, half * blocks // 2 + rest, tap_row)

            for top in range(2):

                @pl.when((core != half) & (other // quarter == top))
                def _():
                    for rest in range(blocks // 2):
                        ref = high_ref if rest // quarter != top else low_ref
                        at = (other ^ rest) % quarter
                        store(ref, at, found, half * blocks // 2 + rest, tap_row)


def conv_body(
    act_ref, latent_ref, outer_ref, inner_ref, stats_ref, gain_ref, bias_ref, weight_ref,
    extra_ref, out_ref, taps_ref, flat_ref,
):
    row_count, channels, cols = latent_ref.shape
    values = column_values(stats_ref, gain_ref, bias_ref)
    slab, last = lax.axis_index("space"), lax.axis_size("space") - 1
    core = lax.rem(slab, 2)
    keep = jnp.where((slab == 0) | (slab == last), 0.0, 1.0).astype(f32)
    outer = (activate(outer_ref[...], values).astype(f32) * keep).astype(bf16)
    put_taps(taps_ref, core * (row_count + 1), outer, False)
    put_taps(taps_ref, (1 - core) * (row_count + 1), activate(inner_ref[...], values), False)
    for row in range(row_count):
        put_taps(taps_ref, row + 1, act_ref[:, row * cols : (row + 1) * cols], False)
    for tap_row in range(3):
        flat_ref[tap_row] = weight_ref[tap_row].reshape(3 * channels, channels).T
    extra = jnp.broadcast_to(extra_ref[...], (8, channels)).T[:, :1]
    for row in range(row_count):
        total = latent_ref[row].astype(f32) + extra
        for tap_row in range(3):
            start = (row + tap_row) * cols
            total = total + contract(
                flat_ref[tap_row], taps_ref[:, start : start + cols], ((1,), (0,))
            )
        out_ref[row] = total.astype(bf16)


def backward_body(
    latent_ref, taps_ref, edge_ref, stats_ref, gain_ref, bias_ref, weight_ref,
    grad_ref, sums_ref, flat_ref,
):
    row_count, channels, cols = latent_ref.shape
    values = column_values(stats_ref, gain_ref, bias_ref)
    for tap_row in range(3):
        flat_ref[tap_row] = jnp.concatenate([weight_ref[tap_row, j] for j in range(3)], axis=1)
    first = jnp.zeros((channels, LANES), f32)
    second = jnp.zeros((channels, LANES), f32)
    for row in range(row_count):
        total = jnp.zeros((channels, cols), f32)
        for tap_row in range(3):
            source = row + 1 - tap_row
            if 0 <= source < row_count:
                piece = taps_ref[:, source * cols : (source + 1) * cols]
            else:
                start = cols if source > 0 else 0
                piece = edge_ref[:, start : start + cols]
            total = total + contract(flat_ref[tap_row], piece, ((1,), (0,)))
        normed, shifted, sigmoid = normalized(latent_ref[row], values)
        grad = total * sigmoid * (1.0 + shifted * (1.0 - sigmoid)) * values[2]
        grad_ref[row] = grad
        first = first + fold_lanes(grad)
        second = second + fold_lanes(grad * normed)
    sums_ref[...] = as_rows(*group_sums(lane_sum(first), lane_sum(second)))


def latent_body(total, grad_ref, latent_ref, cot_ref, stats_ref, sums_ref, out_ref):
    row_count, channels, _ = latent_ref.shape
    sums = sums_ref[0:2] / total
    shape = (8, channels)
    table = rows_of(
        *[
            jnp.broadcast_to(row, shape)
            for row in (stats_ref[0:1], stats_ref[1:2], sums[0:1], sums[1:2])
        ]
    ).T
    mean, inverse, first, second = [table[:, i : i + 1] for i in range(4)]
    for row in range(row_count):
        normed = (latent_ref[row].astype(f32) - mean) * inverse
        change = inverse * (grad_ref[row] - first - normed * second)
        out_ref[row] = (cot_ref[row].astype(f32) + change).astype(bf16)


def place_body(shape, half_blocks, pieces, *refs):
    zones, height, width = shape
    count = len(pieces)
    cells = refs[:count]
    core, mine, other, zone_index = spot(half_blocks.bit_length() - 1)
    spots = [
        (1 - core) * half_blocks + (other ^ rest) if crossed else core * half_blocks + (mine ^ rest)
        for crossed, rest in pieces
    ]
    out_ref, flat_ref, rows_ref, sem = refs[-4:]
    channels = out_ref.shape[1]
    tap_width = zones * width // 3
    whole, part = channels // height, channels % height

    def copies(index, act):
        block = spots[index]

        def copy(size):
            return pltpu.make_async_copy(
                rows_ref.at[index, :, pl.ds(0, size)],
                out_ref.at[:, pl.ds(pl.multiple_of(block * height, 8), size)],
                sem.at[index],
            )

        @pl.when(block < whole)
        def _():
            act(copy(height))

        if part:

            @pl.when(block == whole)
            def _():
                act(copy(part))

    for index in range(count):
        for zone in range(zones):
            left = pl.multiple_of((zone_index ^ zone) * width, LANES)
            flat_ref[index, :, pl.ds(left, width)] = cells[index][zone]
        for tap in range(9):
            left = (tap // 3) * tap_width + (tap % 3) * channels
            rows_ref[index, tap] = flat_ref[index, :, left : left + channels]
        copies(index, lambda copy: copy.start())
    for index in range(count):
        copies(index, lambda copy: copy.wait())


def spread_body(
    known, masks, mine_ref, other_ref, table_ref, scale_ref, back_ref, steps_ref
):
    channels = steps_ref.shape[1]
    table_ref[...] = mine_ref[...]
    for core in range(2):

        @pl.when(lax.rem(lax.axis_index("space"), 2) == core)
        def _():
            for row in known[core]:
                at = row ^ masks[core]
                table_ref[at : at + 1] = other_ref[row : row + 1]

    table = table_ref[...]
    bound = jnp.max(table[:, channels + NOTE : channels + NOTE + 1], axis=0, keepdims=True)
    bound = jnp.maximum(bound, 1e-25) * (1.0 / 30000.0)
    back_ref[...] = bound
    scale_ref[...] = 1.0 / bound
    steps_ref[...] = jnp.broadcast_to(table[:, channels : channels + 1], steps_ref.shape)


def gather_body(images, sums_ref, table_ref, out_ref):
    channels = sums_ref.shape[1]
    rows = [sums_ref[0:1], sums_ref[1:2]]
    rows += [table_ref[i : i + 1, :channels] for i in range(images)]
    out_ref[...] = rows_of(*[jnp.broadcast_to(row, out_ref.shape) for row in rows])


def total_body(*refs):
    refs[-1][...] = tree_sum([ref[...] for ref in refs[:-1]])


def time_body(count, embed_ref, total_ref, out_ref):
    columns = embed_ref[...].T
    terms = [columns[:, i : i + 1] * total_ref[2 + i : 3 + i] for i in range(count)]
    out_ref[...] = tree_sum(terms)


def swap_space(cells, mask):
    count = lax.axis_size("space")
    return lax.ppermute(cells, "space", [(i, i ^ mask) for i in range(count)])


def swap_image(cells, masks):
    images = lax.axis_size("dp")
    count = lax.axis_size("space")
    pairs = [
        (i * count + j, (i ^ masks[j % 2]) * count + j) for i in range(images) for j in range(count)
    ]
    return lax.ppermute(cells, ("dp", "space"), pairs)


def slab_program(
    latent, timesteps, norm_gain, norm_bias, conv_weight, conv_bias, time_weight, cotangent
):
    images, row_count, col_count, channels = latent.shape
    assert images == 1
    per_group = channels // GROUPS
    image_count = lax.axis_size("dp")
    slab_count = lax.axis_size("space")
    zones = slab_count // 2
    bits = image_count.bit_length() - 1
    blocks = 2 * image_count
    height = -(-channels // (8 * blocks)) * 8
    tap_width = -(-3 * channels // LANES) * LANES
    width = 3 * tap_width // zones
    local_count = row_count * col_count * per_group
    total_count = local_count * slab_count
    positions = row_count * col_count

    slab_index = lax.axis_index("space")
    core = slab_index % 2

    lat = latent.transpose(0, 1, 3, 2)[0]
    cot = cotangent.transpose(0, 1, 3, 2)[0]
    gain, bias = norm_gain, norm_bias
    vmem = pl.BlockSpec(memory_space=pltpu.VMEM)
    anywhere = pl.BlockSpec(memory_space=pl.ANY)
    small = jax.ShapeDtypeStruct((8, channels), f32)

    flops = 2 * positions * channels * channels * 9
    taps = pltpu.VMEM((3 * channels, (row_count + 2) * col_count), bf16)
    flat = pltpu.VMEM((3, channels, 3 * channels), bf16)

    slab = pltpu.VMEM((row_count, channels, col_count), bf16)
    own = call(
        functools.partial(stats_body, local_count),
        small,
        (lat, cot),
        specs=(anywhere, anywhere),
        scratch=(slab, slab, pltpu.SemaphoreType.DMA((2, row_count))),
        moved=2 * lat.size * 2,
        flops=positions * channels * 60,
        limit=60 << 20,
    )
    partner = swap_space(own, 1)
    pair = call(
        functools.partial(merge_body, local_count, None),
        small,
        (jnp.maximum(own, jnp.finfo(f32).min), partner),
        limit=4 << 20,
    )
    parts = [pair]
    for mask in range(1, zones):
        parts.append(swap_space(pair, 2 * mask))
    far_row = jnp.where(core == 0, 0, row_count - 1)
    between = [(i, i - 1 if i % 2 == 0 else i + 1) for i in range(1, slab_count - 1)]

    def edges(cells):
        outward = lax.dynamic_index_in_dim(cells, far_row, 0, keepdims=False)
        inward = lax.dynamic_index_in_dim(cells, row_count - 1 - far_row, 0, keepdims=False)
        outer = lax.ppermute(outward, "space", between)
        return outer, swap_space(inward, 1)

    outer, inner = edges(cot)
    lat_outer, lat_inner = edges(lat)
    stats = call(
        functools.partial(merge_body, 2 * local_count, total_count),
        small,
        tuple(parts),
        limit=4 << 20,
    )

    orders = [list(range(bits)), list(range(bits))[::-1]]

    part_shape = jax.ShapeDtypeStruct((blocks // 4, zones, height, width), f32)
    share_shape = jax.ShapeDtypeStruct((blocks // 2, zones, height, width), f32)
    taps_shape = jax.ShapeDtypeStruct((3 * channels, positions), bf16)
    grad_taps, col_sums = call(
        taps_body, (taps_shape, small), (cot,), moved=10 * lat.size, limit=6 << 20
    )
    table_shape = jax.ShapeDtypeStruct((-(-image_count // 8) * 8, channels + 2 * NOTE), f32)
    factor, spread = float(positions * slab_count * image_count), math.sqrt(per_group)
    act, middle_rows, table = call(
        functools.partial(middle_body, factor, spread),
        (
            jax.ShapeDtypeStruct((channels, positions), bf16),
            jax.ShapeDtypeStruct((channels, 3 * channels), f32),
            table_shape,
        ),
        (lat, grad_taps, stats, gain, bias, col_sums, timesteps.astype(f32).reshape(1, 1)),
        flops=flops // 3,
        moved=8 * lat.size,
        limit=8 << 20,
    )
    near, far_low, far_high, edge_taps = call(
        functools.partial(weight_body, (blocks, zones, height, width), col_count),
        (
            share_shape,
            part_shape,
            part_shape,
            jax.ShapeDtypeStruct((3 * channels, 2 * col_count), bf16),
        ),
        (act, grad_taps, outer, inner, middle_rows),
        flops=flops,
        moved=8 * lat.size,
        limit=12 << 20,
    )
    unit = jax.ShapeDtypeStruct((1, 1), f32)
    steps_shape = jax.ShapeDtypeStruct((table_shape.shape[0], channels), f32)
    known = ([0], [0])
    scales = []
    for step in range(bits):
        masks = (1 << orders[0][step], 1 << orders[1][step])
        arrived = swap_image(table, masks)
        table, scale, back, steps = call(
            functools.partial(spread_body, known, masks),
            (table_shape, unit, unit, steps_shape),
            (table, arrived),
            limit=4 << 20,
        )
        scales.append((scale[0, 0], back[0, 0]))
        known = tuple(rows + [row ^ mask for row in rows] for rows, mask in zip(known, masks))

    grad, sums = call(
        backward_body,
        (jax.ShapeDtypeStruct((row_count, channels, col_count), f32), small),
        (lat, grad_taps, edge_taps, stats, gain, bias, conv_weight),
        scratch=(flat,),
        flops=flops,
        moved=8 * lat.size,
        limit=8 << 20,
    )
    message = jax.ShapeDtypeStruct((-(-(2 + image_count) // 8) * 8, channels), f32)
    gathered = call(
        functools.partial(gather_body, image_count), message, (sums, table), limit=4 << 20
    )
    gathered = [gathered + swap_space(gathered, 1)]
    for mask in range(1, zones):
        gathered.append(swap_space(gathered[0], 2 * mask))
    totals = call(total_body, message, tuple(gathered), limit=4 << 20)
    line_scale, line_back = scales[-1]

    middle = blocks // 4
    far_in = swap_space(far_high, 1)
    near_in = swap_space(far_low, 1)
    sent = ((near[middle:] + far_in) * scales[0][0]).astype(f16)
    near, near_in, _ = lax.optimization_barrier((near, near_in, sent))
    keeping = near[:middle] + near_in
    for step in range(bits):
        masks = (1 << orders[0][step], 1 << orders[1][step])
        arrived = swap_image(sent, masks)
        back = scales[step][1]
        middle = keeping.shape[0] // 2
        if middle:
            total = keeping[middle:] + arrived[middle:].astype(f32) * back
            sent = (total * scales[step + 1][0]).astype(f16)
            keeping, arrived, _ = lax.optimization_barrier((keeping, arrived, sent))
            keeping = keeping[:middle] + arrived[:middle].astype(f32) * back
    sent = []
    for mask in range(1, zones):
        total = keeping[0, mask] + arrived[0, mask].astype(f32) * back
        sent.append((total * line_scale).astype(f16))
    keeping, arrived, *_ = lax.optimization_barrier((keeping, arrived, *sent))
    share = keeping[0, 0] + arrived[0, 0].astype(f32) * back
    for mask in range(1, zones):
        share = share + swap_space(sent[mask - 1], 2 * mask).astype(f32) * line_back
    share = (share * line_scale).astype(f16)
    collected = [share]
    for mask in range(1, zones):
        collected.append(swap_space(share, 2 * mask))
    pieces = [jnp.stack(collected)]
    for step in reversed(range(bits)):
        masks = (1 << orders[0][step], 1 << orders[1][step])
        arrived = []
        for piece in pieces:
            arrived.append(swap_image(piece, masks))
        pieces = pieces + arrived
    wide = {}
    for number, piece in enumerate(pieces):
        wide[False, number] = piece.astype(f32) * line_back
        final = number == len(pieces) - 1
        crossed = swap_space(piece if final else wide[False, number], 1)
        if final:
            crossed = crossed.astype(f32) * line_back
        wide[True, number] = crossed
    half_blocks = blocks // 2
    numbers = list(range(half_blocks))

    def place(chosen, before):
        count = len(chosen)
        cells = [wide[key] for key in chosen]
        return pl.pallas_call(
            functools.partial(place_body, (zones, height, width), half_blocks, chosen),
            out_shape=jax.ShapeDtypeStruct((9, channels, channels), f32),
            in_specs=[vmem] * count + [anywhere] * len(before),
            out_specs=anywhere,
            scratch_shapes=[
                pltpu.VMEM((count, height, zones * width), f32),
                pltpu.VMEM((count, 9, height, channels), f32),
                pltpu.SemaphoreType.DMA((count,)),
            ],
            input_output_aliases={count: 0} if before else {},
            compiler_params=pltpu.CompilerParams(vmem_limit_bytes=12 << 20),
            cost_estimate=pl.CostEstimate(
                flops=0,
                bytes_accessed=8 * count * zones * height * width,
                transcendentals=0,
            ),
        )(*cells, *before)

    late = [(False, numbers[-1]), (True, numbers[-1]), (True, 1)][: 2 + (half_blocks > 2)]
    early = [(side, rest) for side in (False, True) for rest in numbers]
    early = [key for key in early if key not in late]
    weight_grad = place(early, ())
    weight_grad = place(late, (weight_grad,))
    weight_grad = weight_grad.reshape(3, 3, channels, channels)

    half_count = channels // 2
    frequency = jnp.exp(-math.log(10000.0) * jnp.arange(half_count, dtype=f32) / half_count)
    angles = steps[:, :half_count] * frequency[None, :]
    embedding = jnp.concatenate([jnp.cos(angles), jnp.sin(angles)], axis=1).astype(bf16)
    time_bias = jnp.dot(embedding[:1], time_weight, preferred_element_type=f32)
    extra = time_bias + conv_bias.reshape(1, channels)
    time_grad = call(
        functools.partial(time_body, image_count),
        jax.ShapeDtypeStruct((channels, channels), f32),
        (embedding.astype(f32), totals),
        limit=4 << 20,
    )
    block_out = call(
        conv_body,
        jax.ShapeDtypeStruct((row_count, channels, col_count), bf16),
        (act, lat, lat_outer, lat_inner, stats, gain, bias, conv_weight, extra),
        scratch=(taps, flat),
        flops=flops,
        moved=8 * lat.size,
        limit=14 << 20,
    )
    latent_grad = call(
        functools.partial(latent_body, total_count),
        jax.ShapeDtypeStruct((row_count, channels, col_count), bf16),
        (grad, lat, cot, stats, totals),
        flops=lat.size * 20,
        moved=10 * lat.size,
        limit=12 << 20,
    )

    block_out = block_out[None].transpose(0, 1, 3, 2)
    latent_grad = latent_grad[None].transpose(0, 1, 3, 2)
    return (block_out, latent_grad, weight_grad, time_grad)


def solution(mesh):
    return jax.shard_map(
        slab_program,
        mesh=mesh,
        in_specs=(
            P("dp", "space", None, None),
            P("dp"),
            P(),
            P(),
            P(),
            P(),
            P(),
            P("dp", "space", None, None),
        ),
        out_specs=(P("dp", "space", None, None), P("dp", "space", None, None), P(), P()),
        check_vma=False,
    )
```
